32 devices in a mesh: grp: 2 (over x), row: 8 (over z, y), col: 2 (over core).
Axes of the slice: x: 2, y: 2, z: 4, core: 2. Of those that a mesh axis runs over, the one named last changes fastest.
Arguments:
- density: bfloat16 [1024, 32, 128], P(('grp', 'row', 'col')), parts along dimension 0, may hold values from -6 to 6
- leaf_target: int32 [1024], P(('grp', 'row', 'col')), parts along dimension 0, may hold values from 0 to 511, as said below
- geometry: float32 [6, 131072], P(None, ('grp', 'row', 'col')), parts along dimension 1, may hold values from -6 to 6
- near_list: int32 [1024, 16], P(('grp', 'row', 'col')), parts along dimension 0, may hold values from -1 to 511, as said below
- far_list: int32 [1024, 16], P(('grp', 'row', 'col')), parts along dimension 0, may hold values from -1 to 511, as said below
- node_list: int32 [128, 32], P(('grp', 'row', 'col')), parts along dimension 0, may hold values from -1 to 63, as said below
- basis_in: bfloat16 [1024, 64, 128], P(('grp', 'row', 'col')), parts along dimension 0, may hold values from -0.5 to 0.5
- basis_out: bfloat16 [1024, 64, 128], P(('grp', 'row', 'col')), parts along dimension 0, may hold values from -0.75 to 0.75
- transfer: bfloat16 [128, 64, 512], P(('grp', 'row', 'col')), parts along dimension 0, may hold values from -0.25 to 0.25
- node_points: float32 [3, 8192], P(None, 'grp'), parts along dimension 1, may hold values from -6 to 6
Outputs:
- potential: bfloat16 [1024, 32, 128], P(('grp', 'row', 'col')), parts along dimension 0
The draws below stay inside these ranges and needn't reach their ends.
There are 2 independent parts, one for each index of `grp`. The reference program is written for one: setup_inputs(seed, part) draws one part's arguments, and reference() takes and returns one part's arrays. A program takes and returns all parts, laid end to end along the dimension named above; each array names one. Nothing has to cross between parts.
Inputs may be any that keep to these rules, and one draw needn't show every extreme that they name: `leaf_target`: A permutation of the tree positions; of the 32 slab leaves of one device, exactly 2 go to the block of 32 tree positions of each device. `near_list`: row t holds t in slot 0; every other slot holds either -1 or a leaf other than t within 16 of t, the leaves of a row distinct; a -1 may stand in any slot after slot 0, also between leaves. `far_list`: every slot of row t holds either -1 or a leaf within 16 of t that is neither t nor in row t of near_list, the leaves of a row distinct; a -1 may stand in any slot, also between leaves. `node_list`: row p holds distinct nodes that differ from p by more than 2, then -1 in the unused slots.
All inputs are finite; a program needn't handle non-finite values.
Results may differ from the reference program's by a relative error of at most 0.0053.
Values may be sent and summed in bfloat16 or wider, within the bound.
No kernel may reach another device: no remote copies, remote signals or barrier semaphores. Data moves between devices by JAX's collectives and lax.ppermute only.
A program may use at most 64 MiB of HBM per device.

```python
import math
import jax
import jax.numpy as jnp
from jax import lax

LEAF = 128
RANK = 64
NRHS = 32
CHILD = 8
REACH = 16
NEAR = 16
FAR = 16
FAR_NODE = 32
LEAF_DEV = 32
LEAVES = 512
PANELS = 65536
NODES = 64


def draw_leaf_target(key, part):
    shards = LEAVES // LEAF_DEV
    per_peer = LEAF_DEV // shards
    first_key, second_key = jax.random.split(jax.random.fold_in(key, 11))
    sender_order = jax.vmap(lambda item: jax.random.permutation(item, LEAF_DEV))(jax.random.split(first_key, shards))
    receiver_order = jax.vmap(lambda item: jax.random.permutation(item, LEAF_DEV))(jax.random.split(second_key, shards))
    sender_ids = jnp.arange(shards, dtype=jnp.int32)[:, None, None]
    receiver_ids = jnp.arange(shards, dtype=jnp.int32)[None, :, None]
    slab_pos = sender_ids * LEAF_DEV + sender_order.reshape(shards, shards, per_peer).astype(jnp.int32)
    tree_pos = receiver_ids * LEAF_DEV + receiver_order.reshape(shards, shards, per_peer).transpose(1, 0, 2).astype(jnp.int32)
    return jnp.zeros((LEAVES,), jnp.int32).at[slab_pos.reshape(-1)].set(tree_pos.reshape(-1))


def leaf_lists(key):
    first_key, second_key, third_key = jax.random.split(jax.random.fold_in(key, 5), 3)
    offsets = jnp.concatenate([jnp.arange(-REACH, 0), jnp.arange(1, REACH + 1)]).astype(jnp.int32)
    order = jax.vmap(lambda item: jax.random.permutation(item, 2 * REACH))(jax.random.split(first_key, LEAVES))
    chosen = offsets[order]
    target = jnp.arange(LEAVES, dtype=jnp.int32)[:, None]
    source = target + chosen
    inside = (source >= 0) & (source < LEAVES)
    near_live = jax.random.randint(second_key, (LEAVES, 1), NEAR // 4, NEAR)
    far_live = jax.random.randint(third_key, (LEAVES, 1), FAR // 2, FAR + 1)
    near_keep = inside[:, :NEAR - 1] & (jnp.arange(NEAR - 1)[None, :] < near_live)
    near_rows = jnp.concatenate([target, jnp.where(near_keep, source[:, :NEAR - 1], -1)], axis=1)
    far_keep = inside[:, NEAR - 1:NEAR - 1 + FAR] & (jnp.arange(FAR)[None, :] < far_live)
    far_rows = jnp.where(far_keep, source[:, NEAR - 1:NEAR - 1 + FAR], -1)
    return (near_rows.astype(jnp.int32), far_rows.astype(jnp.int32))


def draw_near_list(key, part):
    return leaf_lists(key)[0]


def draw_far_list(key, part):
    return leaf_lists(key)[1]


def draw_node_list(key, part):
    first_key, second_key = jax.random.split(jax.random.fold_in(key, 9))
    order = jax.vmap(lambda item: jax.random.permutation(item, NODES))(jax.random.split(first_key, NODES)).astype(jnp.int32)
    owner = jnp.arange(NODES, dtype=jnp.int32)[:, None]
    closeby = (jnp.abs(order - owner) <= 2).astype(jnp.int32)
    places = jnp.argsort(closeby, axis=1, stable=True)[:, :FAR_NODE]
    picked = jnp.take_along_axis(order, places, axis=1)
    live_count = jax.random.randint(second_key, (NODES, 1), FAR_NODE // 2, FAR_NODE + 1)
    return jnp.where(jnp.arange(FAR_NODE)[None, :] < live_count, picked, -1).astype(jnp.int32)


def steps_of(stream_key, shape, cuts, low, largest):
    loudness, own = 1.0, jax.random.fold_in(stream_key, 6)
    for dim, shards_of in cuts:
        draws = jnp.exp(jax.random.uniform(jax.random.fold_in(own, dim), (shards_of,), jnp.float32, low / len(cuts), largest / len(cuts)))
        loudness = loudness * jnp.repeat(draws, shape[dim] // shards_of).reshape([-1 if axis == dim else 1 for axis in range(len(shape))])
    return loudness


def normal_values(own_key, shape, width, limit, cuts=(), kind=jnp.bfloat16):
    level = steps_of(own_key, shape, cuts, -0.22, 0.18) if cuts else 1.0
    result = jax.random.normal(own_key, shape, jnp.float32) * width * level
    return jnp.minimum(jnp.maximum(result, -limit), limit).astype(kind)


def setup_inputs(seed: int = 0, part: int = 0) -> dict:
    arg_keys = jax.random.split(jax.random.key(seed), 11)
    part_keys = jax.random.split(jax.random.fold_in(arg_keys[10], part), 11)
    density = normal_values(part_keys[0], (LEAVES, NRHS, LEAF), 1.0, 6.0, ((0, 16),))
    leaf_target = draw_leaf_target(jax.random.fold_in(jax.random.fold_in(arg_keys[10], part), 71), part)
    geometry = normal_values(part_keys[2], (6, PANELS), 1.0, 6.0, ((1, 16),), jnp.float32)
    near_list = draw_near_list(jax.random.fold_in(jax.random.fold_in(arg_keys[10], part), 71), part)
    far_list = draw_far_list(jax.random.fold_in(jax.random.fold_in(arg_keys[10], part), 71), part)
    node_list = draw_node_list(jax.random.fold_in(jax.random.fold_in(arg_keys[10], part), 71), part)
    basis_in = normal_values(part_keys[6], (LEAVES, RANK, LEAF), LEAF ** -0.5, 0.5, ((0, 16),))
    basis_out = normal_values(part_keys[7], (LEAVES, RANK, LEAF), RANK ** -0.5, 0.75, ((0, 16),))
    transfer = normal_values(part_keys[8], (NODES, RANK, CHILD * RANK), (CHILD * RANK) ** -0.5, 0.25, ((0, 16),))
    node_points = normal_values(part_keys[9], (3, NODES * RANK), 1.0, 6.0, (), jnp.float32)
    return {"density": density, "leaf_target": leaf_target, "geometry": geometry, "near_list": near_list, "far_list": far_list, "node_list": node_list, "basis_in": basis_in, "basis_out": basis_out, "transfer": transfer, "node_points": node_points}


smoothing = 0.1
inv_four_pi = 0.25 / math.pi

def coupling(targets, sources):
    spread = targets - sources
    return inv_four_pi / jnp.sqrt(lax.optimization_barrier(jnp.sum(spread * spread, axis=0)) + smoothing * smoothing)

def double_layer(targets, sources, normals):
    spread = targets - sources
    distance = lax.optimization_barrier(jnp.sum(spread * spread, axis=0)) + smoothing * smoothing
    return inv_four_pi * lax.optimization_barrier(jnp.sum(normals * spread, axis=0)) / (distance * jnp.sqrt(distance))

def reference(density, leaf_target, geometry, near_list, far_list, node_list, basis_in, basis_out, transfer, node_points):
    source_rows = jnp.argsort(leaf_target).astype(jnp.int32)
    ordered = density[source_rows]
    skeleton = jnp.einsum('tnl,trl->tnr', ordered.astype(jnp.float32), basis_in.astype(jnp.float32)).astype(jnp.bfloat16)
    stacked = skeleton.reshape(NODES, CHILD, NRHS, RANK).transpose(0, 2, 1, 3).reshape(NODES, NRHS, CHILD * RANK)
    node_skel = jnp.einsum('pnk,prk->pnr', stacked.astype(jnp.float32), transfer.astype(jnp.float32)).astype(jnp.bfloat16)
    shaped = geometry.reshape(6, LEAVES, LEAF)
    proxies = shaped[0:3, :, :RANK]
    node_pts = node_points.reshape(3, NODES, RANK)
    leaf_ids = jnp.arange(LEAVES, dtype=jnp.int32)
    node_ids = jnp.arange(NODES, dtype=jnp.int32)
    zero_half = jnp.zeros((), jnp.bfloat16)

    def leaf_far_block(packed):
        target_ids, entries = packed
        usable = entries >= 0
        sources = jnp.where(usable, entries, 0)
        weights = coupling(proxies[:, target_ids][:, :, None, :, None], proxies[:, sources][:, :, :, None, :]).astype(jnp.bfloat16)
        skel_src = jnp.where(usable[:, :, None, None], skeleton[sources], zero_half)
        return jnp.einsum('bsij,bsnj->bni', weights.astype(jnp.float32), skel_src.astype(jnp.float32))
    leaf_far = lax.map(leaf_far_block, (leaf_ids.reshape(-1, 16), far_list.reshape(-1, 16, FAR))).reshape(LEAVES, NRHS, RANK)

    def node_far_block(packed):
        target_ids, entries = packed
        usable = entries >= 0
        sources = jnp.where(usable, entries, 0)
        weights = coupling(node_pts[:, target_ids][:, :, None, :, None], node_pts[:, sources][:, :, :, None, :]).astype(jnp.bfloat16)
        skel_src = jnp.where(usable[:, :, None, None], node_skel[sources], zero_half)
        return jnp.einsum('bsij,bsnj->bni', weights.astype(jnp.float32), skel_src.astype(jnp.float32))
    node_far = lax.map(node_far_block, (node_ids.reshape(-1, 8), node_list.reshape(-1, 8, FAR_NODE))).reshape(NODES, NRHS, RANK).astype(jnp.bfloat16)
    down = jnp.einsum('pnr,prk->pnk', node_far.astype(jnp.float32), transfer.astype(jnp.float32))
    down = down.reshape(NODES, NRHS, CHILD, RANK).transpose(0, 2, 1, 3).reshape(LEAVES, NRHS, RANK)
    local = (leaf_far + down).astype(jnp.bfloat16)
    far_out = jnp.einsum('tnr,trl->tnl', local.astype(jnp.float32), basis_out.astype(jnp.float32))

    def near_block(packed):
        target_ids, entries = packed
        usable = entries >= 0
        sources = jnp.where(usable, entries, 0)
        source_geo = shaped[:, sources]
        kernel = double_layer(shaped[0:3, target_ids][:, :, None, :, None], source_geo[0:3][:, :, :, None, :], source_geo[3:6][:, :, :, None, :]).astype(jnp.bfloat16)
        dens_src = jnp.where(usable[:, :, None, None], ordered[sources], zero_half)
        return jnp.einsum('bsij,bsnj->bni', kernel.astype(jnp.float32), dens_src.astype(jnp.float32))
    near_out = lax.map(near_block, (leaf_ids.reshape(-1, 16), near_list.reshape(-1, 16, NEAR))).reshape(LEAVES, NRHS, LEAF)
    return (near_out + far_out).astype(jnp.bfloat16)
```

```python
import math

import jax
import jax.numpy as jnp
from jax import lax
from jax.experimental import pallas as pl
from jax.experimental.pallas import tpu as pltpu
from jax.sharding import PartitionSpec as P

REACH = 16
AXES = ("row", "col")

smoothing = 0.1
inv_four_pi = 0.25 / math.pi
grid_step = 16.0
tiles = 9
bf16 = jnp.bfloat16
f32 = jnp.float32


def split3(x):
    first = x.astype(bf16).astype(f32)
    rest = x - first
    second = rest.astype(bf16).astype(f32)
    third = (rest - second).astype(bf16).astype(f32)
    return first, second, third


def iota(shape, axis):
    return lax.broadcasted_iota(jnp.int32, shape, axis)


def dot(a, b):
    return lax.dot_general(a, b, (((1,), (0,)), ((), ())), preferred_element_type=f32)


def dot_t(a, b):
    return lax.dot_general(a, b, (((1,), (1,)), ((), ())), preferred_element_type=f32)


class Features:
    def __init__(self, g):
        self.shape = g.shape
        self.row = row = iota(g.shape, 0)
        self.point = point = row < 3
        c = jnp.where(point, g, 0.0)
        self.whole = whole = jnp.floor(c * grid_step + 0.5) * (1.0 / grid_step)
        part = c - whole
        self.part = split3(part)
        m = jnp.where(point, 0.0, g) * inv_four_pi
        self.m = split3(m)
        norm = jnp.sum(whole * whole, axis=0, keepdims=True)
        self.norm_hi = jnp.floor(norm)
        self.norm_lo = norm - self.norm_hi
        self.cross = jnp.sum(part * (2.0 * whole + part), axis=0, keepdims=True)
        self.q = split3(jnp.sum(m * pltpu.roll(c, 3, 0), axis=0, keepdims=True))

    def tile(self, points, normals, six, seven):
        row = self.row
        x = jnp.where(row == 7, seven, jnp.where(row == 6, six, 0.0))
        if normals is not None:
            x = jnp.where((row >= 3) & (row < 6), normals, x)
        if points is not None:
            x = jnp.where(row < 3, points, x)
        return x

    def stack(self, parts):
        return jnp.concatenate(
            parts + [jnp.zeros((128 - 8 * len(parts), self.shape[1]), f32)], axis=0
        )

    def source(self):
        w, (p0, p1, p2), (m0, m1, m2) = self.whole, self.part, self.m
        c0, c1, c2 = split3(self.cross)
        q0, q1, q2 = self.q
        points = [w, w, w, p0, p1, p2, p0, p1, p0]
        normals = [m0, m1, m2, m0, m0, m0, m1, m1, m2]
        extra = [(self.norm_hi, self.norm_lo), (1.0, 1.0), (1.0, c0), (c1, c2), (q0, q1), (q2, 0.0)]
        extra += [(0.0, 0.0)] * 3
        return self.stack([self.tile(a, b, *e) for a, b, e in zip(points, normals, extra)])

    def target(self):
        w, (p0, p1, p2) = self.whole, self.part
        c0, c1, c2 = split3(self.cross + smoothing * smoothing)
        none = (0.0, 0.0)
        exact = self.stack(
            [
                self.tile(-2.0 * w, None, 1.0, 1.0),
                self.tile(None, None, self.norm_hi, self.norm_lo),
            ]
        )
        points = [p0, p1, p2, w, w, w, p0, p0, p1]
        extra = [none, (c0, c1), (c2, 1.0), (1.0, 1.0)] + [none] * 5
        rest = self.stack([self.tile(-2.0 * a, None, *e) for a, e in zip(points, extra)])
        w3, p03, p13, p23 = (pltpu.roll(x, 3, 0) for x in (w, p0, p1, p2))
        normals = [w3, w3, w3, p03, p13, p23, p03, p13, p03]
        extra = [none] * 4 + [(-1.0, -1.0), (-1.0, 0.0)] + [none] * 3
        normal = self.stack([self.tile(None, b, *e) for b, e in zip(normals, extra)])
        return exact, rest, normal


def halves(x):
    left = iota(x.shape, 1) < 64
    a = jnp.where(left, x, 0.0)
    b = jnp.where(left, 0.0, x)
    return (a, pltpu.roll(a, 64, 1)), (pltpu.roll(b, 64, 1), b)


def pair_weights(exact, rest):
    return [
        jnp.concatenate(
            [jnp.concatenate([e[0], r[0]], axis=1), jnp.concatenate([e[1], r[1]], axis=1)], axis=0
        ).astype(bf16)
        for e, r in zip(halves(exact), halves(rest))
    ]


def pack_kernel(target_ref, density_ref, out_ref, count_ref, slot_ref, *, peers, per):
    leaves, nrhs, leaf = density_ref.shape
    for d in range(peers):
        count_ref[d] = 0
    for k in range(leaves):
        t = target_ref[k]
        d = t // leaves
        c = count_ref[d]
        count_ref[d] = c + 1
        slot_ref[d * per + c] = t - d * leaves
        out_ref[d, pl.ds(pl.multiple_of(c * nrhs, nrhs), nrhs), :] = density_ref[k]
    row = iota((16, leaf), 0)
    for d in range(peers):
        x = jnp.zeros((16, leaf), f32)
        for c in range(per):
            x = jnp.where(row == c, slot_ref[d * per + c].astype(f32), x)
        out_ref[d, per * nrhs :, :] = x.astype(bf16)


def feature_kernel(
    geo_ref, node_ref, fs_ref, ft_ref, wf_ref, split_ref, fsn_ref, wfn_ref, pad_ref, npad_ref, *, index
):
    leaves = fs_ref.shape[0]
    nodes_here = wfn_ref.shape[0]
    pad_ref[...] = jnp.zeros(pad_ref.shape, f32)
    pad_ref[0:6, :] = geo_ref[...]
    npad_ref[...] = jnp.zeros(npad_ref.shape, f32)
    npad_ref[0:3, :] = node_ref[...]

    def leaf_step(l, _):
        g = pad_ref[:, pl.ds(pl.multiple_of(l * 128, 128), 128)]
        f = Features(g)
        fs_ref[l] = f.source().T.astype(bf16)
        exact, rest, normal = f.target()
        ft_ref[l] = jnp.concatenate([exact, rest, normal], axis=1).astype(bf16)
        wf_ref[l] = pair_weights(exact, rest)[0]
        return 0

    lax.fori_loop(0, leaves, leaf_step, 0)

    def split_step(l, _):
        parts = []
        for k in range(2):
            parts += split3(pad_ref[:, pl.ds(pl.multiple_of((l * 2 + k) * 128, 128), 128)])
        split_ref[pl.ds(pl.multiple_of(l * 48, 48), 48), :] = jnp.concatenate(parts, axis=0).astype(bf16)
        return 0

    lax.fori_loop(0, leaves // 2, split_step, 0)

    def node_step(l, _):
        f = Features(npad_ref[:, pl.ds(pl.multiple_of(l * 128, 128), 128)])
        fsn_ref[l] = f.source().T.astype(bf16)
        return 0

    lax.fori_loop(0, fsn_ref.shape[0], node_step, 0)
    first = lax.axis_index(AXES) * (nodes_here // 2)
    for l in range(nodes_here // 2):
        f = Features(npad_ref[:, pl.ds(pl.multiple_of((first + l) * 128, 128), 128)])
        exact, rest, _ = f.target()
        wfn_ref[2 * l], wfn_ref[2 * l + 1] = pair_weights(exact, rest)


def skeleton_kernel(
    arrived_ref, basis_ref, transfer_ref, split_ref, own_ref, a_ref, b_ref, node_ref, *, per
):
    peers = arrived_ref.shape[0]
    leaves = peers * per
    nrhs = 32
    half = leaves // 2
    for d in range(peers):
        slots = arrived_ref[d, per * nrhs :, :].astype(f32).astype(jnp.int32)
        for c in range(per):
            s = slots[c, 0]
            h = s // half
            own_ref[h, pl.ds(pl.multiple_of((s - h * half) * nrhs, nrhs), nrhs), :] = arrived_ref[
                d, c * nrhs : (c + 1) * nrhs, :
            ]
    left = iota((nrhs, 128), 1) < 64
    skels = []
    for p in range(leaves // 2):
        h, q = divmod(p, half // 2)
        out = dot_t(own_ref[h, q * 64 : (q + 1) * 64, :], basis_ref[p])
        pair = jnp.where(left, out[:nrhs], out[nrhs:]).astype(bf16)
        own_ref[h, half * nrhs + q * nrhs : half * nrhs + (q + 1) * nrhs, :] = pair
        skels.append(pair)
    base = half * nrhs + (half // 2) * nrhs
    n_split = half * 24
    for h in range(2):
        own_ref[h, base : base + n_split, :] = split_ref[h * n_split : (h + 1) * n_split, :]
    kids = transfer_ref.shape[2] // 128
    n_pairs = len(skels) // (2 * kids)
    for p in range(n_pairs):
        stack = jnp.concatenate(
            [jnp.concatenate(skels[(2 * p + h) * kids : (2 * p + h + 1) * kids], axis=1) for h in range(2)], axis=0
        )
        out = dot_t(stack, transfer_ref[p])
        pair = jnp.where(left, out[:nrhs], out[nrhs:]).astype(bf16)
        for d in range(peers):
            node_ref[d, p * nrhs : (p + 1) * nrhs, :] = pair
    odd = lax.axis_index(AXES) % 2
    a_ref[...] = own_ref[1 - odd]
    b_ref[...] = own_ref[odd]


def spread(pair, lo_ref, hi_ref, k):
    (a, a_hi), (b_lo, b) = halves(pair.astype(f32))
    lo_ref[k] = a.astype(bf16)
    hi_ref[k] = a_hi.astype(bf16)
    lo_ref[k + 1] = b_lo.astype(bf16)
    hi_ref[k + 1] = b.astype(bf16)


def far_group(ids, clamp, features, weights, lo_ref, hi_ref):
    f = [features(jnp.minimum(s, clamp)) for s in ids]
    x = jnp.concatenate(
        [jnp.concatenate([f[0], f[1]], axis=1), jnp.concatenate([f[2], f[3]], axis=1)], axis=0
    )
    out = dot(x, weights)
    g = (lax.rsqrt(out[:, :128] + out[:, 128:]) * inv_four_pi).astype(bf16)
    lhs = jnp.concatenate(
        [lo_ref[ids[0]] + hi_ref[ids[2]], lo_ref[ids[1]] + hi_ref[ids[3]]], axis=0
    )
    return dot(lhs, g)


def leaf_kernel(
    near_ref, far_ref, fs_own_ref, ft_ref, wf_ref, own_ref, a_ref, b_ref,
    near_out, far_out,
    fs_ref, dens_ref, lo_ref, hi_ref, got_ref, list_ref, count_ref,
):
    leaves = ft_ref.shape[0]
    nrhs = 32
    half = leaves // 2
    wide = leaves + 2 * REACH
    index = lax.axis_index(AXES)
    first = index * leaves - REACH
    odd = index % 2
    slots = near_ref.shape[1]

    def compact(t, _):
        c = t * slots
        for k in range(slots):
            e = near_ref[t, k]
            list_ref[c] = e - first
            c = c + jnp.where(e >= 0, 1, 0)
        for k in range(4):
            list_ref[c + k] = wide
        count_ref[t] = c - t * slots
        return 0

    got_ref[0] = a_ref[...]
    got_ref[1] = b_ref[...]
    base = half * nrhs + (half // 2) * nrhs
    fs_ref[REACH : REACH + leaves] = fs_own_ref[...]
    for side, k in ((1 - odd, 0), (odd, REACH + leaves)):

        def halo(l, _, side=side, k=k):
            x = got_ref[side, pl.ds(pl.multiple_of(base + l * 48, 16), 48), :].astype(f32)
            for j in range(2):
                g = x[24 * j : 24 * j + 8] + x[24 * j + 8 : 24 * j + 16] + x[24 * j + 16 : 24 * j + 24]
                fs_ref[k + 2 * l + j] = Features(g).source().T.astype(bf16)
            return 0

        lax.fori_loop(0, half // 2, halo, 0)

    def fill(view, k):
        for l in range(half):
            dens_ref[k + l] = view(l * nrhs, nrhs)
        for l in range(half // 2):
            spread(view(half * nrhs + l * nrhs, nrhs), lo_ref, hi_ref, k + 2 * l)

    fill(lambda at, n: got_ref[1 - odd, at : at + n, :], 0)
    fill(lambda at, n: own_ref[0, at : at + n, :], REACH)
    fill(lambda at, n: own_ref[1, at : at + n, :], REACH + half)
    fill(lambda at, n: got_ref[odd, at : at + n, :], REACH + leaves)
    zero = jnp.zeros((nrhs, 128), bf16)
    dens_ref[wide] = zero
    lo_ref[wide] = zero
    hi_ref[wide] = zero

    lax.fori_loop(0, leaves, compact, 0)

    def near_leaf(t, _):
        weights = ft_ref[t]

        def group(j, acc):
            for u in range(4):
                w = list_ref[t * slots + j * 4 + u]
                out = dot(fs_ref[jnp.minimum(w, wide - 1)], weights)
                r = lax.rsqrt(out[:, :128] + out[:, 128:256])
                k = ((out[:, 256:] * r) * (r * r)).astype(bf16)
                acc = acc + dot(dens_ref[w], k)
            return acc

        groups = (count_ref[t] + 3) // 4
        near_out[t] = lax.fori_loop(0, groups, group, jnp.zeros((nrhs, 128), f32))
        return 0

    lax.fori_loop(0, leaves, near_leaf, 0)

    left = iota((nrhs, 128), 1) < 64
    far_slots = far_ref.shape[1]

    def far_pair(p, _):
        total = []
        for h in range(2):
            t = 2 * p + h
            acc = jnp.zeros((2 * nrhs, 128), f32)
            for j in range(far_slots // 4):
                ids = []
                for u in range(4):
                    e = far_ref[t, 4 * j + u]
                    ids.append(jnp.where(e < 0, wide, e - first))
                acc = acc + far_group(
                    ids, wide - 1, lambda s: fs_ref[s, 0:64, :], wf_ref[t], lo_ref, hi_ref
                )
            total.append(acc)
        e, o = total
        even = e[:nrhs] + pltpu.roll(e[nrhs:], 64, 1)
        odd_ = pltpu.roll(o[:nrhs], 64, 1) + o[nrhs:]
        far_out[p] = jnp.where(left, even, odd_)
        return 0

    lax.fori_loop(0, leaves // 2, far_pair, 0)


def node_kernel(
    list_ref, near_ref, far_ref, skel_ref, fsn_ref, wfn_ref, transfer_ref, basis_ref,
    out_ref,
    lo_ref, hi_ref,
):
    nrhs = 32
    nodes_here = wfn_ref.shape[0]
    pairs = skel_ref.shape[0]
    for p in range(pairs):
        spread(skel_ref[p], lo_ref, hi_ref, 2 * p)
    zero = jnp.zeros((nrhs, 128), bf16)
    lo_ref[2 * pairs] = zero
    hi_ref[2 * pairs] = zero
    slots = list_ref.shape[1]
    left = iota((nrhs, 128), 1) < 64
    kids = transfer_ref.shape[2] // 128

    def node(p, _):
        acc = jnp.zeros((2 * nrhs, 128), f32)
        for j in range(slots // 4):
            ids = []
            for u in range(4):
                e = list_ref[p, 4 * j + u]
                ids.append(jnp.where(e < 0, 2 * pairs, e))
            acc = acc + far_group(
                ids, 2 * pairs - 1,
                lambda s: fsn_ref[s // 2, pl.ds(pl.multiple_of((s % 2) * 64, 64), 64), :],
                wfn_ref[p], lo_ref, hi_ref,
            )
        x = acc[:nrhs] + pltpu.roll(acc[nrhs:], 64, 1)
        down = dot(x[:, :64].astype(bf16), transfer_ref[p])
        for c in range(kids):
            q = p * kids + c
            local = (far_ref[q] + down[:, c * 128 : (c + 1) * 128]).astype(bf16).astype(f32)
            both = jnp.concatenate(
                [jnp.where(left, local, 0.0), jnp.where(left, 0.0, local)], axis=0
            ).astype(bf16)
            y = dot(both, basis_ref[q])
            out_ref[2 * q] = (near_ref[2 * q] + y[:nrhs]).astype(bf16)
            out_ref[2 * q + 1] = (near_ref[2 * q + 1] + y[nrhs:]).astype(bf16)
        return 0

    lax.fori_loop(0, nodes_here, node, 0)


def vmem():
    return pl.BlockSpec(memory_space=pltpu.VMEM)


def smem():
    return pl.BlockSpec(memory_space=pltpu.SMEM)


def call(kernel, out, in_specs, scratch, name, flops):
    many = isinstance(out, tuple)
    return pl.pallas_call(
        kernel,
        out_shape=out,
        in_specs=in_specs,
        out_specs=tuple(vmem() for _ in out) if many else vmem(),
        scratch_shapes=scratch,
        name=name,
        cost_estimate=pl.CostEstimate(flops=flops, bytes_accessed=1 << 20, transcendentals=0),
        compiler_params=pltpu.CompilerParams(vmem_limit_bytes=56 << 20),
    )


def on_device(
    density, leaf_target, geometry, near_list, far_list, node_list, basis_in, basis_out, transfer, node_points
):
    leaves, nrhs, leaf = density.shape
    nodes_here = transfer.shape[0]
    peers = lax.axis_size(AXES)
    per = leaves // peers
    half = leaves // 2
    nodes = node_points.shape[1] // 64
    wide = leaves + 2 * REACH
    shape = jax.ShapeDtypeStruct

    outgoing = call(
        lambda *r: pack_kernel(*r, peers=peers, per=per),
        shape((peers, per * nrhs + 16, leaf), bf16),
        [smem(), vmem()],
        [pltpu.SMEM((peers,), jnp.int32), pltpu.SMEM((leaves,), jnp.int32)],
        "pack",
        1 << 20,
    )(leaf_target, density)
    arrived = lax.all_to_all(outgoing, AXES, split_axis=0, concat_axis=0, tiled=True)

    fs, ft, wf, split, fsn, wfn = call(
        lambda *r: feature_kernel(*r, index=None),
        (
            shape((leaves, 128, 128), bf16),
            shape((leaves, 128, 384), bf16),
            shape((leaves, 256, 256), bf16),
            shape((leaves * 24, 128), bf16),
            shape((nodes // 2, 128, 128), bf16),
            shape((nodes_here, 256, 256), bf16),
        ),
        [vmem(), vmem()],
        [pltpu.VMEM((8, leaves * leaf), f32), pltpu.VMEM((8, nodes * 64), f32)],
        "features",
        1 << 30,
    )(geometry, node_points)

    rows = half * nrhs + (half // 2) * nrhs + half * 24
    own, to_a, to_b, node_out = call(
        lambda *r: skeleton_kernel(*r, per=per),
        (
            shape((2, rows, 128), bf16),
            shape((rows, 128), bf16),
            shape((rows, 128), bf16),
            shape((peers, nodes_here // 2 * nrhs, 128), bf16),
        ),
        [vmem()] * 4,
        [],
        "skeleton",
        1 << 26,
    )(
        arrived,
        basis_in.reshape(leaves // 2, 128, leaf),
        transfer.reshape(nodes_here // 2, 128, -1),
        split,
    )
    all_skel = lax.all_to_all(node_out, AXES, split_axis=0, concat_axis=0, tiled=True)
    swap_a = [(i, i ^ 1) for i in range(peers)]
    swap_b = [(i, i + 1) for i in range(1, peers - 1, 2)] + [(i + 1, i) for i in range(1, peers - 1, 2)]
    got_a = lax.ppermute(to_a, AXES, swap_a)
    got_b = lax.ppermute(to_b, AXES, swap_b)

    near, far = call(
        leaf_kernel,
        (shape((leaves, nrhs, leaf), f32), shape((leaves // 2, nrhs, 128), f32)),
        [smem(), smem()] + [vmem()] * 6,
        [
            pltpu.VMEM((wide, 128, 128), bf16),
            pltpu.VMEM((wide + 1, nrhs, 128), bf16),
            pltpu.VMEM((wide + 1, nrhs, 128), bf16),
            pltpu.VMEM((wide + 1, nrhs, 128), bf16),
            pltpu.VMEM((2, rows, 128), bf16),
            pltpu.SMEM((leaves * near_list.shape[1] + 8,), jnp.int32),
            pltpu.SMEM((leaves,), jnp.int32),
        ],
        "leaves",
        1 << 31,
    )(near_list, far_list, fs, ft, wf, own, got_a, got_b)

    return call(
        node_kernel,
        shape((leaves, nrhs, leaf), bf16),
        [smem()] + [vmem()] * 7,
        [pltpu.VMEM((nodes + 1, nrhs, 128), bf16), pltpu.VMEM((nodes + 1, nrhs, 128), bf16)],
        "nodes",
        1 << 28,
    )(
        node_list,
        near,
        far,
        all_skel.reshape(nodes // 2, nrhs, 128),
        fsn,
        wfn,
        transfer,
        basis_out.reshape(leaves // 2, 128, leaf),
    )


def solution(mesh):
    split = ("grp", "row", "col")
    return jax.shard_map(
        on_device,
        mesh=mesh,
        in_specs=(
            P(split, None, None),
            P(split),
            P(None, split),
            P(split, None),
            P(split, None),
            P(split, None),
            P(split, None, None),
            P(split, None, None),
            P(split, None, None),
            P(None, "grp"),
        ),
        out_specs=P(split, None, None),
        check_vma=False,
    )
```

```python
import math

import jax
import jax.numpy as jnp
from jax import lax
from jax.experimental import pallas as pl
from jax.experimental.pallas import tpu as pltpu
from jax.sharding import PartitionSpec as P

REACH = 16
AXES = ("row", "col")

smoothing = 0.1
inv_four_pi = 0.25 / math.pi
grid_step = 16.0
tiles = 9
bf16 = jnp.bfloat16
f32 = jnp.float32


def split3(x):
    first = x.astype(bf16).astype(f32)
    rest = x - first
    second = rest.astype(bf16).astype(f32)
    third = (rest - second).astype(bf16).astype(f32)
    return first, second, third


def iota(shape, axis):
    return lax.broadcasted_iota(jnp.int32, shape, axis)


def dot(a, b):
    return lax.dot_general(a, b, (((1,), (0,)), ((), ())), preferred_element_type=f32)


def dot_t(a, b):
    return lax.dot_general(a, b, (((1,), (1,)), ((), ())), preferred_element_type=f32)


class Features:
    def __init__(self, g):
        self.shape = g.shape
        self.row = row = iota(g.shape, 0)
        self.point = point = row < 3
        c = jnp.where(point, g, 0.0)
        self.whole = whole = jnp.floor(c * grid_step + 0.5) * (1.0 / grid_step)
        part = c - whole
        self.part = split3(part)
        m = jnp.where(point, 0.0, g) * inv_four_pi
        self.m = split3(m)
        norm = jnp.sum(whole * whole, axis=0, keepdims=True)
        self.norm_hi = jnp.floor(norm)
        self.norm_lo = norm - self.norm_hi
        self.cross = jnp.sum(part * (2.0 * whole + part), axis=0, keepdims=True)
        self.q = split3(jnp.sum(m * pltpu.roll(c, 3, 0), axis=0, keepdims=True))

    def tile(self, points, normals, six, seven):
        row = self.row
        x = jnp.where(row == 7, seven, jnp.where(row == 6, six, 0.0))
        if normals is not None:
            x = jnp.where((row >= 3) & (row < 6), normals, x)
        if points is not None:
            x = jnp.where(row < 3, points, x)
        return x

    def first(self, points, three, four, five, six):
        row = self.row
        x = jnp.where(row == 3, three, jnp.where(row == 4, four, 0.0))
        x = jnp.where(row == 5, five, jnp.where(row == 6, six, x))
        return jnp.where(row < 3, points, x)

    def stack(self, parts):
        return jnp.concatenate(
            parts + [jnp.zeros((128 - 8 * len(parts), self.shape[1]), f32)], axis=0
        )

    def source(self):
        w, (p0, p1, p2), (m0, m1, m2) = self.whole, self.part, self.m
        c0, c1, c2 = split3(self.cross)
        q0, q1, q2 = self.q
        points = [w, w, w, p0, p1, p2, p0, p1, p0]
        normals = [m0, m1, m2, m0, m0, m0, m1, m1, m2]
        extra = [(1.0, 1.0), (1.0, c0), (c1, c2), (q0, q1), (q2, 0.0)] + [(0.0, 0.0)] * 4
        return self.stack(
            [self.first(w, self.norm_hi, self.norm_lo, 1.0, 1.0)]
            + [self.tile(a, b, *e) for a, b, e in zip(points, normals, extra)]
        )

    def target(self):
        w, (p0, p1, p2) = self.whole, self.part
        c0, c1, c2 = split3(self.cross + smoothing * smoothing)
        none = (0.0, 0.0)
        points = [p0, p1, p2, w, w, w, p0, p0, p1]
        extra = [(c0, c1), (c2, 1.0), (1.0, 1.0)] + [none] * 6
        square = self.stack(
            [self.first(-2.0 * w, 1.0, 1.0, self.norm_hi, self.norm_lo)]
            + [self.tile(-2.0 * a, None, *e) for a, e in zip(points, extra)]
        )
        w3, p03, p13, p23 = (pltpu.roll(x, 3, 0) for x in (w, p0, p1, p2))
        normals = [w3, w3, w3, p03, p13, p23, p03, p13, p03]
        extra = [none] * 3 + [(-1.0, -1.0), (-1.0, 0.0)] + [none] * 4
        normal = self.stack(
            [jnp.zeros(self.shape, f32)] + [self.tile(None, b, *e) for b, e in zip(normals, extra)]
        )
        return square, normal


def halves(x):
    left = iota(x.shape, 1) < 64
    a = jnp.where(left, x, 0.0)
    b = jnp.where(left, 0.0, x)
    return (a, pltpu.roll(a, 64, 1)), (pltpu.roll(b, 64, 1), b)


def pair_weights(square):
    return [jnp.concatenate(x, axis=0).astype(bf16) for x in halves(square)]


def compact(entries, first, dead):
    slots, targets = entries.shape
    place = iota(entries.shape, 0)
    out = jnp.full(entries.shape, dead, jnp.int32)
    count = jnp.zeros((1, targets), jnp.int32)
    for k in range(slots):
        e = entries[k : k + 1]
        live = e >= 0
        at = jnp.where(live, count, -1)
        out = jnp.where(place == at, e - first, out)
        count = count + jnp.where(live, 1, 0)
    return out, count


def pack_kernel(target_ref, density_ref, out_ref, count_ref, slot_ref, *, peers, per):
    leaves, nrhs, leaf = density_ref.shape
    for d in range(peers):
        count_ref[d] = 0
    for k in range(leaves):
        t = target_ref[k]
        d = t // leaves
        c = count_ref[d]
        count_ref[d] = c + 1
        slot_ref[d * per + c] = t - d * leaves
        out_ref[d, pl.ds(pl.multiple_of(c * nrhs, nrhs), nrhs), :] = density_ref[k]
    row = iota((16, leaf), 0)
    for d in range(peers):
        x = jnp.zeros((16, leaf), f32)
        for c in range(per):
            x = jnp.where(row == c, slot_ref[d * per + c].astype(f32), x)
        out_ref[d, per * nrhs :, :] = x.astype(bf16)


def feature_kernel(
    node_list_ref, geo_ref, node_ref, near_ref, far_ref,
    fs_ref, ft_ref, wf_ref, split_ref, gn_ref, list_ref,
    pad_ref, npad_ref, fsn_ref, wfn_ref,
):
    leaves = fs_ref.shape[0]
    nodes_here = wfn_ref.shape[0]
    slots = near_ref.shape[0]
    index = lax.axis_index(AXES)
    first = index * leaves - REACH
    wide = leaves + 2 * REACH
    pad_ref[...] = jnp.zeros(pad_ref.shape, f32)
    pad_ref[0:6, :] = geo_ref[...]
    npad_ref[...] = jnp.zeros(npad_ref.shape, f32)
    npad_ref[0:3, :] = node_ref[...]
    near, near_count = compact(near_ref[...], first, wide)
    far, far_count = compact(far_ref[...], first, wide)
    list_ref[0:slots] = near
    list_ref[slots : 2 * slots] = far
    list_ref[2 * slots : 2 * slots + 1] = near_count
    list_ref[2 * slots + 1 : 2 * slots + 2] = far_count

    def leaf_step(l, _):
        g = pad_ref[:, pl.ds(pl.multiple_of(l * 128, 128), 128)]
        f = Features(g)
        fs_ref[l] = f.source().T.astype(bf16)
        square, normal = f.target()
        ft_ref[l] = jnp.concatenate([square, normal], axis=1).astype(bf16)
        wf_ref[l] = pair_weights(square)[0]
        return 0

    lax.fori_loop(0, leaves, leaf_step, 0, unroll=4)

    def split_step(l, _):
        parts = []
        for k in range(2):
            parts += split3(pad_ref[:, pl.ds(pl.multiple_of((l * 2 + k) * 128, 128), 128)])
        split_ref[pl.ds(pl.multiple_of(l * 48, 48), 48), :] = jnp.concatenate(parts, axis=0).astype(bf16)
        return 0

    lax.fori_loop(0, leaves // 2, split_step, 0, unroll=4)

    def node_step(l, _):
        f = Features(npad_ref[:, pl.ds(pl.multiple_of(l * 128, 128), 128)])
        fsn_ref[l] = f.source().T.astype(bf16)
        return 0

    n_nodes = 2 * fsn_ref.shape[0]
    lax.fori_loop(0, n_nodes // 2, node_step, 0, unroll=4)
    chunk = index * (nodes_here // 2)
    for l in range(nodes_here // 2):
        f = Features(npad_ref[:, pl.ds(pl.multiple_of((chunk + l) * 128, 128), 128)])
        wfn_ref[2 * l], wfn_ref[2 * l + 1] = pair_weights(f.target()[0])

    node_slots = node_list_ref.shape[1]

    def node_field(p, _):
        x = []
        for j in range(node_slots // 2):
            pair = []
            for u in range(2):
                s = jnp.maximum(node_list_ref[p, (j // 2) * 4 + (j % 2) * 2 + u], 0)
                pair.append(fsn_ref[s // 2, pl.ds(pl.multiple_of((s % 2) * 64, 64), 64), :])
            x.append(jnp.concatenate(pair, axis=1))
        out = dot(jnp.concatenate(x, axis=0), wfn_ref[p])
        gn_ref[p] = (lax.rsqrt(out) * inv_four_pi).astype(bf16)
        return 0

    lax.fori_loop(0, nodes_here, node_field, 0)


def skeleton_kernel(
    arrived_ref, basis_ref, transfer_ref, split_ref, own_ref, a_ref, b_ref, node_ref, *, per
):
    peers = arrived_ref.shape[0]
    leaves = peers * per
    nrhs = 32
    half = leaves // 2
    for d in range(peers):
        slots = arrived_ref[d, per * nrhs :, :].astype(f32).astype(jnp.int32)
        for c in range(per):
            s = slots[c, 0]
            h = s // half
            own_ref[h, pl.ds(pl.multiple_of((s - h * half) * nrhs, nrhs), nrhs), :] = arrived_ref[
                d, c * nrhs : (c + 1) * nrhs, :
            ]
    left = iota((nrhs, 128), 1) < 64
    skels = []
    for p in range(leaves // 2):
        h, q = divmod(p, half // 2)
        out = dot_t(own_ref[h, q * 64 : (q + 1) * 64, :], basis_ref[p])
        pair = jnp.where(left, out[:nrhs], out[nrhs:]).astype(bf16)
        own_ref[h, half * nrhs + q * nrhs : half * nrhs + (q + 1) * nrhs, :] = pair
        skels.append(pair)
    base = half * nrhs + (half // 2) * nrhs
    n_split = half * 24
    for h in range(2):
        own_ref[h, base : base + n_split, :] = split_ref[h * n_split : (h + 1) * n_split, :]
    kids = transfer_ref.shape[2] // 128
    n_pairs = len(skels) // (2 * kids)
    for p in range(n_pairs):
        stack = jnp.concatenate(
            [jnp.concatenate(skels[(2 * p + h) * kids : (2 * p + h + 1) * kids], axis=1) for h in range(2)], axis=0
        )
        out = dot_t(stack, transfer_ref[p])
        pair = jnp.where(left, out[:nrhs], out[nrhs:]).astype(bf16)
        for d in range(peers):
            node_ref[d, p * nrhs : (p + 1) * nrhs, :] = pair
    odd = lax.axis_index(AXES) % 2
    a_ref[...] = own_ref[1 - odd]
    b_ref[...] = own_ref[odd]


def doubled(pairs, out_ref, k):
    rows = pairs.shape[0]
    i, j = iota((128, 256), 0), iota((128, 256), 1)
    pick = jnp.where(i == (j % 64) + 64 * (j // 128), 1.0, 0.0).astype(bf16)
    both = dot(pairs, pick).astype(bf16)
    for p in range(rows // 32):
        for h in range(2):
            out_ref[k + 2 * p + h] = both[32 * p : 32 * p + 32, 128 * h : 128 * h + 128]


def far_left(ids, skel_ref):
    left = iota((32, 128), 1) < 64
    cols = []
    for j in range(0, len(ids), 4):
        a, b, c, d = (skel_ref[s] for s in ids[j : j + 4])
        cols.append(jnp.concatenate([jnp.where(left, a, c), jnp.where(left, b, d)], axis=0))
    return jnp.concatenate(cols, axis=1)


def leaf_kernel(
    list_ref, fs_own_ref, ft_ref, wf_ref, own_ref, a_ref, b_ref,
    near_out, far_out,
    fs_ref, dens_ref, skel_ref, got_ref, k_ref, g_ref, item_ref,
):
    leaves = ft_ref.shape[0]
    nrhs = 32
    half = leaves // 2
    wide = leaves + 2 * REACH
    odd = lax.axis_index(AXES) % 2
    slots = (list_ref.shape[0] - 2) // 2
    groups = slots // 4

    got_ref[0] = a_ref[...]
    got_ref[1] = b_ref[...]
    base = half * nrhs + (half // 2) * nrhs
    fs_ref[REACH : REACH + leaves] = fs_own_ref[...]
    for side, k in ((1 - odd, 0), (odd, REACH + leaves)):

        def halo(l, _, side=side, k=k):
            x = got_ref[side, pl.ds(pl.multiple_of(base + l * 48, 16), 48), :].astype(f32)
            for j in range(2):
                g = x[24 * j : 24 * j + 8] + x[24 * j + 8 : 24 * j + 16] + x[24 * j + 16 : 24 * j + 24]
                fs_ref[k + 2 * l + j] = Features(g).source().T.astype(bf16)
            return 0

        lax.fori_loop(0, half // 2, halo, 0, unroll=2)

    item_ref[0] = 0
    n = 1
    for t in range(leaves):
        for g in range(groups):
            item_ref[n + g] = t * groups + g
        n = n + (list_ref[2 * slots, t] + 3) // 4
    item_ref[n] = 0

    def fill(view, k):
        for l in range(half):
            dens_ref[k + l] = view(l * nrhs, nrhs)
        doubled(view(half * nrhs, half // 2 * nrhs), skel_ref, k)

    fill(lambda at, n: got_ref[1 - odd, at : at + n, :], 0)
    fill(lambda at, n: own_ref[0, at : at + n, :], REACH)
    fill(lambda at, n: own_ref[1, at : at + n, :], REACH + half)
    fill(lambda at, n: got_ref[odd, at : at + n, :], REACH + leaves)
    dens_ref[wide] = jnp.zeros((nrhs, 128), bf16)
    skel_ref[wide] = jnp.zeros((nrhs, 128), bf16)
    k_ref[...] = jnp.zeros(k_ref.shape, bf16)
    g_ref[...] = jnp.zeros(g_ref.shape, bf16)
    near_out[...] = jnp.zeros(near_out.shape, f32)

    def source(s):
        return fs_ref[jnp.minimum(s, wide - 1)]

    def near_step(i, _):
        def ids_of(item):
            t = item // groups
            g = item - t * groups
            return t, [list_ref[g * 4 + u, t] for u in range(4)]

        t, ids = ids_of(item_ref[i - 1])
        lhs = jnp.concatenate([dens_ref[s] for s in ids], axis=1)
        near_out[t] += dot(lhs, k_ref[...]) * jnp.where(i > 1, 1.0, 0.0)
        t, ids = ids_of(item_ref[i])
        out = dot(jnp.concatenate([source(s) for s in ids], axis=0), ft_ref[t])
        r = lax.rsqrt(out[:, :128])
        k_ref[...] = ((out[:, 128:] * r) * (r * r)).astype(bf16)
        return 0

    lax.fori_loop(1, n + 1, near_step, 0)

    left = iota((nrhs, 128), 1) < 64

    def far_step(p, _):
        both = []
        for h in range(2):
            t = 2 * jnp.maximum(p - 1, 0) + h
            ids = [list_ref[slots + u, t] for u in range(slots)]
            both.append(dot(far_left(ids, skel_ref), g_ref[h]))
        e, o = both
        even = e[:nrhs] + pltpu.roll(e[nrhs:], 64, 1)
        odd_ = pltpu.roll(o[:nrhs], 64, 1) + o[nrhs:]
        far_out[jnp.maximum(p - 1, 0)] = jnp.where(left, even, odd_)
        for h in range(2):
            t = 2 * jnp.minimum(p, half - 1) + h
            ids = [list_ref[slots + u, t] for u in range(slots)]
            x = [
                jnp.concatenate([source(ids[j])[:64], source(ids[j + 1])[:64]], axis=1)
                for j in range(0, slots, 2)
            ]
            out = dot(jnp.concatenate(x, axis=0), wf_ref[t])
            g_ref[h] = (lax.rsqrt(out) * inv_four_pi).astype(bf16)
        return 0

    lax.fori_loop(0, half + 1, far_step, 0)


def node_kernel(
    list_ref, near_ref, far_ref, skel_ref, gn_ref, transfer_ref, basis_ref,
    out_ref,
    all_ref,
):
    nrhs = 32
    nodes_here = gn_ref.shape[0]
    pairs = skel_ref.shape[0] // nrhs
    doubled(skel_ref[...], all_ref, 0)
    all_ref[2 * pairs] = jnp.zeros((nrhs, 128), bf16)
    slots = list_ref.shape[1]
    left = iota((nrhs, 128), 1) < 64
    kids = transfer_ref.shape[2] // 128

    def node(p, _):
        ids = []
        for j in range(slots):
            e = list_ref[p, j]
            ids.append(jnp.where(e < 0, 2 * pairs, e))
        acc = dot(far_left(ids, all_ref), gn_ref[p])
        x = acc[:nrhs] + pltpu.roll(acc[nrhs:], 64, 1)
        down = dot(x[:, :64].astype(bf16), transfer_ref[p])
        for c in range(kids):
            q = p * kids + c
            local = (far_ref[q] + down[:, c * 128 : (c + 1) * 128]).astype(bf16).astype(f32)
            both = jnp.concatenate(
                [jnp.where(left, local, 0.0), jnp.where(left, 0.0, local)], axis=0
            ).astype(bf16)
            y = dot(both, basis_ref[q])
            out_ref[2 * q] = (near_ref[2 * q] + y[:nrhs]).astype(bf16)
            out_ref[2 * q + 1] = (near_ref[2 * q + 1] + y[nrhs:]).astype(bf16)
        return 0

    lax.fori_loop(0, nodes_here, node, 0)


def vmem():
    return pl.BlockSpec(memory_space=pltpu.VMEM)


def smem():
    return pl.BlockSpec(memory_space=pltpu.SMEM)


def call(kernel, out, in_specs, scratch, name, flops, vmem_mib):
    many = isinstance(out, tuple)
    return pl.pallas_call(
        kernel,
        out_shape=out,
        in_specs=in_specs,
        out_specs=tuple(vmem() for _ in out) if many else vmem(),
        scratch_shapes=scratch,
        name=name,
        cost_estimate=pl.CostEstimate(flops=flops, bytes_accessed=1 << 20, transcendentals=0),
        compiler_params=pltpu.CompilerParams(vmem_limit_bytes=vmem_mib << 20),
    )


def pack(peers, per, density, leaf_target):
    leaves, nrhs, leaf = density.shape
    return call(
        lambda *r: pack_kernel(*r, peers=peers, per=per),
        jax.ShapeDtypeStruct((peers, per * nrhs + 16, leaf), bf16),
        [smem(), vmem()],
        [pltpu.SMEM((peers,), jnp.int32), pltpu.SMEM((leaves,), jnp.int32)],
        "pack",
        1 << 20,
        2,
    )(leaf_target, density)


def features(node_list, geometry, node_points, near_list, far_list):
    leaves, slots = near_list.shape
    nodes = node_points.shape[1] // 64
    nodes_here, node_slots = node_list.shape
    shape = jax.ShapeDtypeStruct
    return call(
        feature_kernel,
        (
            shape((leaves, 128, 128), bf16),
            shape((leaves, 128, 256), bf16),
            shape((leaves, 256, 128), bf16),
            shape((leaves * 24, 128), bf16),
            shape((nodes_here, node_slots * 32, 128), bf16),
            shape((2 * slots + 2, leaves), jnp.int32),
        ),
        [smem()] + [vmem()] * 4,
        [
            pltpu.VMEM((8, leaves * 128), f32),
            pltpu.VMEM((8, nodes * 64), f32),
            pltpu.VMEM((nodes // 2, 128, 128), bf16),
            pltpu.VMEM((nodes_here, 256, 128), bf16),
        ],
        "features",
        1 << 30,
        14,
    )(node_list, geometry, node_points, near_list.T, far_list.T)


def skeletons(arrived, basis_in, transfer, split, per):
    peers = arrived.shape[0]
    leaves = peers * per
    nodes_here = transfer.shape[0]
    rows = leaves // 2 * 32 + leaves // 4 * 32 + leaves // 2 * 24
    shape = jax.ShapeDtypeStruct
    return call(
        lambda *r: skeleton_kernel(*r, per=per),
        (
            shape((2, rows, 128), bf16),
            shape((rows, 128), bf16),
            shape((rows, 128), bf16),
            shape((peers, nodes_here // 2 * 32, 128), bf16),
        ),
        [vmem()] * 4,
        [],
        "skeleton",
        1 << 26,
        6,
    )(
        arrived,
        basis_in.reshape(leaves // 2, 128, -1),
        transfer.reshape(nodes_here // 2, 128, -1),
        split,
    )


def leaf_fields(lists, fs, ft, wf, own, got_a, got_b):
    leaves = ft.shape[0]
    rows = got_a.shape[0]
    wide = leaves + 2 * REACH
    slots = (lists.shape[0] - 2) // 2
    shape = jax.ShapeDtypeStruct
    return call(
        leaf_kernel,
        (shape((leaves, 32, 128), f32), shape((leaves // 2, 32, 128), f32)),
        [smem()] + [vmem()] * 6,
        [
            pltpu.VMEM((wide, 128, 128), bf16),
            pltpu.VMEM((wide + 1, 32, 128), bf16),
            pltpu.VMEM((wide + 1, 32, 128), bf16),
            pltpu.VMEM((2, rows, 128), bf16),
            pltpu.VMEM((4 * 128, 128), bf16),
            pltpu.VMEM((2, slots * 32, 128), bf16),
            pltpu.SMEM((leaves * (slots // 4) + 8,), jnp.int32),
        ],
        "leaves",
        1 << 31,
        16,
    )(lists, fs, ft, wf, own, got_a, got_b)


def finish(node_list, near, far, all_skel, gn, transfer, basis_out):
    leaves, nrhs, leaf = near.shape
    nodes = all_skel.shape[0] // 16
    return call(
        node_kernel,
        jax.ShapeDtypeStruct((leaves, nrhs, leaf), bf16),
        [smem()] + [vmem()] * 6,
        [pltpu.VMEM((nodes + 1, nrhs, 128), bf16)],
        "nodes",
        1 << 28,
        8,
    )(node_list, near, far, all_skel, gn, transfer, basis_out.reshape(leaves // 2, 128, leaf))


def on_device(
    density, leaf_target, geometry, near_list, far_list, node_list, basis_in, basis_out, transfer, node_points
):
    peers = lax.axis_size(AXES)
    per = density.shape[0] // peers
    outgoing = pack(peers, per, density, leaf_target)
    arrived = lax.all_to_all(outgoing, AXES, split_axis=0, concat_axis=0, tiled=True)
    fs, ft, wf, split, gn, lists = features(node_list, geometry, node_points, near_list, far_list)
    own, to_a, to_b, node_out = skeletons(arrived, basis_in, transfer, split, per)
    all_skel = lax.all_to_all(node_out, AXES, split_axis=0, concat_axis=0, tiled=True)
    swap_a = [(i, i ^ 1) for i in range(peers)]
    swap_b = [(i, i + 1) for i in range(1, peers - 1, 2)] + [(i + 1, i) for i in range(1, peers - 1, 2)]
    got_a = lax.ppermute(to_a, AXES, swap_a)
    got_b = lax.ppermute(to_b, AXES, swap_b)
    near, far = leaf_fields(lists, fs, ft, wf, own, got_a, got_b)
    return finish(node_list, near, far, all_skel.reshape(-1, 128), gn, transfer, basis_out)


def solution(mesh):
    split = ("grp", "row", "col")
    return jax.shard_map(
        on_device,
        mesh=mesh,
        in_specs=(
            P(split, None, None),
            P(split),
            P(None, split),
            P(split, None),
            P(split, None),
            P(split, None),
            P(split, None, None),
            P(split, None, None),
            P(split, None, None),
            P(None, "grp"),
        ),
        out_specs=P(split, None, None),
        check_vma=False,
    )
```

```python
import math

import jax
import jax.numpy as jnp
from jax import lax
from jax.experimental import pallas as pl
from jax.experimental.pallas import tpu as pltpu
from jax.sharding import PartitionSpec as P

REACH = 16
AXES = ("row", "col")

smoothing = 0.1
inv_four_pi = 0.25 / math.pi
grid_step = 16.0
UNROLL = 8
LEAD = UNROLL
bf16 = jnp.bfloat16
f32 = jnp.float32


def split3(x):
    first = x.astype(bf16).astype(f32)
    rest = x - first
    second = rest.astype(bf16).astype(f32)
    third = (rest - second).astype(bf16).astype(f32)
    return first, second, third


def iota(shape, axis):
    return lax.broadcasted_iota(jnp.int32, shape, axis)


def dot(a, b):
    return lax.dot_general(a, b, (((1,), (0,)), ((), ())), preferred_element_type=f32)


def dot_t(a, b):
    return lax.dot_general(a, b, (((1,), (1,)), ((), ())), preferred_element_type=f32)


class Features:
    def __init__(self, g):
        self.shape = g.shape
        self.row = row = iota(g.shape, 0)
        point = row < 3
        c = jnp.where(point, g, 0.0)
        self.whole = whole = jnp.floor(c * grid_step + 0.5) * (1.0 / grid_step)
        part = c - whole
        self.part = split3(part)
        m = jnp.where(point, 0.0, g) * inv_four_pi
        self.m = split3(m)
        norm = jnp.sum(whole * whole, axis=0, keepdims=True)
        self.norm_hi = jnp.floor(norm)
        self.norm_lo = norm - self.norm_hi
        self.cross = jnp.sum(part * (2.0 * whole + part), axis=0, keepdims=True)
        self.q = split3(jnp.sum(m * pltpu.roll(c, 3, 0), axis=0, keepdims=True))
        self.low = {}

    def moved(self, x):
        if id(x) not in self.low:
            self.low[id(x)] = pltpu.roll(x, 3, 0)
        return self.low[id(x)]

    def tile(self, upper, lower, six, seven):
        row = self.row
        x = jnp.where(row < 3, upper, 0.0)
        if lower is not None:
            x = jnp.where(row < 3, upper, jnp.where(row < 6, lower, 0.0))
        if six is not None:
            x = jnp.where(row == 6, six, x)
        if seven is not None:
            x = jnp.where(row == 7, seven, x)
        return x

    def first(self, points, three, four, five, six):
        row = self.row
        x = jnp.where(row == 3, three, jnp.where(row == 4, four, 0.0))
        x = jnp.where(row == 5, five, jnp.where(row == 6, six, x))
        return jnp.where(row < 3, points, x)

    def zeros(self, rows):
        return jnp.zeros((rows, self.shape[1]), f32)

    def source_square(self):
        w, (p0, p1, p2) = self.whole, self.part
        c0, c1, c2 = split3(self.cross)
        move = self.moved
        return [
            self.first(w, self.norm_hi, self.norm_lo, 1.0, 1.0),
            self.tile(w, move(w), 1.0, 1.0),
            self.tile(w, move(p0), 1.0, c0),
            self.tile(p1, move(p2), c1, c2),
            self.tile(p0, move(p1), None, None),
            self.tile(p0, None, None, None),
            self.zeros(16),
        ]

    def source_normal(self):
        m0, m1, m2 = self.m
        u0, u1, u2 = (pltpu.roll(x, 5, 0) for x in self.m)
        q0, q1, q2 = self.q
        return [
            self.tile(u0, m1, q0, q1),
            self.tile(u2, m0, q2, None),
            self.tile(u0, m0, None, None),
            self.tile(u1, m1, None, None),
            self.tile(u2, None, None, None),
            self.zeros(24),
        ]

    def target_square(self):
        w, part = -2.0 * self.whole, [-2.0 * p for p in self.part]
        p0, p1, p2 = part
        c0, c1, c2 = split3(self.cross + smoothing * smoothing)
        w3, p03, p13 = (pltpu.roll(x, 3, 0) for x in (w, p0, p1))
        return [
            self.first(w, 1.0, 1.0, self.norm_hi, self.norm_lo),
            self.tile(p0, p13, c0, c1),
            self.tile(p2, w3, c2, 1.0),
            self.tile(w, w3, 1.0, 1.0),
            self.tile(p0, p03, None, None),
            self.tile(p1, None, None, None),
            self.zeros(16),
        ]

    def target_normal(self):
        w, (p0, p1, p2) = self.whole, self.part
        move = self.moved
        return [
            self.tile(w, move(w), -1.0, -1.0),
            self.tile(w, move(p0), -1.0, None),
            self.tile(p1, move(p2), None, None),
            self.tile(p0, move(p1), None, None),
            self.tile(p0, None, None, None),
            self.zeros(24),
        ]


def sources(f):
    x = jnp.concatenate(f.source_square() + f.source_normal(), axis=0).T
    top = x[:64]
    left = iota(top.shape, 1) < 64
    return x.astype(bf16), jnp.where(left, top, pltpu.roll(top, 64, 1)).astype(bf16)


def point_sources(f):
    x = f.source_square()
    return jnp.concatenate(x + x, axis=0).T.astype(bf16)


def halves(x):
    left = iota(x.shape, 1) < 64
    a = jnp.where(left, x, 0.0)
    b = jnp.where(left, 0.0, x)
    return (a, pltpu.roll(a, 64, 1)), (pltpu.roll(b, 64, 1), b)


def pair_weights(square):
    return [jnp.concatenate(x, axis=0).astype(bf16) for x in halves(jnp.concatenate(square, axis=0))]


def compact(entries, first, dead):
    slots, targets = entries.shape
    place = iota(entries.shape, 0)
    out = jnp.full(entries.shape, dead, jnp.int32)
    count = jnp.zeros((1, targets), jnp.int32)
    for k in range(slots):
        e = entries[k : k + 1]
        live = e >= 0
        at = jnp.where(live, count, -1)
        out = jnp.where(place == at, e - first, out)
        count = count + jnp.where(live, 1, 0)
    return out, count


def items(near, count, dead, out_ref, at):
    slots, targets = near.shape
    mine = (count + 1) // 2
    before = jnp.where(iota((targets, targets), 0) < iota((targets, targets), 1), 1.0, 0.0).astype(bf16)
    start = dot(jnp.broadcast_to(mine.astype(f32), (8, targets)).astype(bf16), before)[0:1]
    total = jnp.sum(mine, axis=1, keepdims=True).astype(f32)
    table = near.astype(f32).astype(bf16)
    rows = out_ref.shape[0] - at - 1
    wide = iota((rows, targets), 1)
    slot = iota((rows, slots), 1)
    lane = iota((rows, 128), 1)
    out = jnp.zeros((rows, 128), f32)
    for u in range(UNROLL):
        place = (iota((rows, 1), 0) * UNROLL + (u - LEAD)).astype(f32)
        begun = start <= place
        target = jnp.sum(jnp.where(begun, 1.0, 0.0), axis=1, keepdims=True) - 1.0
        base = jnp.max(jnp.where(begun, start, 0.0), axis=1, keepdims=True)
        pick = jnp.where(wide.astype(f32) == target, 1.0, 0.0).astype(bf16)
        lists = dot_t(pick, table)
        used = (place >= 0.0) & (place < total)
        first = 2.0 * (place - base)
        out = jnp.where(lane == u, jnp.where(used, target, float(targets)), out)
        for h in range(2):
            chosen = jnp.where(slot.astype(f32) == first + float(h), lists, 0.0)
            ids = jnp.where(used, jnp.sum(chosen, axis=1, keepdims=True), float(dead))
            out = jnp.where(lane == (h + 1) * UNROLL + u, ids, out)
    out_ref[at : at + rows] = out.astype(jnp.int32)
    out_ref[at + rows :] = jnp.broadcast_to(total, (1, 128)).astype(jnp.int32)


def list_rows(slots, leaves):
    return leaves + -(-(leaves * (slots // 2) // UNROLL + 3) // 8) * 8 + 1


def pack_kernel(target_ref, density_ref, out_ref, count_ref, slot_ref, *, peers, per):
    leaves, nrhs, leaf = density_ref.shape
    for d in range(peers):
        count_ref[d] = 0
    for k in range(leaves):
        t = target_ref[k]
        d = t // leaves
        c = count_ref[d]
        count_ref[d] = c + 1
        slot_ref[d * per + c] = t - d * leaves
        out_ref[d, pl.ds(pl.multiple_of(c * nrhs, nrhs), nrhs), :] = density_ref[k]
    row = iota((16, leaf), 0)
    for d in range(peers):
        x = jnp.zeros((16, leaf), f32)
        for c in range(per):
            x = jnp.where(row == c, slot_ref[d * per + c].astype(f32), x)
        out_ref[d, per * nrhs :, :] = x.astype(bf16)


def feature_kernel(
    node_list_ref, geo_ref, node_ref, near_ref, far_ref,
    fs_ref, fd_ref, ft_ref, wf_ref, split_ref, gn_ref, list_ref,
    pad_ref, npad_ref, fsn_ref, wfn_ref,
):
    leaves = fs_ref.shape[0]
    nodes_here = wfn_ref.shape[0]
    slots = near_ref.shape[0]
    index = lax.axis_index(AXES)
    first = index * leaves - REACH
    wide = leaves + 2 * REACH
    pad_ref[...] = jnp.zeros(pad_ref.shape, f32)
    pad_ref[0:6, :] = geo_ref[...]
    npad_ref[...] = jnp.zeros(npad_ref.shape, f32)
    npad_ref[0:3, :] = node_ref[...]
    near, near_count = compact(near_ref[...], first, wide)
    far, _ = compact(far_ref[...], first, wide)
    same = jnp.where(iota((leaves, leaves), 0) == iota((leaves, leaves), 1), 1.0, 0.0).astype(bf16)
    list_ref[0:leaves, 0:slots] = dot_t(same, far.astype(f32).astype(bf16)).astype(jnp.int32)
    items(near, near_count, wide, list_ref, leaves)

    def leaf_step(l, _):
        g = pad_ref[:, pl.ds(pl.multiple_of(l * 128, 128), 128)]
        f = Features(g)
        fs_ref[l], fd_ref[l] = sources(f)
        square = f.target_square()
        normal = f.target_normal()
        ft_ref[l] = jnp.concatenate(
            [
                jnp.concatenate(square + [f.zeros(64)], axis=0),
                jnp.concatenate([f.zeros(64)] + normal, axis=0),
            ],
            axis=1,
        ).astype(bf16)
        wf_ref[l] = pair_weights(square)[0]
        return 0

    lax.fori_loop(0, leaves, leaf_step, 0, unroll=4)

    def split_step(l, _):
        parts = []
        for k in range(2):
            parts += split3(pad_ref[:, pl.ds(pl.multiple_of((l * 2 + k) * 128, 128), 128)])
        split_ref[pl.ds(pl.multiple_of(l * 48, 48), 48), :] = jnp.concatenate(parts, axis=0).astype(bf16)
        return 0

    lax.fori_loop(0, leaves // 2, split_step, 0, unroll=4)

    def node_step(l, _):
        fsn_ref[l] = point_sources(Features(npad_ref[:, pl.ds(pl.multiple_of(l * 128, 128), 128)]))
        return 0

    n_nodes = 2 * fsn_ref.shape[0]
    lax.fori_loop(0, n_nodes // 2, node_step, 0, unroll=4)
    chunk = index * (nodes_here // 2)
    for l in range(nodes_here // 2):
        f = Features(npad_ref[:, pl.ds(pl.multiple_of((chunk + l) * 128, 128), 128)])
        wfn_ref[2 * l], wfn_ref[2 * l + 1] = pair_weights(f.target_square())

    node_slots = node_list_ref.shape[1]
    left = iota((64, 128), 1) < 64

    def node_field(p, _):
        x = []
        for j in range(0, node_slots, 2):
            pair = []
            for u in range(2):
                s = jnp.maximum(node_list_ref[p, j + u], 0)
                pair.append(fsn_ref[s // 2, pl.ds(pl.multiple_of((s % 2) * 64, 64), 64), :])
            x.append(jnp.where(left, pair[0], pair[1]))
        out = dot(jnp.concatenate(x, axis=0), wfn_ref[p])
        gn_ref[p] = (lax.rsqrt(out) * inv_four_pi).astype(bf16)
        return 0

    lax.fori_loop(0, nodes_here, node_field, 0)


def skeleton_kernel(
    arrived_ref, basis_ref, transfer_ref, split_ref, own_ref, a_ref, b_ref, node_ref, *, per
):
    peers = arrived_ref.shape[0]
    leaves = peers * per
    nrhs = 32
    half = leaves // 2
    for d in range(peers):
        slots = arrived_ref[d, per * nrhs :, :].astype(f32).astype(jnp.int32)
        for c in range(per):
            s = slots[c, 0]
            h = s // half
            own_ref[h, pl.ds(pl.multiple_of((s - h * half) * nrhs, nrhs), nrhs), :] = arrived_ref[
                d, c * nrhs : (c + 1) * nrhs, :
            ]
    left = iota((nrhs, 128), 1) < 64
    skels = []
    for p in range(leaves // 2):
        h, q = divmod(p, half // 2)
        out = dot_t(own_ref[h, q * 64 : (q + 1) * 64, :], basis_ref[p])
        pair = jnp.where(left, out[:nrhs], out[nrhs:]).astype(bf16)
        own_ref[h, half * nrhs + q * nrhs : half * nrhs + (q + 1) * nrhs, :] = pair
        skels.append(pair)
    base = half * nrhs + (half // 2) * nrhs
    n_split = half * 24
    for h in range(2):
        own_ref[h, base : base + n_split, :] = split_ref[h * n_split : (h + 1) * n_split, :]
    kids = transfer_ref.shape[2] // 128
    n_pairs = len(skels) // (2 * kids)
    for p in range(n_pairs):
        stack = jnp.concatenate(
            [jnp.concatenate(skels[(2 * p + h) * kids : (2 * p + h + 1) * kids], axis=1) for h in range(2)], axis=0
        )
        out = dot_t(stack, transfer_ref[p])
        pair = jnp.where(left, out[:nrhs], out[nrhs:]).astype(bf16)
        for d in range(peers):
            node_ref[d, p * nrhs : (p + 1) * nrhs, :] = pair
    odd = lax.axis_index(AXES) % 2
    a_ref[...] = own_ref[1 - odd]
    b_ref[...] = own_ref[odd]


def doubled(pairs, out_ref, k):
    rows = pairs.shape[0]
    i, j = iota((128, 256), 0), iota((128, 256), 1)
    pick = jnp.where(i == (j % 64) + 64 * (j // 128), 1.0, 0.0).astype(bf16)
    both = dot(pairs, pick).astype(bf16)
    for p in range(rows // 32):
        for h in range(2):
            out_ref[k + 2 * p + h] = both[32 * p : 32 * p + 32, 128 * h : 128 * h + 128]


def far_left(ids, skel_ref):
    left = iota((32, 128), 1) < 64
    cols = []
    for j in range(0, len(ids), 4):
        a, b, c, d = (skel_ref[s] for s in ids[j : j + 4])
        cols.append(jnp.concatenate([jnp.where(left, a, c), jnp.where(left, b, d)], axis=0))
    return jnp.concatenate(cols, axis=1)


def leaf_kernel(
    list_ref, fs_own_ref, fd_own_ref, ft_hbm, wf_hbm, own_ref, a_ref, b_ref,
    near_out, far_out,
    fs_ref, fd_ref, ft_ref, wf_ref, dens_ref, skel_ref, k_ref, g_ref, sem,
):
    leaves = wf_ref.shape[0]
    nrhs = 32
    half = leaves // 2
    wide = leaves + 2 * REACH
    odd = lax.axis_index(AXES) % 2 == 1
    slots = g_ref.shape[1] // 32
    mine = pl.ds(REACH, leaves)
    copies = [
        pltpu.make_async_copy(fs_own_ref, fs_ref.at[mine], sem.at[0]),
        pltpu.make_async_copy(ft_hbm, ft_ref.at[pl.ds(0, leaves)], sem.at[1]),
        pltpu.make_async_copy(fd_own_ref, fd_ref.at[mine], sem.at[2]),
        pltpu.make_async_copy(wf_hbm, wf_ref, sem.at[3]),
        pltpu.make_async_copy(fs_own_ref.at[0], fs_ref.at[wide], sem.at[4]),
        pltpu.make_async_copy(fd_own_ref.at[0], fd_ref.at[wide], sem.at[5]),
    ]
    for c in copies:
        c.start()

    base = half * nrhs + (half // 2) * nrhs
    for right, k in ((False, 0), (True, REACH + leaves)):

        def halo(l, _, right=right, k=k):
            at = pl.ds(pl.multiple_of(base + l * 48, 16), 48)
            x, y = a_ref[at, :].astype(f32), b_ref[at, :].astype(f32)
            x = jnp.where(odd, y, x) if right else jnp.where(odd, x, y)
            for j in range(2):
                g = x[24 * j : 24 * j + 8] + x[24 * j + 8 : 24 * j + 16] + x[24 * j + 16 : 24 * j + 24]
                fs_ref[k + 2 * l + j], fd_ref[k + 2 * l + j] = sources(Features(g))
            return 0

        lax.fori_loop(0, half // 2, halo, 0, unroll=2)

    def fill(view, k):
        for l in range(half):
            dens_ref[k + l] = view(l * nrhs, nrhs)
        doubled(view(half * nrhs, half // 2 * nrhs), skel_ref, k)

    fill(lambda at, n: jnp.where(odd, a_ref[at : at + n, :], b_ref[at : at + n, :]), 0)
    fill(lambda at, n: own_ref[0, at : at + n, :], REACH)
    fill(lambda at, n: own_ref[1, at : at + n, :], REACH + half)
    fill(lambda at, n: jnp.where(odd, b_ref[at : at + n, :], a_ref[at : at + n, :]), REACH + leaves)
    dens_ref[wide] = jnp.zeros((nrhs, 128), bf16)
    skel_ref[wide] = jnp.zeros((nrhs, 128), bf16)
    near_out[...] = jnp.zeros(near_out.shape, f32)
    for c in copies:
        c.wait()

    def item(i, u, part):
        return list_ref[leaves + i, part * UNROLL + u]

    def near_step(i, _):
        for u in range(UNROLL):
            lhs = jnp.concatenate([dens_ref[item(i, u, 1)], dens_ref[item(i, u, 2)]], axis=1)
            near_out[item(i, u, 0)] += dot(lhs, k_ref[u])
        for u in range(UNROLL):
            x = jnp.concatenate([fs_ref[item(i + 1, u, 1)], fs_ref[item(i + 1, u, 2)]], axis=0)
            out = dot(x, ft_ref[item(i + 1, u, 0)])
            r = lax.rsqrt(out[:, :128])
            k_ref[u] = ((out[:, 128:] * r) * (r * r)).astype(bf16)
        return 0

    n = list_ref[list_ref.shape[0] - 1, 0]
    lax.fori_loop(0, (n + UNROLL - 1) // UNROLL + 1, near_step, 0)

    left = iota((nrhs, 128), 1) < 64
    left64 = iota((64, 128), 1) < 64

    def far_ids(t):
        return [list_ref[t, u] for u in range(slots)]

    def far_step(p, _):
        done = jnp.maximum(p - 1, 0)
        e, o = (dot(far_left(far_ids(2 * done + h), skel_ref), g_ref[h]) for h in range(2))
        even = e[:nrhs] + pltpu.roll(e[nrhs:], 64, 1)
        odd_ = pltpu.roll(o[:nrhs], 64, 1) + o[nrhs:]
        far_out[done] = jnp.where(left, even, odd_)
        for h in range(2):
            t = 2 * jnp.minimum(p, half - 1) + h
            ids = far_ids(t)
            x = [
                jnp.where(left64, fd_ref[ids[j]], fd_ref[ids[j + 1]]) for j in range(0, slots, 2)
            ]
            out = dot(jnp.concatenate(x, axis=0), wf_ref[t])
            g_ref[h] = (lax.rsqrt(out) * inv_four_pi).astype(bf16)
        return 0

    lax.fori_loop(0, half + 1, far_step, 0)


def node_kernel(
    list_ref, near_ref, far_ref, skel_ref, gn_ref, transfer_ref, basis_ref,
    out_ref,
    all_ref,
):
    nrhs = 32
    nodes_here = gn_ref.shape[0]
    pairs = skel_ref.shape[0] // nrhs
    doubled(skel_ref[...], all_ref, 0)
    all_ref[2 * pairs] = jnp.zeros((nrhs, 128), bf16)
    slots = list_ref.shape[1]
    left = iota((nrhs, 128), 1) < 64
    kids = transfer_ref.shape[2] // 128

    def node(p, _):
        ids = []
        for j in range(slots):
            e = list_ref[p, j]
            ids.append(jnp.where(e < 0, 2 * pairs, e))
        acc = dot(far_left(ids, all_ref), gn_ref[p])
        x = acc[:nrhs] + pltpu.roll(acc[nrhs:], 64, 1)
        down = dot(x[:, :64].astype(bf16), transfer_ref[p])
        for c in range(kids):
            q = p * kids + c
            local = (far_ref[q] + down[:, c * 128 : (c + 1) * 128]).astype(bf16).astype(f32)
            both = jnp.concatenate(
                [jnp.where(left, local, 0.0), jnp.where(left, 0.0, local)], axis=0
            ).astype(bf16)
            y = dot(both, basis_ref[q])
            out_ref[2 * q] = (near_ref[2 * q] + y[:nrhs]).astype(bf16)
            out_ref[2 * q + 1] = (near_ref[2 * q + 1] + y[nrhs:]).astype(bf16)
        return 0

    lax.fori_loop(0, nodes_here, node, 0)


def vmem():
    return pl.BlockSpec(memory_space=pltpu.VMEM)


def smem():
    return pl.BlockSpec(memory_space=pltpu.SMEM)


def call(kernel, out, in_specs, scratch, name, flops, vmem_mib):
    many = isinstance(out, tuple)
    return pl.pallas_call(
        kernel,
        out_shape=out,
        in_specs=in_specs,
        out_specs=tuple(vmem() for _ in out) if many else vmem(),
        scratch_shapes=scratch,
        name=name,
        cost_estimate=pl.CostEstimate(flops=flops, bytes_accessed=1 << 20, transcendentals=0),
        compiler_params=pltpu.CompilerParams(vmem_limit_bytes=vmem_mib << 20),
    )


def pack(peers, per, density, leaf_target):
    leaves, nrhs, leaf = density.shape
    return call(
        lambda *r: pack_kernel(*r, peers=peers, per=per),
        jax.ShapeDtypeStruct((peers, per * nrhs + 16, leaf), bf16),
        [smem(), vmem()],
        [pltpu.SMEM((peers,), jnp.int32), pltpu.SMEM((leaves,), jnp.int32)],
        "pack",
        1 << 20,
        2,
    )(hbm(leaf_target), hbm(density))


def features(node_list, geometry, node_points, near_list, far_list):
    leaves, slots = near_list.shape
    nodes = node_points.shape[1] // 64
    nodes_here, node_slots = node_list.shape
    shape = jax.ShapeDtypeStruct
    return call(
        feature_kernel,
        (
            pltpu.HBM((leaves, 128, 128), bf16),
            pltpu.HBM((leaves, 64, 128), bf16),
            pltpu.HBM((leaves, 128, 256), bf16),
            pltpu.HBM((leaves, 128, 128), bf16),
            pltpu.VMEM((leaves * 24, 128), bf16),
            pltpu.VMEM((nodes_here, node_slots * 32, 128), bf16),
            pltpu.HBM((list_rows(slots, leaves), 128), jnp.int32),
        ),
        [smem()] + [vmem()] * 4,
        [
            pltpu.VMEM((8, leaves * 128), f32),
            pltpu.VMEM((8, nodes * 64), f32),
            pltpu.VMEM((nodes // 2, 128, 128), bf16),
            pltpu.VMEM((nodes_here, 128, 128), bf16),
        ],
        "features",
        1 << 30,
        14,
    )(hbm(node_list), hbm(geometry), hbm(node_points), hbm(near_list.T), hbm(far_list.T))


def skeletons(arrived, basis_in, transfer, split, per):
    peers = arrived.shape[0]
    leaves = peers * per
    nodes_here = transfer.shape[0]
    rows = leaves // 2 * 32 + leaves // 4 * 32 + leaves // 2 * 24
    shape = jax.ShapeDtypeStruct
    return call(
        lambda *r: skeleton_kernel(*r, per=per),
        (
            pltpu.VMEM((2, rows, 128), bf16),
            shape((rows, 128), bf16),
            shape((rows, 128), bf16),
            shape((peers, nodes_here // 2 * 32, 128), bf16),
        ),
        [vmem()] * 4,
        [],
        "skeleton",
        1 << 26,
        6,
    )(
        arrived,
        hbm(basis_in.reshape(leaves // 2, 128, -1)),
        hbm(transfer.reshape(nodes_here // 2, 128, -1)),
        split,
    )


def leaf_fields(slots, lists, fs, fd, ft, wf, own, got_a, got_b):
    leaves = ft.shape[0]
    wide = leaves + 2 * REACH
    anywhere = pl.BlockSpec(memory_space=pl.ANY)
    return call(
        leaf_kernel,
        (pltpu.VMEM((leaves + 1, 32, 128), f32), pltpu.VMEM((leaves // 2, 32, 128), f32)),
        [smem()] + [anywhere] * 4 + [vmem()] * 3,
        [
            pltpu.VMEM((wide + 1, 128, 128), bf16),
            pltpu.VMEM((wide + 1, 64, 128), bf16),
            pltpu.VMEM((leaves + 1, 128, 256), bf16),
            pltpu.VMEM((leaves, 128, 128), bf16),
            pltpu.VMEM((wide + 1, 32, 128), bf16),
            pltpu.VMEM((wide + 1, 32, 128), bf16),
            pltpu.VMEM((UNROLL, 256, 128), bf16),
            pltpu.VMEM((2, slots * 32, 128), bf16),
            pltpu.SemaphoreType.DMA((6,)),
        ],
        "leaves",
        1 << 31,
        20,
    )(hbm(lists), hbm(fs), hbm(fd), hbm(ft), hbm(wf), own, got_a, got_b)


def finish(node_list, near, far, all_skel, gn, transfer, basis_out):
    leaves, _, leaf = basis_out.shape
    nrhs = near.shape[1]
    nodes = all_skel.shape[0] // 16
    return call(
        node_kernel,
        jax.ShapeDtypeStruct((leaves, nrhs, leaf), bf16),
        [smem()] + [vmem()] * 6,
        [pltpu.VMEM((nodes + 1, nrhs, 128), bf16)],
        "nodes",
        1 << 28,
        8,
    )(hbm(node_list), near, far, all_skel, gn, hbm(transfer), hbm(basis_out.reshape(leaves // 2, 128, leaf)))


def hbm(x):
    return pltpu.with_memory_space_constraint(x, pltpu.HBM)


def on_device(
    density, leaf_target, geometry, near_list, far_list, node_list, basis_in, basis_out, transfer, node_points
):
    peers = lax.axis_size(AXES)
    per = density.shape[0] // peers
    outgoing = pack(peers, per, density, leaf_target)
    arrived = lax.all_to_all(outgoing, AXES, split_axis=0, concat_axis=0, tiled=True)
    fs, fd, ft, wf, split, gn, lists = features(node_list, geometry, node_points, near_list, far_list)
    own, to_a, to_b, node_out = skeletons(arrived, basis_in, transfer, split, per)
    all_skel = lax.all_to_all(node_out, AXES, split_axis=0, concat_axis=0, tiled=True)
    swap_a = [(i, i ^ 1) for i in range(peers)]
    swap_b = [(i, i + 1) for i in range(1, peers - 1, 2)] + [(i + 1, i) for i in range(1, peers - 1, 2)]
    got_a = lax.ppermute(to_a, AXES, swap_a)
    got_b = lax.ppermute(to_b, AXES, swap_b)
    near, far = leaf_fields(near_list.shape[1], lists, fs, fd, ft, wf, own, got_a, got_b)
    return finish(node_list, near, far, all_skel.reshape(-1, 128), gn, transfer, basis_out)


def solution(mesh):
    split = ("grp", "row", "col")
    return jax.shard_map(
        on_device,
        mesh=mesh,
        in_specs=(
            P(split, None, None),
            P(split),
            P(None, split),
            P(split, None),
            P(split, None),
            P(split, None),
            P(split, None, None),
            P(split, None, None),
            P(split, None, None),
            P(None, "grp"),
        ),
        out_specs=P(split, None, None),
        check_vma=False,
    )
```

```python
import math

import jax
import jax.numpy as jnp
from jax import lax
from jax.experimental import pallas as pl
from jax.experimental.pallas import tpu as pltpu
from jax.sharding import PartitionSpec as P

REACH = 16
AXES = ("row", "col")

smoothing = 0.1
inv_four_pi = 0.25 / math.pi
grid_step = 16.0
UNROLL = 8
LEAD = UNROLL
bf16 = jnp.bfloat16
f32 = jnp.float32


def split3(x):
    first = x.astype(bf16).astype(f32)
    rest = x - first
    second = rest.astype(bf16).astype(f32)
    third = (rest - second).astype(bf16).astype(f32)
    return first, second, third


def iota(shape, axis):
    return lax.broadcasted_iota(jnp.int32, shape, axis)


def dot(a, b):
    return lax.dot_general(a, b, (((1,), (0,)), ((), ())), preferred_element_type=f32)


def dot_t(a, b):
    return lax.dot_general(a, b, (((1,), (1,)), ((), ())), preferred_element_type=f32)


class Features:
    def __init__(self, g):
        self.shape = g.shape
        self.row = row = iota(g.shape, 0)
        point = row < 3
        c = jnp.where(point, g, 0.0)
        self.whole = whole = jnp.floor(c * grid_step + 0.5) * (1.0 / grid_step)
        part = c - whole
        self.part = split3(part)
        m = jnp.where(point, 0.0, g) * inv_four_pi
        self.m = split3(m)
        norm = jnp.sum(whole * whole, axis=0, keepdims=True)
        self.norm_hi = jnp.floor(norm)
        self.norm_lo = norm - self.norm_hi
        self.cross = jnp.sum(part * (2.0 * whole + part), axis=0, keepdims=True)
        self.q = split3(jnp.sum(m * pltpu.roll(c, 3, 0), axis=0, keepdims=True))
        self.low = {}

    def moved(self, x):
        if id(x) not in self.low:
            self.low[id(x)] = pltpu.roll(x, 3, 0)
        return self.low[id(x)]

    def tile(self, upper, lower, six, seven):
        row = self.row
        x = jnp.where(row < 3, upper, 0.0)
        if lower is not None:
            x = jnp.where(row < 3, upper, jnp.where(row < 6, lower, 0.0))
        if six is not None:
            x = jnp.where(row == 6, six, x)
        if seven is not None:
            x = jnp.where(row == 7, seven, x)
        return x

    def first(self, points, three, four, five, six):
        row = self.row
        x = jnp.where(row == 3, three, jnp.where(row == 4, four, 0.0))
        x = jnp.where(row == 5, five, jnp.where(row == 6, six, x))
        return jnp.where(row < 3, points, x)

    def zeros(self, rows):
        return jnp.zeros((rows, self.shape[1]), f32)

    def source_square(self):
        w, (p0, p1, p2) = self.whole, self.part
        c0, c1, c2 = split3(self.cross)
        move = self.moved
        return [
            self.first(w, self.norm_hi, self.norm_lo, 1.0, 1.0),
            self.tile(w, move(w), 1.0, 1.0),
            self.tile(w, move(p0), 1.0, c0),
            self.tile(p1, move(p2), c1, c2),
            self.tile(p0, move(p1), None, None),
            self.tile(p0, None, None, None),
            self.zeros(16),
        ]

    def source_normal(self):
        m0, m1, m2 = self.m
        u0, u1, u2 = (pltpu.roll(x, 5, 0) for x in self.m)
        q0, q1, q2 = self.q
        return [
            self.tile(u0, m1, q0, q1),
            self.tile(u2, m0, q2, None),
            self.tile(u0, m0, None, None),
            self.tile(u1, m1, None, None),
            self.tile(u2, None, None, None),
            self.zeros(24),
        ]

    def target_square(self):
        w, part = -2.0 * self.whole, [-2.0 * p for p in self.part]
        p0, p1, p2 = part
        c0, c1, c2 = split3(self.cross + smoothing * smoothing)
        w3, p03, p13 = (pltpu.roll(x, 3, 0) for x in (w, p0, p1))
        return [
            self.first(w, 1.0, 1.0, self.norm_hi, self.norm_lo),
            self.tile(p0, p13, c0, c1),
            self.tile(p2, w3, c2, 1.0),
            self.tile(w, w3, 1.0, 1.0),
            self.tile(p0, p03, None, None),
            self.tile(p1, None, None, None),
            self.zeros(16),
        ]

    def target_normal(self):
        w, (p0, p1, p2) = self.whole, self.part
        move = self.moved
        return [
            self.tile(w, move(w), -1.0, -1.0),
            self.tile(w, move(p0), -1.0, None),
            self.tile(p1, move(p2), None, None),
            self.tile(p0, move(p1), None, None),
            self.tile(p0, None, None, None),
            self.zeros(24),
        ]


def sources(f):
    x = jnp.concatenate(f.source_square() + f.source_normal(), axis=0).T
    top = x[:64]
    left = iota(top.shape, 1) < 64
    return x.astype(bf16), jnp.where(left, top, pltpu.roll(top, 64, 1)).astype(bf16)


def point_sources(f):
    x = f.source_square()
    return jnp.concatenate(x + x, axis=0).T.astype(bf16)


def halves(x):
    left = iota(x.shape, 1) < 64
    a = jnp.where(left, x, 0.0)
    b = jnp.where(left, 0.0, x)
    return (a, pltpu.roll(a, 64, 1)), (pltpu.roll(b, 64, 1), b)


def pair_weights(square):
    return [jnp.concatenate(x, axis=0).astype(bf16) for x in halves(jnp.concatenate(square, axis=0))]


def compact(entries, first, dead):
    slots, targets = entries.shape
    place = iota(entries.shape, 0)
    out = jnp.full(entries.shape, dead, jnp.int32)
    count = jnp.zeros((1, targets), jnp.int32)
    for k in range(slots):
        e = entries[k : k + 1]
        live = e >= 0
        at = jnp.where(live, count, -1)
        out = jnp.where(place == at, e - first, out)
        count = count + jnp.where(live, 1, 0)
    return out, count


def items(near, count, dead, out_ref):
    slots, targets = near.shape
    mine = (count + 1) // 2
    before = jnp.where(iota((targets, targets), 0) < iota((targets, targets), 1), 1.0, 0.0).astype(bf16)
    start = dot(jnp.broadcast_to(mine.astype(f32), (8, targets)).astype(bf16), before)[0:1]
    total = jnp.sum(mine, axis=1, keepdims=True).astype(f32)
    table = near.astype(f32).astype(bf16)
    rows = out_ref.shape[0] - 1
    wide = iota((rows, targets), 1)
    slot = iota((rows, slots), 1)
    lane = iota((rows, 128), 1)
    out = jnp.zeros((rows, 128), f32)
    for u in range(UNROLL):
        place = (iota((rows, 1), 0) * UNROLL + (u - LEAD)).astype(f32)
        begun = start <= place
        target = jnp.sum(jnp.where(begun, 1.0, 0.0), axis=1, keepdims=True) - 1.0
        base = jnp.max(jnp.where(begun, start, 0.0), axis=1, keepdims=True)
        pick = jnp.where(wide.astype(f32) == target, 1.0, 0.0).astype(bf16)
        lists = dot_t(pick, table)
        used = (place >= 0.0) & (place < total)
        first = 2.0 * (place - base)
        out = jnp.where(lane == u, jnp.where(used, target, float(targets)), out)
        for h in range(2):
            chosen = jnp.where(slot.astype(f32) == first + float(h), lists, 0.0)
            ids = jnp.where(used, jnp.sum(chosen, axis=1, keepdims=True), float(dead))
            out = jnp.where(lane == (h + 1) * UNROLL + u, ids, out)
    out_ref[0:rows] = out.astype(jnp.int32)
    out_ref[rows:] = jnp.broadcast_to(total, (1, 128)).astype(jnp.int32)


def list_rows(slots, leaves):
    return -(-(leaves * (slots // 2) // UNROLL + 3) // 8) * 8 + 1


def pack_kernel(target_ref, density_ref, out_ref, count_ref, slot_ref, *, peers, per):
    leaves, nrhs, leaf = density_ref.shape
    for d in range(peers):
        count_ref[d] = 0
    for k in range(leaves):
        t = target_ref[k]
        d = t // leaves
        c = count_ref[d]
        count_ref[d] = c + 1
        slot_ref[d * per + c] = t - d * leaves
        out_ref[d, pl.ds(pl.multiple_of(c * nrhs, nrhs), nrhs), :] = density_ref[k]
    row = iota((8, leaf), 0)
    for d in range(peers):
        x = jnp.zeros((8, leaf), f32)
        for c in range(per):
            x = jnp.where(row == c, slot_ref[d * per + c].astype(f32), x)
        out_ref[d, per * nrhs :, :] = x.astype(bf16)


def feature_kernel(
    node_list_ref, geo_ref, node_ref, near_ref, far_ref,
    fs_ref, fd_ref, ft_ref, wf_ref, split_ref, gn_ref, own_list_ref, halo_list_ref, far_list_ref,
    pad_ref, npad_ref, fsn_ref, wfn_ref,
):
    leaves = fs_ref.shape[0]
    nodes_here = wfn_ref.shape[0]
    slots = near_ref.shape[0]
    index = lax.axis_index(AXES)
    first = index * leaves - REACH
    wide = leaves + 2 * REACH
    pad_ref[...] = jnp.zeros(pad_ref.shape, f32)
    pad_ref[0:6, :] = geo_ref[...]
    npad_ref[...] = jnp.zeros(npad_ref.shape, f32)
    npad_ref[0:3, :] = node_ref[...]
    entries = near_ref[...]
    local = (entries >= index * leaves) & (entries < (index + 1) * leaves)
    items(*compact(jnp.where(local, entries, -1), index * leaves, leaves), leaves, own_list_ref)
    items(*compact(jnp.where(local, -1, entries), first, wide), wide, halo_list_ref)
    far, _ = compact(far_ref[...], first, wide)
    same = jnp.where(iota((leaves, leaves), 0) == iota((leaves, leaves), 1), 1.0, 0.0).astype(bf16)
    far_list_ref[:, 0:slots] = dot_t(same, far.astype(f32).astype(bf16)).astype(jnp.int32)

    def leaf_step(l, _):
        g = pad_ref[:, pl.ds(pl.multiple_of(l * 128, 128), 128)]
        f = Features(g)
        fs_ref[l], fd_ref[l] = sources(f)
        square = f.target_square()
        normal = f.target_normal()
        ft_ref[l] = jnp.concatenate(
            [
                jnp.concatenate(square + [f.zeros(64)], axis=0),
                jnp.concatenate([f.zeros(64)] + normal, axis=0),
            ],
            axis=1,
        ).astype(bf16)
        wf_ref[l] = pair_weights(square)[0]
        return 0

    lax.fori_loop(0, leaves, leaf_step, 0, unroll=4)

    def split_step(l, _):
        parts = []
        for k in range(2):
            parts += split3(pad_ref[:, pl.ds(pl.multiple_of((l * 2 + k) * 128, 128), 128)])
        split_ref[pl.ds(pl.multiple_of(l * 48, 48), 48), :] = jnp.concatenate(parts, axis=0).astype(bf16)
        return 0

    lax.fori_loop(0, leaves // 2, split_step, 0, unroll=4)

    def node_step(l, _):
        fsn_ref[l] = point_sources(Features(npad_ref[:, pl.ds(pl.multiple_of(l * 128, 128), 128)]))
        return 0

    n_nodes = 2 * fsn_ref.shape[0]
    lax.fori_loop(0, n_nodes // 2, node_step, 0, unroll=4)
    chunk = index * (nodes_here // 2)
    for l in range(nodes_here // 2):
        f = Features(npad_ref[:, pl.ds(pl.multiple_of((chunk + l) * 128, 128), 128)])
        wfn_ref[2 * l], wfn_ref[2 * l + 1] = pair_weights(f.target_square())

    node_slots = node_list_ref.shape[1]
    left = iota((64, 128), 1) < 64

    def node_field(p, _):
        x = []
        for j in range(0, node_slots, 2):
            pair = []
            for u in range(2):
                s = jnp.maximum(node_list_ref[p, j + u], 0)
                pair.append(fsn_ref[s // 2, pl.ds(pl.multiple_of((s % 2) * 64, 64), 64), :])
            x.append(jnp.where(left, pair[0], pair[1]))
        out = dot(jnp.concatenate(x, axis=0), wfn_ref[p])
        gn_ref[p] = (lax.rsqrt(out) * inv_four_pi).astype(bf16)
        return 0

    lax.fori_loop(0, nodes_here, node_field, 0)


def skeleton_kernel(
    arrived_ref, basis_ref, transfer_ref, split_ref, own_ref, a_ref, b_ref, node_ref, *, per
):
    peers = arrived_ref.shape[0]
    leaves = peers * per
    nrhs = 32
    half = leaves // 2
    for d in range(peers):
        slots = arrived_ref[d, per * nrhs :, :].astype(f32).astype(jnp.int32)
        for c in range(per):
            s = slots[c, 0]
            h = s // half
            own_ref[h, pl.ds(pl.multiple_of((s - h * half) * nrhs, nrhs), nrhs), :] = arrived_ref[
                d, c * nrhs : (c + 1) * nrhs, :
            ]
    left = iota((nrhs, 128), 1) < 64
    skels = []
    for p in range(leaves // 2):
        h, q = divmod(p, half // 2)
        out = dot_t(own_ref[h, q * 64 : (q + 1) * 64, :], basis_ref[p])
        pair = jnp.where(left, out[:nrhs], out[nrhs:]).astype(bf16)
        own_ref[h, half * nrhs + q * nrhs : half * nrhs + (q + 1) * nrhs, :] = pair
        skels.append(pair)
    base = half * nrhs + (half // 2) * nrhs
    n_split = half * 24
    for h in range(2):
        own_ref[h, base : base + n_split, :] = split_ref[h * n_split : (h + 1) * n_split, :]
    kids = transfer_ref.shape[2] // 128
    n_pairs = len(skels) // (2 * kids)
    for p in range(n_pairs):
        stack = jnp.concatenate(
            [jnp.concatenate(skels[(2 * p + h) * kids : (2 * p + h + 1) * kids], axis=1) for h in range(2)], axis=0
        )
        out = dot_t(stack, transfer_ref[p])
        pair = jnp.where(left, out[:nrhs], out[nrhs:]).astype(bf16)
        for d in range(peers):
            node_ref[d, p * nrhs : (p + 1) * nrhs, :] = pair
    odd = lax.axis_index(AXES) % 2
    a_ref[...] = own_ref[1 - odd]
    b_ref[...] = own_ref[odd]


def doubled(pairs, out_ref, k):
    rows = pairs.shape[0]
    i, j = iota((128, 256), 0), iota((128, 256), 1)
    pick = jnp.where(i == (j % 64) + 64 * (j // 128), 1.0, 0.0).astype(bf16)
    both = dot(pairs, pick).astype(bf16)
    for p in range(rows // 32):
        for h in range(2):
            out_ref[k + 2 * p + h] = both[32 * p : 32 * p + 32, 128 * h : 128 * h + 128]


def far_left(ids, skel_ref):
    left = iota((32, 128), 1) < 64
    cols = []
    for j in range(0, len(ids), 4):
        a, b, c, d = (skel_ref[s] for s in ids[j : j + 4])
        cols.append(jnp.concatenate([jnp.where(left, a, c), jnp.where(left, b, d)], axis=0))
    return jnp.concatenate(cols, axis=1)


def near_pairs(list_ref, fs_ref, ft_ref, dens_ref, k_ref, near_ref):
    def item(i, u, part):
        return list_ref[i, part * UNROLL + u]

    def step(i, _):
        for u in range(UNROLL):
            lhs = jnp.concatenate([dens_ref[item(i, u, 1)], dens_ref[item(i, u, 2)]], axis=1)
            near_ref[item(i, u, 0)] += dot(lhs, k_ref[u])
        for u in range(UNROLL):
            x = jnp.concatenate([fs_ref[item(i + 1, u, 1)], fs_ref[item(i + 1, u, 2)]], axis=0)
            out = dot(x, ft_ref[item(i + 1, u, 0)])
            r = lax.rsqrt(out[:, :128])
            k_ref[u] = ((out[:, 128:] * r) * (r * r)).astype(bf16)
        return 0

    n = list_ref[list_ref.shape[0] - 1, 0]
    lax.fori_loop(0, (n + UNROLL - 1) // UNROLL + 1, step, 0)


def own_kernel(list_ref, fs_hbm, ft_hbm, own_ref, near_ref, fs_ref, ft_ref, dens_ref, k_ref, sem):
    leaves = fs_hbm.shape[0]
    half = leaves // 2
    nrhs = 32
    copies = [
        pltpu.make_async_copy(fs_hbm, fs_ref.at[pl.ds(0, leaves)], sem.at[0]),
        pltpu.make_async_copy(ft_hbm, ft_ref.at[pl.ds(0, leaves)], sem.at[1]),
        pltpu.make_async_copy(fs_hbm.at[0], fs_ref.at[leaves], sem.at[2]),
    ]
    for c in copies:
        c.start()
    for l in range(leaves):
        dens_ref[l] = own_ref[l // half, l % half * nrhs : (l % half + 1) * nrhs, :]
    dens_ref[leaves] = jnp.zeros((nrhs, 128), bf16)
    near_ref[...] = jnp.zeros(near_ref.shape, f32)
    for c in copies:
        c.wait()
    near_pairs(list_ref, fs_ref, ft_ref, dens_ref, k_ref, near_ref)


def leaf_kernel(
    list_ref, far_list_ref, fs_own_ref, fd_own_ref, ft_hbm, wf_hbm, own_ref, a_ref, b_ref, first_ref,
    basis_hbm, transfer_hbm,
    near_out, far_out, basis_out_ref, transfer_out_ref,
    fs_ref, fd_ref, ft_ref, wf_ref, dens_ref, skel_ref, k_ref, g_ref, sem,
):
    leaves = wf_ref.shape[0]
    nrhs = 32
    half = leaves // 2
    wide = leaves + 2 * REACH
    odd = lax.axis_index(AXES) % 2 == 1
    slots = g_ref.shape[1] // 32
    mine = pl.ds(REACH, leaves)
    copies = [
        pltpu.make_async_copy(fd_own_ref, fd_ref.at[mine], sem.at[0]),
        pltpu.make_async_copy(ft_hbm, ft_ref.at[pl.ds(0, leaves)], sem.at[1]),
        pltpu.make_async_copy(wf_hbm, wf_ref, sem.at[2]),
        pltpu.make_async_copy(fs_own_ref.at[0], fs_ref.at[wide], sem.at[3]),
        pltpu.make_async_copy(fd_own_ref.at[0], fd_ref.at[wide], sem.at[4]),
    ]
    ahead = [
        pltpu.make_async_copy(basis_hbm, basis_out_ref, sem.at[5]),
        pltpu.make_async_copy(transfer_hbm, transfer_out_ref, sem.at[6]),
    ]
    for c in copies + ahead:
        c.start()

    base = half * nrhs + (half // 2) * nrhs
    for right, k in ((False, 0), (True, REACH + leaves)):

        def halo(l, _, right=right, k=k):
            at = pl.ds(pl.multiple_of(base + l * 48, 16), 48)
            x, y = a_ref[at, :].astype(f32), b_ref[at, :].astype(f32)
            x = jnp.where(odd, y, x) if right else jnp.where(odd, x, y)
            for j in range(2):
                g = x[24 * j : 24 * j + 8] + x[24 * j + 8 : 24 * j + 16] + x[24 * j + 16 : 24 * j + 24]
                fs_ref[k + 2 * l + j], fd_ref[k + 2 * l + j] = sources(Features(g))
            return 0

        lax.fori_loop(0, half // 2, halo, 0, unroll=2)

    def fill(view, k, dens=True):
        if dens:
            for l in range(half):
                dens_ref[k + l] = view(l * nrhs, nrhs)
        doubled(view(half * nrhs, half // 2 * nrhs), skel_ref, k)

    fill(lambda at, n: jnp.where(odd, a_ref[at : at + n, :], b_ref[at : at + n, :]), 0)
    fill(lambda at, n: own_ref[0, at : at + n, :], REACH, False)
    fill(lambda at, n: own_ref[1, at : at + n, :], REACH + half, False)
    fill(lambda at, n: jnp.where(odd, b_ref[at : at + n, :], a_ref[at : at + n, :]), REACH + leaves)
    dens_ref[wide] = jnp.zeros((nrhs, 128), bf16)
    skel_ref[wide] = jnp.zeros((nrhs, 128), bf16)
    near_out[...] = first_ref[...]
    for c in copies:
        c.wait()
    near_pairs(list_ref, fs_ref, ft_ref, dens_ref, k_ref, near_out)

    left = iota((nrhs, 128), 1) < 64
    left64 = iota((64, 128), 1) < 64

    def far_ids(t):
        return [far_list_ref[t, u] for u in range(slots)]

    def far_step(p, _):
        done = jnp.maximum(p - 1, 0)
        e, o = (dot(far_left(far_ids(2 * done + h), skel_ref), g_ref[h]) for h in range(2))
        even = e[:nrhs] + pltpu.roll(e[nrhs:], 64, 1)
        odd_ = pltpu.roll(o[:nrhs], 64, 1) + o[nrhs:]
        far_out[done] = jnp.where(left, even, odd_)
        for h in range(2):
            t = 2 * jnp.minimum(p, half - 1) + h
            ids = far_ids(t)
            x = [
                jnp.where(left64, fd_ref[ids[j]], fd_ref[ids[j + 1]]) for j in range(0, slots, 2)
            ]
            out = dot(jnp.concatenate(x, axis=0), wf_ref[t])
            g_ref[h] = (lax.rsqrt(out) * inv_four_pi).astype(bf16)
        return 0

    lax.fori_loop(0, half + 1, far_step, 0)
    for c in ahead:
        c.wait()


def node_kernel(
    list_ref, near_ref, far_ref, skel_ref, gn_ref, transfer_ref, basis_ref,
    out_ref,
    all_ref,
):
    nrhs = 32
    nodes_here = gn_ref.shape[0]
    pairs = skel_ref.shape[0] // nrhs
    doubled(skel_ref[...], all_ref, 0)
    all_ref[2 * pairs] = jnp.zeros((nrhs, 128), bf16)
    slots = list_ref.shape[1]
    left = iota((nrhs, 128), 1) < 64
    kids = transfer_ref.shape[2] // 128

    def node(p, _):
        ids = []
        for j in range(slots):
            e = list_ref[p, j]
            ids.append(jnp.where(e < 0, 2 * pairs, e))
        acc = dot(far_left(ids, all_ref), gn_ref[p])
        x = acc[:nrhs] + pltpu.roll(acc[nrhs:], 64, 1)
        down = dot(x[:, :64].astype(bf16), transfer_ref[p])
        for c in range(kids):
            q = p * kids + c
            local = (far_ref[q] + down[:, c * 128 : (c + 1) * 128]).astype(bf16).astype(f32)
            both = jnp.concatenate(
                [jnp.where(left, local, 0.0), jnp.where(left, 0.0, local)], axis=0
            ).astype(bf16)
            y = dot(both, basis_ref[q])
            out_ref[2 * q] = (near_ref[2 * q] + y[:nrhs]).astype(bf16)
            out_ref[2 * q + 1] = (near_ref[2 * q + 1] + y[nrhs:]).astype(bf16)
        return 0

    lax.fori_loop(0, nodes_here, node, 0)


def vmem():
    return pl.BlockSpec(memory_space=pltpu.VMEM)


def smem():
    return pl.BlockSpec(memory_space=pltpu.SMEM)


def call(kernel, out, in_specs, scratch, name, flops, vmem_mib):
    many = isinstance(out, tuple)
    return pl.pallas_call(
        kernel,
        out_shape=out,
        in_specs=in_specs,
        out_specs=tuple(vmem() for _ in out) if many else vmem(),
        scratch_shapes=scratch,
        name=name,
        cost_estimate=pl.CostEstimate(flops=flops, bytes_accessed=1 << 20, transcendentals=0),
        compiler_params=pltpu.CompilerParams(vmem_limit_bytes=vmem_mib << 20),
    )


def pack(peers, per, density, leaf_target):
    leaves, nrhs, leaf = density.shape
    return call(
        lambda *r: pack_kernel(*r, peers=peers, per=per),
        jax.ShapeDtypeStruct((peers, per * nrhs + 8, leaf), bf16),
        [smem(), vmem()],
        [pltpu.SMEM((peers,), jnp.int32), pltpu.SMEM((leaves,), jnp.int32)],
        "pack",
        1 << 20,
        2,
    )(hbm(leaf_target), hbm(density))


def features(node_list, geometry, node_points, near_list, far_list):
    leaves, slots = near_list.shape
    nodes = node_points.shape[1] // 64
    nodes_here, node_slots = node_list.shape
    shape = jax.ShapeDtypeStruct
    return call(
        feature_kernel,
        (
            pltpu.HBM((leaves, 128, 128), bf16),
            pltpu.HBM((leaves, 64, 128), bf16),
            pltpu.HBM((leaves, 128, 256), bf16),
            pltpu.HBM((leaves, 128, 128), bf16),
            pltpu.VMEM((leaves * 24, 128), bf16),
            pltpu.VMEM((nodes_here, node_slots * 32, 128), bf16),
            pltpu.HBM((list_rows(slots, leaves), 128), jnp.int32),
            pltpu.HBM((list_rows(slots, leaves), 128), jnp.int32),
            pltpu.HBM((leaves, 128), jnp.int32),
        ),
        [smem()] + [vmem()] * 4,
        [
            pltpu.VMEM((8, leaves * 128), f32),
            pltpu.VMEM((8, nodes * 64), f32),
            pltpu.VMEM((nodes // 2, 128, 128), bf16),
            pltpu.VMEM((nodes_here, 128, 128), bf16),
        ],
        "features",
        1 << 30,
        14,
    )(hbm(node_list), hbm(geometry), hbm(node_points), hbm(near_list.T), hbm(far_list.T))


def skeletons(arrived, basis_in, transfer, split, per):
    peers = arrived.shape[0]
    leaves = peers * per
    nodes_here = transfer.shape[0]
    rows = leaves // 2 * 32 + leaves // 4 * 32 + leaves // 2 * 24
    shape = jax.ShapeDtypeStruct
    return call(
        lambda *r: skeleton_kernel(*r, per=per),
        (
            pltpu.VMEM((2, rows, 128), bf16),
            shape((rows, 128), bf16),
            shape((rows, 128), bf16),
            shape((peers, nodes_here // 2 * 32, 128), bf16),
        ),
        [vmem()] * 4,
        [],
        "skeleton",
        1 << 26,
        6,
    )(
        arrived,
        basis_in.reshape(leaves // 2, 128, -1),
        transfer.reshape(nodes_here // 2, 128, -1),
        split,
    )


def own_fields(own_list, fs, ft, own):
    leaves = ft.shape[0]
    anywhere = pl.BlockSpec(memory_space=pl.ANY)
    return call(
        own_kernel,
        pltpu.VMEM((leaves + 1, 32, 128), f32),
        [smem(), anywhere, anywhere, vmem()],
        [
            pltpu.VMEM((leaves + 1, 128, 128), bf16),
            pltpu.VMEM((leaves + 1, 128, 256), bf16),
            pltpu.VMEM((leaves + 1, 32, 128), bf16),
            pltpu.VMEM((UNROLL, 256, 128), bf16),
            pltpu.SemaphoreType.DMA((3,)),
        ],
        "own",
        1 << 31,
        12,
    )(hbm(own_list), hbm(fs), hbm(ft), own)


def leaf_fields(slots, halo_list, far_list, fs, fd, ft, wf, own, got_a, got_b, first, basis_out, transfer):
    leaves = ft.shape[0]
    wide = leaves + 2 * REACH
    anywhere = pl.BlockSpec(memory_space=pl.ANY)
    return call(
        leaf_kernel,
        (
            pltpu.VMEM((leaves + 1, 32, 128), f32),
            pltpu.VMEM((leaves // 2, 32, 128), f32),
            pltpu.VMEM(basis_out.shape, bf16),
            pltpu.VMEM(transfer.shape, bf16),
        ),
        [smem()] * 2 + [anywhere] * 4 + [vmem()] * 4 + [anywhere] * 2,
        [
            pltpu.VMEM((wide + 1, 128, 128), bf16),
            pltpu.VMEM((wide + 1, 64, 128), bf16),
            pltpu.VMEM((leaves + 1, 128, 256), bf16),
            pltpu.VMEM((leaves, 128, 128), bf16),
            pltpu.VMEM((wide + 1, 32, 128), bf16),
            pltpu.VMEM((wide + 1, 32, 128), bf16),
            pltpu.VMEM((UNROLL, 256, 128), bf16),
            pltpu.VMEM((2, slots * 32, 128), bf16),
            pltpu.SemaphoreType.DMA((7,)),
        ],
        "leaves",
        1 << 31,
        20,
    )(
        hbm(halo_list), hbm(far_list), hbm(fs), hbm(fd), hbm(ft), hbm(wf), own, hbm(got_a), hbm(got_b), first,
        hbm(basis_out), hbm(transfer),
    )


def finish(node_list, near, far, all_skel, gn, transfer, basis_out):
    leaves, leaf = 2 * basis_out.shape[0], basis_out.shape[2]
    nrhs = near.shape[1]
    nodes = all_skel.shape[0] // 16
    return call(
        node_kernel,
        jax.ShapeDtypeStruct((leaves, nrhs, leaf), bf16),
        [smem()] + [vmem()] * 6,
        [pltpu.VMEM((nodes + 1, nrhs, 128), bf16)],
        "nodes",
        1 << 28,
        8,
    )(hbm(node_list), near, far, all_skel, gn, transfer, basis_out)


def hbm(x):
    return pltpu.with_memory_space_constraint(x, pltpu.HBM)


def on_device(
    density, leaf_target, geometry, near_list, far_list, node_list, basis_in, basis_out, transfer, node_points
):
    peers = lax.axis_size(AXES)
    per = density.shape[0] // peers
    outgoing = pack(peers, per, density, leaf_target)
    arrived = lax.all_to_all(outgoing, AXES, split_axis=0, concat_axis=0, tiled=True)
    fs, fd, ft, wf, split, gn, own_pairs, halo_pairs, far_rows = features(node_list, geometry, node_points, near_list, far_list)
    own, to_a, to_b, node_out = skeletons(arrived, basis_in, transfer, split, per)
    all_skel = lax.all_to_all(node_out, AXES, split_axis=0, concat_axis=0, tiled=True)
    swap_a = [(i, i ^ 1) for i in range(peers)]
    swap_b = [(i, i + 1) for i in range(1, peers - 1, 2)] + [(i + 1, i) for i in range(1, peers - 1, 2)]
    got_a = lax.ppermute(to_a, AXES, swap_a)
    got_b = lax.ppermute(to_b, AXES, swap_b)
    first = own_fields(own_pairs, fs, ft, own)
    near, far, basis_out, transfer = leaf_fields(
        near_list.shape[1], halo_pairs, far_rows, fs, fd, ft, wf, own, got_a, got_b, first,
        basis_out.reshape(basis_out.shape[0] // 2, 128, -1), transfer,
    )
    return finish(node_list, near, far, all_skel.reshape(-1, 128), gn, transfer, basis_out)


def solution(mesh):
    split = ("grp", "row", "col")
    return jax.shard_map(
        on_device,
        mesh=mesh,
        in_specs=(
            P(split, None, None),
            P(split),
            P(None, split),
            P(split, None),
            P(split, None),
            P(split, None),
            P(split, None, None),
            P(split, None, None),
            P(split, None, None),
            P(None, "grp"),
        ),
        out_specs=P(split, None, None),
        check_vma=False,
    )
```

```python
import math

import jax
import jax.numpy as jnp
from jax import lax
from jax.experimental import pallas as pl
from jax.experimental.pallas import tpu as pltpu
from jax.sharding import PartitionSpec as P

REACH = 16
AXES = ("row", "col")

smoothing = 0.1
inv_four_pi = 0.25 / math.pi
grid_step = 16.0
UNROLL = 12
FAR_UNROLL = 8
bf16 = jnp.bfloat16
f32 = jnp.float32


def split3(x):
    first = x.astype(bf16).astype(f32)
    rest = x - first
    second = rest.astype(bf16).astype(f32)
    third = (rest - second).astype(bf16).astype(f32)
    return first, second, third


def iota(shape, axis):
    return lax.broadcasted_iota(jnp.int32, shape, axis)


def dot(a, b):
    return lax.dot_general(a, b, (((1,), (0,)), ((), ())), preferred_element_type=f32)


def dot_t(a, b):
    return lax.dot_general(a, b, (((1,), (1,)), ((), ())), preferred_element_type=f32)


class Features:
    def __init__(self, g):
        self.shape = g.shape
        self.row = row = iota(g.shape, 0)
        point = row < 3
        c = jnp.where(point, g, 0.0)
        self.whole = whole = jnp.floor(c * grid_step + 0.5) * (1.0 / grid_step)
        part = c - whole
        self.part = split3(part)
        m = jnp.where(point, 0.0, g) * inv_four_pi
        self.m = split3(m)
        norm = jnp.sum(whole * whole, axis=0, keepdims=True)
        self.norm_hi = jnp.floor(norm)
        self.norm_lo = norm - self.norm_hi
        self.cross = jnp.sum(part * (2.0 * whole + part), axis=0, keepdims=True)
        self.q = split3(jnp.sum(m * pltpu.roll(c, 3, 0), axis=0, keepdims=True))
        self.low = {}

    def moved(self, x):
        if id(x) not in self.low:
            self.low[id(x)] = pltpu.roll(x, 3, 0)
        return self.low[id(x)]

    def tile(self, upper, lower, six, seven):
        row = self.row
        x = jnp.where(row < 3, upper, 0.0)
        if lower is not None:
            x = jnp.where(row < 3, upper, jnp.where(row < 6, lower, 0.0))
        if six is not None:
            x = jnp.where(row == 6, six, x)
        if seven is not None:
            x = jnp.where(row == 7, seven, x)
        return x

    def first(self, points, three, four, five, six):
        row = self.row
        x = jnp.where(row == 3, three, jnp.where(row == 4, four, 0.0))
        x = jnp.where(row == 5, five, jnp.where(row == 6, six, x))
        return jnp.where(row < 3, points, x)

    def zeros(self, rows):
        return jnp.zeros((rows, self.shape[1]), f32)

    def source_square(self):
        w, (p0, p1, p2) = self.whole, self.part
        c0, c1, c2 = split3(self.cross)
        move = self.moved
        return [
            self.first(w, self.norm_hi, self.norm_lo, 1.0, 1.0),
            self.tile(w, move(w), 1.0, 1.0),
            self.tile(w, move(p0), 1.0, c0),
            self.tile(p1, move(p2), c1, c2),
            self.tile(p0, move(p1), None, None),
            self.tile(p0, None, None, None),
            self.zeros(16),
        ]

    def source_normal(self):
        m0, m1, m2 = self.m
        u0, u1, u2 = (pltpu.roll(x, 5, 0) for x in self.m)
        q0, q1, q2 = self.q
        return [
            self.tile(u0, m1, q0, q1),
            self.tile(u2, m0, q2, None),
            self.tile(u0, m0, None, None),
            self.tile(u1, m1, None, None),
            self.tile(u2, None, None, None),
            self.zeros(24),
        ]

    def target_square(self):
        w, part = -2.0 * self.whole, [-2.0 * p for p in self.part]
        p0, p1, p2 = part
        c0, c1, c2 = split3(self.cross + smoothing * smoothing)
        w3, p03, p13 = (pltpu.roll(x, 3, 0) for x in (w, p0, p1))
        return [
            self.first(w, 1.0, 1.0, self.norm_hi, self.norm_lo),
            self.tile(p0, p13, c0, c1),
            self.tile(p2, w3, c2, 1.0),
            self.tile(w, w3, 1.0, 1.0),
            self.tile(p0, p03, None, None),
            self.tile(p1, None, None, None),
            self.zeros(16),
        ]

    def target_normal(self):
        w, (p0, p1, p2) = self.whole, self.part
        move = self.moved
        return [
            self.tile(w, move(w), -1.0, -1.0),
            self.tile(w, move(p0), -1.0, None),
            self.tile(p1, move(p2), None, None),
            self.tile(p0, move(p1), None, None),
            self.tile(p0, None, None, None),
            self.zeros(24),
        ]


def sources(f):
    x = jnp.concatenate(f.source_square() + f.source_normal(), axis=0).T
    top = x[:64]
    left = iota(top.shape, 1) < 64
    return x.astype(bf16), jnp.where(left, top, pltpu.roll(top, 64, 1)).astype(bf16)


def point_sources(f):
    x = f.source_square()
    return jnp.concatenate(x + x, axis=0).T.astype(bf16)


def halves(x):
    left = iota(x.shape, 1) < 64
    a = jnp.where(left, x, 0.0)
    b = jnp.where(left, 0.0, x)
    return (a, pltpu.roll(a, 64, 1)), (pltpu.roll(b, 64, 1), b)


def pair_weights(square):
    return [jnp.concatenate(x, axis=0).astype(bf16) for x in halves(jnp.concatenate(square, axis=0))]


def compact(entries, first, dead):
    slots, targets = entries.shape
    place = iota(entries.shape, 0)
    out = jnp.full(entries.shape, dead, jnp.int32)
    count = jnp.zeros((1, targets), jnp.int32)
    for k in range(slots):
        e = entries[k : k + 1]
        live = e >= 0
        at = jnp.where(live, count, -1)
        out = jnp.where(place == at, e - first, out)
        count = count + jnp.where(live, 1, 0)
    return out, count


def items(near, count, dead, out_ref):
    slots, targets = near.shape
    mine = (count + 1) // 2
    before = jnp.where(iota((targets, targets), 0) < iota((targets, targets), 1), 1.0, 0.0).astype(bf16)
    start = dot(jnp.broadcast_to(mine.astype(f32), (8, targets)).astype(bf16), before)[0:1]
    total = jnp.sum(mine, axis=1, keepdims=True).astype(f32)
    table = near.astype(f32).astype(bf16)
    rows = out_ref.shape[0] - 1
    wide = iota((rows, targets), 1)
    slot = iota((rows, slots), 1)
    lane = iota((rows, 128), 1)
    out = jnp.zeros((rows, 128), f32)
    for u in range(UNROLL):
        place = (iota((rows, 1), 0) * UNROLL + u).astype(f32)
        begun = start <= place
        target = jnp.sum(jnp.where(begun, 1.0, 0.0), axis=1, keepdims=True) - 1.0
        base = jnp.max(jnp.where(begun, start, 0.0), axis=1, keepdims=True)
        pick = jnp.where(wide.astype(f32) == target, 1.0, 0.0).astype(bf16)
        lists = dot_t(pick, table)
        used = (place >= 0.0) & (place < total)
        first = 2.0 * (place - base)
        out = jnp.where(lane == u, jnp.where(used, target, float(targets)), out)
        for h in range(2):
            chosen = jnp.where(slot.astype(f32) == first + float(h), lists, 0.0)
            ids = jnp.where(used, jnp.sum(chosen, axis=1, keepdims=True), float(dead))
            out = jnp.where(lane == (h + 1) * UNROLL + u, ids, out)
    out_ref[0:rows] = out.astype(jnp.int32)
    out_ref[rows:] = jnp.broadcast_to(total, (1, 128)).astype(jnp.int32)


def list_rows(slots, leaves):
    return -(-(leaves * (slots // 2) // UNROLL + 1) // 8) * 8 + 1


def pack_kernel(target_ref, density_ref, out_ref, count_ref, slot_ref, *, peers, per):
    leaves, nrhs, leaf = density_ref.shape
    for d in range(peers):
        count_ref[d] = 0
    for k in range(leaves):
        t = target_ref[k]
        d = t // leaves
        c = count_ref[d]
        count_ref[d] = c + 1
        slot_ref[d * per + c] = t - d * leaves
        out_ref[d, pl.ds(pl.multiple_of(c * nrhs, nrhs), nrhs), :] = density_ref[k]
    row = iota((8, leaf), 0)
    for d in range(peers):
        x = jnp.zeros((8, leaf), f32)
        for c in range(per):
            x = jnp.where(row == c, slot_ref[d * per + c].astype(f32), x)
        out_ref[d, per * nrhs :, :] = x.astype(bf16)


def feature_kernel(
    node_list_ref, geo_ref, node_ref, near_ref, far_ref,
    fs_ref, fd_ref, ft_ref, wf_ref, split_ref, gn_ref, own_list_ref, halo_list_ref, far_list_ref,
    pad_ref, npad_ref, fsn_ref, wfn_ref,
):
    leaves = fs_ref.shape[0]
    nodes_here = wfn_ref.shape[0]
    slots = near_ref.shape[0]
    index = lax.axis_index(AXES)
    first = index * leaves - REACH
    wide = leaves + 2 * REACH
    pad_ref[...] = jnp.zeros(pad_ref.shape, f32)
    pad_ref[0:6, :] = geo_ref[...]
    npad_ref[...] = jnp.zeros(npad_ref.shape, f32)
    npad_ref[0:3, :] = node_ref[...]
    entries = near_ref[...]
    local = (entries >= index * leaves) & (entries < (index + 1) * leaves)
    items(*compact(jnp.where(local, entries, -1), index * leaves, leaves), leaves, own_list_ref)
    items(*compact(jnp.where(local, -1, entries), first, wide), wide, halo_list_ref)
    far, _ = compact(far_ref[...], first, wide)
    same = jnp.where(iota((leaves, leaves), 0) == iota((leaves, leaves), 1), 1.0, 0.0).astype(bf16)
    far_list_ref[:, 0:slots] = dot_t(same, far.astype(f32).astype(bf16)).astype(jnp.int32)

    def leaf_step(l, _):
        g = pad_ref[:, pl.ds(pl.multiple_of(l * 128, 128), 128)]
        f = Features(g)
        fs_ref[l], fd_ref[l] = sources(f)
        square = f.target_square()
        normal = f.target_normal()
        ft_ref[l] = jnp.concatenate(
            [
                jnp.concatenate(square + [f.zeros(64)], axis=0),
                jnp.concatenate([f.zeros(64)] + normal, axis=0),
            ],
            axis=1,
        ).astype(bf16)
        wf_ref[l] = pair_weights(square)[0]
        return 0

    lax.fori_loop(0, leaves, leaf_step, 0, unroll=4)

    def split_step(l, _):
        parts = []
        for k in range(2):
            parts += split3(pad_ref[:, pl.ds(pl.multiple_of((l * 2 + k) * 128, 128), 128)])
        split_ref[pl.ds(pl.multiple_of(l * 48, 48), 48), :] = jnp.concatenate(parts, axis=0).astype(bf16)
        return 0

    lax.fori_loop(0, leaves // 2, split_step, 0, unroll=4)

    def node_step(l, _):
        fsn_ref[l] = point_sources(Features(npad_ref[:, pl.ds(pl.multiple_of(l * 128, 128), 128)]))
        return 0

    n_nodes = 2 * fsn_ref.shape[0]
    lax.fori_loop(0, n_nodes // 2, node_step, 0, unroll=4)
    chunk = index * (nodes_here // 2)
    for l in range(nodes_here // 2):
        f = Features(npad_ref[:, pl.ds(pl.multiple_of((chunk + l) * 128, 128), 128)])
        wfn_ref[2 * l], wfn_ref[2 * l + 1] = pair_weights(f.target_square())

    node_slots = node_list_ref.shape[1]
    left = iota((64, 128), 1) < 64

    def node_field(p, _):
        x = []
        for j in range(0, node_slots, 2):
            pair = []
            for u in range(2):
                s = jnp.maximum(node_list_ref[p, j + u], 0)
                pair.append(fsn_ref[s // 2, pl.ds(pl.multiple_of((s % 2) * 64, 64), 64), :])
            x.append(jnp.where(left, pair[0], pair[1]))
        out = dot(jnp.concatenate(x, axis=0), wfn_ref[p])
        gn_ref[p] = (lax.rsqrt(out) * inv_four_pi).astype(bf16)
        return 0

    lax.fori_loop(0, nodes_here, node_field, 0)


def skeleton_kernel(
    arrived_ref, basis_ref, transfer_ref, split_ref, own_ref, a_ref, b_ref, node_ref, *, per
):
    peers = arrived_ref.shape[0]
    leaves = peers * per
    nrhs = 32
    half = leaves // 2
    for d in range(peers):
        slots = arrived_ref[d, per * nrhs :, :].astype(f32).astype(jnp.int32)
        for c in range(per):
            s = slots[c, 0]
            h = s // half
            own_ref[h, pl.ds(pl.multiple_of((s - h * half) * nrhs, nrhs), nrhs), :] = arrived_ref[
                d, c * nrhs : (c + 1) * nrhs, :
            ]
    left = iota((nrhs, 128), 1) < 64
    skels = []
    for p in range(leaves // 2):
        h, q = divmod(p, half // 2)
        out = dot_t(own_ref[h, q * 64 : (q + 1) * 64, :], basis_ref[p])
        pair = jnp.where(left, out[:nrhs], out[nrhs:]).astype(bf16)
        own_ref[h, half * nrhs + q * nrhs : half * nrhs + (q + 1) * nrhs, :] = pair
        skels.append(pair)
    base = half * nrhs + (half // 2) * nrhs
    n_split = half * 24
    for h in range(2):
        own_ref[h, base : base + n_split, :] = split_ref[h * n_split : (h + 1) * n_split, :]
    kids = transfer_ref.shape[2] // 128
    n_pairs = len(skels) // (2 * kids)
    for p in range(n_pairs):
        stack = jnp.concatenate(
            [jnp.concatenate(skels[(2 * p + h) * kids : (2 * p + h + 1) * kids], axis=1) for h in range(2)], axis=0
        )
        out = dot_t(stack, transfer_ref[p])
        pair = jnp.where(left, out[:nrhs], out[nrhs:]).astype(bf16)
        for d in range(peers):
            node_ref[d, p * nrhs : (p + 1) * nrhs, :] = pair
    odd = lax.axis_index(AXES) % 2
    a_ref[...] = own_ref[1 - odd]
    b_ref[...] = own_ref[odd]


def doubled(pairs, out_ref, k):
    rows = pairs.shape[0]
    i, j = iota((128, 256), 0), iota((128, 256), 1)
    pick = jnp.where(i == (j % 64) + 64 * (j // 128), 1.0, 0.0).astype(bf16)
    both = dot(pairs, pick).astype(bf16)
    for p in range(rows // 32):
        for h in range(2):
            out_ref[k + 2 * p + h] = both[32 * p : 32 * p + 32, 128 * h : 128 * h + 128]


def far_left(ids, skel_ref):
    left = iota((32, 128), 1) < 64
    cols = []
    for j in range(0, len(ids), 4):
        a, b, c, d = (skel_ref[s] for s in ids[j : j + 4])
        cols.append(jnp.concatenate([jnp.where(left, a, c), jnp.where(left, b, d)], axis=0))
    return jnp.concatenate(cols, axis=1)


def near_pairs(list_ref, fs_ref, ft_ref, dens_ref, k_ref, near_ref):
    def item(i, u, part):
        return list_ref[i, part * UNROLL + u]

    def matrices(i):
        for u in range(UNROLL):
            x = jnp.concatenate([fs_ref[item(i, u, 1)], fs_ref[item(i, u, 2)]], axis=0)
            out = dot(x, ft_ref[item(i, u, 0)])
            r = lax.rsqrt(out[:, :128])
            k_ref[u] = ((out[:, 128:] * r) * (r * r)).astype(bf16)

    def apply(i):
        for u in range(UNROLL):
            lhs = jnp.concatenate([dens_ref[item(i, u, 1)], dens_ref[item(i, u, 2)]], axis=1)
            near_ref[item(i, u, 0)] += dot(lhs, k_ref[u])

    def step(i, _):
        apply(i - 1)
        matrices(i)
        return 0

    steps = jnp.maximum((list_ref[list_ref.shape[0] - 1, 0] + UNROLL - 1) // UNROLL, 1)
    matrices(0)
    lax.fori_loop(1, steps, step, 0)
    apply(steps - 1)


def own_kernel(
    list_hbm, fs_hbm, ft_hbm, own_ref, near_ref, fs_ref, ft_ref, dens_ref, k_ref, list_ref, sem
):
    leaves = fs_hbm.shape[0]
    half = leaves // 2
    nrhs = 32
    copies = [
        pltpu.make_async_copy(list_hbm, list_ref, sem.at[3]),
        pltpu.make_async_copy(fs_hbm, fs_ref.at[pl.ds(0, leaves)], sem.at[0]),
        pltpu.make_async_copy(ft_hbm, ft_ref.at[pl.ds(0, leaves)], sem.at[1]),
        pltpu.make_async_copy(fs_hbm.at[0], fs_ref.at[leaves], sem.at[2]),
    ]
    for c in copies:
        c.start()
    for l in range(leaves):
        dens_ref[l] = own_ref[l // half, l % half * nrhs : (l % half + 1) * nrhs, :]
    dens_ref[leaves] = jnp.zeros((nrhs, 128), bf16)
    near_ref[...] = jnp.zeros(near_ref.shape, f32)
    for c in copies:
        c.wait()
    near_pairs(list_ref, fs_ref, ft_ref, dens_ref, k_ref, near_ref)


def leaf_kernel(
    list_hbm, far_list_hbm, fs_own_ref, fd_own_ref, ft_hbm, wf_hbm, own_ref, a_ref, b_ref, first_ref,
    basis_hbm, transfer_hbm,
    near_out, far_out, basis_out_ref, transfer_out_ref,
    fs_ref, fd_ref, ft_ref, wf_ref, dens_ref, skel_ref, k_ref, g_ref, list_ref, far_list_ref, sem,
):
    leaves = wf_ref.shape[0]
    nrhs = 32
    half = leaves // 2
    wide = leaves + 2 * REACH
    odd = lax.axis_index(AXES) % 2 == 1
    slots = g_ref.shape[1] // 32
    mine = pl.ds(REACH, leaves)
    copies = [
        pltpu.make_async_copy(fd_own_ref, fd_ref.at[mine], sem.at[0]),
        pltpu.make_async_copy(ft_hbm, ft_ref.at[pl.ds(0, leaves)], sem.at[1]),
        pltpu.make_async_copy(wf_hbm, wf_ref, sem.at[2]),
        pltpu.make_async_copy(fs_own_ref.at[0], fs_ref.at[wide], sem.at[3]),
        pltpu.make_async_copy(fd_own_ref.at[0], fd_ref.at[wide], sem.at[4]),
    ]
    ahead = [
        pltpu.make_async_copy(basis_hbm, basis_out_ref, sem.at[5]),
        pltpu.make_async_copy(transfer_hbm, transfer_out_ref, sem.at[6]),
    ]
    copies += [
        pltpu.make_async_copy(list_hbm, list_ref, sem.at[7]),
        pltpu.make_async_copy(far_list_hbm, far_list_ref, sem.at[8]),
    ]
    for c in copies + ahead:
        c.start()

    base = half * nrhs + (half // 2) * nrhs
    for right, k in ((False, 0), (True, REACH + leaves)):

        def halo(l, _, right=right, k=k):
            at = pl.ds(pl.multiple_of(base + l * 48, 16), 48)
            x, y = a_ref[at, :].astype(f32), b_ref[at, :].astype(f32)
            x = jnp.where(odd, y, x) if right else jnp.where(odd, x, y)
            for j in range(2):
                g = x[24 * j : 24 * j + 8] + x[24 * j + 8 : 24 * j + 16] + x[24 * j + 16 : 24 * j + 24]
                fs_ref[k + 2 * l + j], fd_ref[k + 2 * l + j] = sources(Features(g))
            return 0

        lax.fori_loop(0, half // 2, halo, 0, unroll=2)

    def fill(view, k, dens=True):
        if dens:
            for l in range(half):
                dens_ref[k + l] = view(l * nrhs, nrhs)
        doubled(view(half * nrhs, half // 2 * nrhs), skel_ref, k)

    fill(lambda at, n: jnp.where(odd, a_ref[at : at + n, :], b_ref[at : at + n, :]), 0)
    fill(lambda at, n: own_ref[0, at : at + n, :], REACH, False)
    fill(lambda at, n: own_ref[1, at : at + n, :], REACH + half, False)
    fill(lambda at, n: jnp.where(odd, b_ref[at : at + n, :], a_ref[at : at + n, :]), REACH + leaves)
    dens_ref[wide] = jnp.zeros((nrhs, 128), bf16)
    skel_ref[wide] = jnp.zeros((nrhs, 128), bf16)
    near_out[...] = first_ref[...]
    for c in copies:
        c.wait()
    near_pairs(list_ref, fs_ref, ft_ref, dens_ref, k_ref, near_out)

    left = iota((nrhs, 128), 1) < 64
    left64 = iota((64, 128), 1) < 64

    def far_ids(t):
        return [far_list_ref[t, u] for u in range(slots)]

    def far_matrices(p):
        for h in range(FAR_UNROLL):
            ids = far_ids(FAR_UNROLL * p + h)
            x = [
                jnp.where(left64, fd_ref[ids[j]], fd_ref[ids[j + 1]]) for j in range(0, slots, 2)
            ]
            out = dot(jnp.concatenate(x, axis=0), wf_ref[FAR_UNROLL * p + h])
            g_ref[h] = (lax.rsqrt(out) * inv_four_pi).astype(bf16)

    def far_apply(p):
        for h in range(0, FAR_UNROLL, 2):
            t = FAR_UNROLL * p + h
            e, o = (dot(far_left(far_ids(t + k), skel_ref), g_ref[h + k]) for k in range(2))
            even = e[:nrhs] + pltpu.roll(e[nrhs:], 64, 1)
            odd_ = pltpu.roll(o[:nrhs], 64, 1) + o[nrhs:]
            far_out[(FAR_UNROLL // 2) * p + h // 2] = jnp.where(left, even, odd_)

    def far_step(p, _):
        far_apply(p - 1)
        far_matrices(p)
        return 0

    far_steps = leaves // FAR_UNROLL
    far_matrices(0)
    lax.fori_loop(1, far_steps, far_step, 0)
    far_apply(far_steps - 1)
    for c in ahead:
        c.wait()


def node_kernel(
    list_hbm, near_ref, far_ref, skel_ref, gn_ref, transfer_ref, basis_ref,
    out_hbm,
    all_ref, out_ref, list_ref, sem,
):
    nrhs = 32
    nodes_here = gn_ref.shape[0]
    pairs = skel_ref.shape[0] // nrhs
    listed = pltpu.make_async_copy(list_hbm, list_ref, sem.at[nodes_here])
    listed.start()
    doubled(skel_ref[...], all_ref, 0)
    all_ref[2 * pairs] = jnp.zeros((nrhs, 128), bf16)
    slots = list_ref.shape[1]
    left = iota((nrhs, 128), 1) < 64
    kids = transfer_ref.shape[2] // 128
    listed.wait()
    sent = []
    for p in range(nodes_here):
        ids = []
        for j in range(slots):
            e = list_ref[p, j]
            ids.append(jnp.where(e < 0, 2 * pairs, e))
        acc = dot(far_left(ids, all_ref), gn_ref[p])
        x = acc[:nrhs] + pltpu.roll(acc[nrhs:], 64, 1)
        down = dot(x[:, :64].astype(bf16), transfer_ref[p])
        for c in range(kids):
            q = p * kids + c
            local = (far_ref[q] + down[:, c * 128 : (c + 1) * 128]).astype(bf16).astype(f32)
            both = jnp.concatenate(
                [jnp.where(left, local, 0.0), jnp.where(left, 0.0, local)], axis=0
            ).astype(bf16)
            y = dot(both, basis_ref[q])
            out_ref[2 * q] = (near_ref[2 * q] + y[:nrhs]).astype(bf16)
            out_ref[2 * q + 1] = (near_ref[2 * q + 1] + y[nrhs:]).astype(bf16)
        here = pl.ds(p * 2 * kids, 2 * kids)
        sent.append(pltpu.make_async_copy(out_ref.at[here], out_hbm.at[here], sem.at[p]))
        sent[-1].start()
    for c in sent:
        c.wait()


def vmem():
    return pl.BlockSpec(memory_space=pltpu.VMEM)


def smem():
    return pl.BlockSpec(memory_space=pltpu.SMEM)


def call(kernel, out, in_specs, scratch, name, flops, vmem_mib, out_specs=None):
    many = isinstance(out, tuple)
    if out_specs is None:
        out_specs = tuple(vmem() for _ in out) if many else vmem()
    return pl.pallas_call(
        kernel,
        out_shape=out,
        in_specs=in_specs,
        out_specs=out_specs,
        scratch_shapes=scratch,
        name=name,
        cost_estimate=pl.CostEstimate(flops=flops, bytes_accessed=1 << 20, transcendentals=0),
        compiler_params=pltpu.CompilerParams(vmem_limit_bytes=vmem_mib << 20),
    )


def pack(peers, per, density, leaf_target):
    leaves, nrhs, leaf = density.shape
    return call(
        lambda *r: pack_kernel(*r, peers=peers, per=per),
        jax.ShapeDtypeStruct((peers, per * nrhs + 8, leaf), bf16),
        [smem(), vmem()],
        [pltpu.SMEM((peers,), jnp.int32), pltpu.SMEM((leaves,), jnp.int32)],
        "pack",
        1 << 20,
        2,
    )(hbm(leaf_target), hbm(density))


def features(node_list, geometry, node_points, near_list, far_list):
    leaves, slots = near_list.shape
    nodes = node_points.shape[1] // 64
    nodes_here, node_slots = node_list.shape
    shape = jax.ShapeDtypeStruct
    return call(
        feature_kernel,
        (
            pltpu.HBM((leaves, 128, 128), bf16),
            pltpu.HBM((leaves, 64, 128), bf16),
            pltpu.HBM((leaves, 128, 256), bf16),
            pltpu.HBM((leaves, 128, 128), bf16),
            pltpu.VMEM((leaves * 24, 128), bf16),
            pltpu.VMEM((nodes_here, node_slots * 32, 128), bf16),
            pltpu.HBM((list_rows(slots, leaves), 128), jnp.int32),
            pltpu.HBM((list_rows(slots, leaves), 128), jnp.int32),
            pltpu.HBM((leaves, 128), jnp.int32),
        ),
        [smem()] + [vmem()] * 4,
        [
            pltpu.VMEM((8, leaves * 128), f32),
            pltpu.VMEM((8, nodes * 64), f32),
            pltpu.VMEM((nodes // 2, 128, 128), bf16),
            pltpu.VMEM((nodes_here, 128, 128), bf16),
        ],
        "features",
        1 << 30,
        14,
    )(hbm(node_list), hbm(geometry), hbm(node_points), hbm(near_list.T), hbm(far_list.T))


def skeletons(arrived, basis_in, transfer, split, per):
    peers = arrived.shape[0]
    leaves = peers * per
    nodes_here = transfer.shape[0]
    rows = leaves // 2 * 32 + leaves // 4 * 32 + leaves // 2 * 24
    shape = jax.ShapeDtypeStruct
    return call(
        lambda *r: skeleton_kernel(*r, per=per),
        (
            pltpu.VMEM((2, rows, 128), bf16),
            shape((rows, 128), bf16),
            shape((rows, 128), bf16),
            shape((peers, nodes_here // 2 * 32, 128), bf16),
        ),
        [vmem()] * 4,
        [],
        "skeleton",
        1 << 26,
        6,
    )(
        arrived,
        basis_in.reshape(leaves // 2, 128, -1),
        transfer.reshape(nodes_here // 2, 128, -1),
        split,
    )


def own_fields(own_list, fs, ft, own):
    leaves = ft.shape[0]
    anywhere = pl.BlockSpec(memory_space=pl.ANY)
    return call(
        own_kernel,
        pltpu.VMEM((leaves + 1, 32, 128), f32),
        [anywhere] * 3 + [vmem()],
        [
            pltpu.VMEM((leaves + 1, 128, 128), bf16),
            pltpu.VMEM((leaves + 1, 128, 256), bf16),
            pltpu.VMEM((leaves + 1, 32, 128), bf16),
            pltpu.VMEM((UNROLL, 256, 128), bf16),
            pltpu.SMEM(own_list.shape, jnp.int32),
            pltpu.SemaphoreType.DMA((4,)),
        ],
        "own",
        1 << 31,
        12,
    )(hbm(own_list), hbm(fs), hbm(ft), own)


def leaf_fields(slots, halo_list, far_list, fs, fd, ft, wf, own, got_a, got_b, first, basis_out, transfer):
    leaves = ft.shape[0]
    wide = leaves + 2 * REACH
    anywhere = pl.BlockSpec(memory_space=pl.ANY)
    return call(
        leaf_kernel,
        (
            pltpu.VMEM((leaves + 1, 32, 128), f32),
            pltpu.VMEM((leaves // 2, 32, 128), f32),
            pltpu.VMEM(basis_out.shape, bf16),
            pltpu.VMEM(transfer.shape, bf16),
        ),
        [anywhere] * 6 + [vmem()] * 4 + [anywhere] * 2,
        [
            pltpu.VMEM((wide + 1, 128, 128), bf16),
            pltpu.VMEM((wide + 1, 64, 128), bf16),
            pltpu.VMEM((leaves + 1, 128, 256), bf16),
            pltpu.VMEM((leaves, 128, 128), bf16),
            pltpu.VMEM((wide + 1, 32, 128), bf16),
            pltpu.VMEM((wide + 1, 32, 128), bf16),
            pltpu.VMEM((UNROLL, 256, 128), bf16),
            pltpu.VMEM((FAR_UNROLL, slots * 32, 128), bf16),
            pltpu.SMEM(halo_list.shape, jnp.int32),
            pltpu.SMEM(far_list.shape, jnp.int32),
            pltpu.SemaphoreType.DMA((9,)),
        ],
        "leaves",
        1 << 31,
        20,
    )(
        hbm(halo_list), hbm(far_list), hbm(fs), hbm(fd), hbm(ft), hbm(wf), own, hbm(got_a), hbm(got_b), first,
        hbm(basis_out), hbm(transfer),
    )


def finish(node_list, near, far, all_skel, gn, transfer, basis_out):
    leaves, leaf = 2 * basis_out.shape[0], basis_out.shape[2]
    nrhs = near.shape[1]
    nodes = all_skel.shape[0] // 16
    anywhere = pl.BlockSpec(memory_space=pl.ANY)
    return call(
        node_kernel,
        jax.ShapeDtypeStruct((leaves, nrhs, leaf), bf16),
        [anywhere] + [vmem()] * 6,
        [
            pltpu.VMEM((nodes + 1, nrhs, 128), bf16),
            pltpu.VMEM((leaves, nrhs, leaf), bf16),
            pltpu.SMEM(node_list.shape, jnp.int32),
            pltpu.SemaphoreType.DMA((node_list.shape[0] + 1,)),
        ],
        "nodes",
        1 << 28,
        8,
        anywhere,
    )(hbm(node_list), near, far, all_skel, gn, transfer, basis_out)


def hbm(x):
    return pltpu.with_memory_space_constraint(x, pltpu.HBM)


def on_device(
    density, leaf_target, geometry, near_list, far_list, node_list, basis_in, basis_out, transfer, node_points
):
    peers = lax.axis_size(AXES)
    per = density.shape[0] // peers
    outgoing = pack(peers, per, density, leaf_target)
    arrived = lax.all_to_all(outgoing, AXES, split_axis=0, concat_axis=0, tiled=True)
    fs, fd, ft, wf, split, gn, own_pairs, halo_pairs, far_rows = features(node_list, geometry, node_points, near_list, far_list)
    own, to_a, to_b, node_out = skeletons(arrived, basis_in, transfer, split, per)
    all_skel = lax.all_to_all(node_out, AXES, split_axis=0, concat_axis=0, tiled=True)
    swap_a = [(i, i ^ 1) for i in range(peers)]
    swap_b = [(i, i + 1) for i in range(1, peers - 1, 2)] + [(i + 1, i) for i in range(1, peers - 1, 2)]
    got_a = lax.ppermute(to_a, AXES, swap_a)
    got_b = lax.ppermute(to_b, AXES, swap_b)
    first = own_fields(own_pairs, fs, ft, own)
    near, far, basis_out, transfer = leaf_fields(
        near_list.shape[1], halo_pairs, far_rows, fs, fd, ft, wf, own, got_a, got_b, first,
        basis_out.reshape(basis_out.shape[0] // 2, 128, -1), transfer,
    )
    return finish(node_list, near, far, all_skel.reshape(-1, 128), gn, transfer, basis_out)


def solution(mesh):
    split = ("grp", "row", "col")
    return jax.shard_map(
        on_device,
        mesh=mesh,
        in_specs=(
            P(split, None, None),
            P(split),
            P(None, split),
            P(split, None),
            P(split, None),
            P(split, None),
            P(split, None, None),
            P(split, None, None),
            P(split, None, None),
            P(None, "grp"),
        ),
        out_specs=P(split, None, None),
        check_vma=False,
    )
```

```python
import math

import jax
import jax.numpy as jnp
from jax import lax
from jax.experimental import pallas as pl
from jax.experimental.pallas import tpu as pltpu
from jax.sharding import PartitionSpec as P

REACH = 16
AXES = ("row", "col")

smoothing = 0.1
inv_four_pi = 0.25 / math.pi
grid_step = 16.0
UNROLL = 12
FAR_UNROLL = 8
bf16 = jnp.bfloat16
f32 = jnp.float32


def split3(x):
    first = x.astype(bf16).astype(f32)
    rest = x - first
    second = rest.astype(bf16).astype(f32)
    third = (rest - second).astype(bf16).astype(f32)
    return first, second, third


def iota(shape, axis):
    return lax.broadcasted_iota(jnp.int32, shape, axis)


def dot(a, b):
    return lax.dot_general(a, b, (((1,), (0,)), ((), ())), preferred_element_type=f32)


def dot_t(a, b):
    return lax.dot_general(a, b, (((1,), (1,)), ((), ())), preferred_element_type=f32)


class Features:
    def __init__(self, g):
        self.shape = g.shape
        self.row = row = iota(g.shape, 0)
        point = row < 3
        c = jnp.where(point, g, 0.0)
        self.whole = whole = jnp.floor(c * grid_step + 0.5) * (1.0 / grid_step)
        part = c - whole
        self.part = split3(part)
        m = jnp.where(point, 0.0, g) * inv_four_pi
        self.m = split3(m)
        norm = jnp.sum(whole * whole, axis=0, keepdims=True)
        self.norm_hi = jnp.floor(norm)
        self.norm_lo = norm - self.norm_hi
        self.cross = jnp.sum(part * (2.0 * whole + part), axis=0, keepdims=True)
        self.q = split3(jnp.sum(m * pltpu.roll(c, 3, 0), axis=0, keepdims=True))
        self.low = {}

    def moved(self, x):
        if id(x) not in self.low:
            self.low[id(x)] = pltpu.roll(x, 3, 0)
        return self.low[id(x)]

    def tile(self, upper, lower, six, seven):
        row = self.row
        x = jnp.where(row < 3, upper, 0.0)
        if lower is not None:
            x = jnp.where(row < 3, upper, jnp.where(row < 6, lower, 0.0))
        if six is not None:
            x = jnp.where(row == 6, six, x)
        if seven is not None:
            x = jnp.where(row == 7, seven, x)
        return x

    def first(self, points, three, four, five, six):
        row = self.row
        x = jnp.where(row == 3, three, jnp.where(row == 4, four, 0.0))
        x = jnp.where(row == 5, five, jnp.where(row == 6, six, x))
        return jnp.where(row < 3, points, x)

    def zeros(self, rows):
        return jnp.zeros((rows, self.shape[1]), f32)

    def source_square(self):
        w, (p0, p1, p2) = self.whole, self.part
        c0, c1, c2 = split3(self.cross)
        move = self.moved
        return [
            self.first(w, self.norm_hi, self.norm_lo, 1.0, 1.0),
            self.tile(w, move(w), 1.0, 1.0),
            self.tile(w, move(p0), 1.0, c0),
            self.tile(p1, move(p2), c1, c2),
            self.tile(p0, move(p1), None, None),
            self.tile(p0, None, None, None),
            self.zeros(16),
        ]

    def source_normal(self):
        m0, m1, m2 = self.m
        u0, u1, u2 = (pltpu.roll(x, 5, 0) for x in self.m)
        q0, q1, q2 = self.q
        return [
            self.tile(u0, m1, q0, q1),
            self.tile(u2, m0, q2, None),
            self.tile(u0, m0, None, None),
            self.tile(u1, m1, None, None),
            self.tile(u2, None, None, None),
            self.zeros(24),
        ]

    def target_square(self):
        w, part = -2.0 * self.whole, [-2.0 * p for p in self.part]
        p0, p1, p2 = part
        c0, c1, c2 = split3(self.cross + smoothing * smoothing)
        w3, p03, p13 = (pltpu.roll(x, 3, 0) for x in (w, p0, p1))
        return [
            self.first(w, 1.0, 1.0, self.norm_hi, self.norm_lo),
            self.tile(p0, p13, c0, c1),
            self.tile(p2, w3, c2, 1.0),
            self.tile(w, w3, 1.0, 1.0),
            self.tile(p0, p03, None, None),
            self.tile(p1, None, None, None),
            self.zeros(16),
        ]

    def target_normal(self):
        w, (p0, p1, p2) = self.whole, self.part
        move = self.moved
        return [
            self.tile(w, move(w), -1.0, -1.0),
            self.tile(w, move(p0), -1.0, None),
            self.tile(p1, move(p2), None, None),
            self.tile(p0, move(p1), None, None),
            self.tile(p0, None, None, None),
            self.zeros(24),
        ]


def sources(f):
    x = jnp.concatenate(f.source_square() + f.source_normal(), axis=0).T
    top = x[:64]
    left = iota(top.shape, 1) < 64
    return x.astype(bf16), jnp.where(left, top, pltpu.roll(top, 64, 1)).astype(bf16)


def point_sources(f):
    x = f.source_square()
    return jnp.concatenate(x + x, axis=0).T.astype(bf16)


def halves(x):
    left = iota(x.shape, 1) < 64
    a = jnp.where(left, x, 0.0)
    b = jnp.where(left, 0.0, x)
    return (a, pltpu.roll(a, 64, 1)), (pltpu.roll(b, 64, 1), b)


def pair_weights(square):
    return [jnp.concatenate(x, axis=0).astype(bf16) for x in halves(jnp.concatenate(square, axis=0))]


def compact(entries, first, dead):
    slots, targets = entries.shape
    place = iota(entries.shape, 0)
    out = jnp.full(entries.shape, dead, jnp.int32)
    count = jnp.zeros((1, targets), jnp.int32)
    for k in range(slots):
        e = entries[k : k + 1]
        live = e >= 0
        at = jnp.where(live, count, -1)
        out = jnp.where(place == at, e - first, out)
        count = count + jnp.where(live, 1, 0)
    return out, count


def items(near, count, dead, out_ref):
    slots, targets = near.shape
    mine = (count + 1) // 2
    before = jnp.where(iota((targets, targets), 0) < iota((targets, targets), 1), 1.0, 0.0).astype(bf16)
    start = dot(jnp.broadcast_to(mine.astype(f32), (8, targets)).astype(bf16), before)[0:1]
    total = jnp.sum(mine, axis=1, keepdims=True).astype(f32)
    table = near.astype(f32).astype(bf16)
    rows = out_ref.shape[0] - 1
    wide = iota((rows, targets), 1)
    slot = iota((rows, slots), 1)
    lane = iota((rows, 128), 1)
    out = jnp.zeros((rows, 128), f32)
    for u in range(UNROLL):
        place = (iota((rows, 1), 0) * UNROLL + u).astype(f32)
        begun = start <= place
        target = jnp.sum(jnp.where(begun, 1.0, 0.0), axis=1, keepdims=True) - 1.0
        base = jnp.max(jnp.where(begun, start, 0.0), axis=1, keepdims=True)
        pick = jnp.where(wide.astype(f32) == target, 1.0, 0.0).astype(bf16)
        lists = dot_t(pick, table)
        used = (place >= 0.0) & (place < total)
        first = 2.0 * (place - base)
        out = jnp.where(lane == u, jnp.where(used, target, float(targets)), out)
        for h in range(2):
            chosen = jnp.where(slot.astype(f32) == first + float(h), lists, 0.0)
            ids = jnp.where(used, jnp.sum(chosen, axis=1, keepdims=True), float(dead))
            out = jnp.where(lane == (h + 1) * UNROLL + u, ids, out)
    out_ref[0:rows] = out.astype(jnp.int32)
    out_ref[rows:] = jnp.broadcast_to(total, (1, 128)).astype(jnp.int32)


def list_rows(slots, leaves):
    return -(-(leaves * (slots // 2) // UNROLL + 1) // 8) * 8 + 1


def pack_kernel(target_ref, density_ref, out_ref, count_ref, slot_ref, *, peers, per):
    leaves, nrhs, leaf = density_ref.shape
    for d in range(peers):
        count_ref[d] = 0
    for k in range(leaves):
        t = target_ref[k]
        d = t // leaves
        c = count_ref[d]
        count_ref[d] = c + 1
        slot_ref[d * per + c] = t - d * leaves
        out_ref[d, pl.ds(pl.multiple_of(c * nrhs, nrhs), nrhs), :] = density_ref[k]
    row = iota((8, leaf), 0)
    for d in range(peers):
        x = jnp.zeros((8, leaf), f32)
        for c in range(per):
            x = jnp.where(row == c, slot_ref[d * per + c].astype(f32), x)
        out_ref[d, per * nrhs :, :] = x.astype(bf16)


def feature_kernel(
    node_list_ref, geo_ref, node_ref, near_ref, far_ref,
    fs_ref, fd_ref, ft_ref, wf_ref, split_ref, gn_ref, own_list_ref, halo_list_ref, far_list_ref,
    pad_ref, npad_ref, fsn_ref, wfn_ref,
):
    leaves = fs_ref.shape[0]
    nodes_here = wfn_ref.shape[0]
    slots = near_ref.shape[0]
    index = lax.axis_index(AXES)
    first = index * leaves - REACH
    wide = leaves + 2 * REACH
    pad_ref[...] = jnp.zeros(pad_ref.shape, f32)
    pad_ref[0:6, :] = geo_ref[...]
    npad_ref[...] = jnp.zeros(npad_ref.shape, f32)
    npad_ref[0:3, :] = node_ref[...]
    entries = near_ref[...]
    local = (entries >= index * leaves) & (entries < (index + 1) * leaves)
    items(*compact(jnp.where(local, entries, -1), index * leaves, leaves), leaves, own_list_ref)
    items(*compact(jnp.where(local, -1, entries), first, wide), wide, halo_list_ref)
    far, _ = compact(far_ref[...], first, wide)
    same = jnp.where(iota((leaves, leaves), 0) == iota((leaves, leaves), 1), 1.0, 0.0).astype(bf16)
    far_list_ref[:, 0:slots] = dot_t(same, far.astype(f32).astype(bf16)).astype(jnp.int32)

    def leaf_step(l, _):
        g = pad_ref[:, pl.ds(pl.multiple_of(l * 128, 128), 128)]
        f = Features(g)
        fs_ref[l], fd_ref[l] = sources(f)
        square = f.target_square()
        normal = f.target_normal()
        ft_ref[l] = jnp.concatenate(
            [
                jnp.concatenate(square + [f.zeros(64)], axis=0),
                jnp.concatenate([f.zeros(64)] + normal, axis=0),
            ],
            axis=1,
        ).astype(bf16)
        wf_ref[l] = pair_weights(square)[0]
        return 0

    lax.fori_loop(0, leaves, leaf_step, 0, unroll=4)

    def split_step(l, _):
        parts = []
        for k in range(2):
            parts += split3(pad_ref[:, pl.ds(pl.multiple_of((l * 2 + k) * 128, 128), 128)])
        split_ref[pl.ds(pl.multiple_of(l * 48, 48), 48), :] = jnp.concatenate(parts, axis=0).astype(bf16)
        return 0

    lax.fori_loop(0, leaves // 2, split_step, 0, unroll=4)

    def node_step(l, _):
        fsn_ref[l] = point_sources(Features(npad_ref[:, pl.ds(pl.multiple_of(l * 128, 128), 128)]))
        return 0

    n_nodes = 2 * fsn_ref.shape[0]
    lax.fori_loop(0, n_nodes // 2, node_step, 0, unroll=4)
    chunk = index * (nodes_here // 2)
    for l in range(nodes_here // 2):
        f = Features(npad_ref[:, pl.ds(pl.multiple_of((chunk + l) * 128, 128), 128)])
        wfn_ref[2 * l], wfn_ref[2 * l + 1] = pair_weights(f.target_square())

    node_slots = node_list_ref.shape[1]
    left = iota((64, 128), 1) < 64

    def node_field(p, _):
        x = []
        for j in range(0, node_slots, 2):
            pair = []
            for u in range(2):
                s = jnp.maximum(node_list_ref[p, j + u], 0)
                pair.append(fsn_ref[s // 2, pl.ds(pl.multiple_of((s % 2) * 64, 64), 64), :])
            x.append(jnp.where(left, pair[0], pair[1]))
        out = dot(jnp.concatenate(x, axis=0), wfn_ref[p])
        gn_ref[p] = (lax.rsqrt(out) * inv_four_pi).astype(bf16)
        return 0

    lax.fori_loop(0, nodes_here, node_field, 0)


def skeleton_kernel(
    arrived_ref, basis_ref, transfer_ref, split_ref, own_ref, a_ref, b_ref, node_ref, *, per
):
    peers = arrived_ref.shape[0]
    leaves = peers * per
    nrhs = 32
    half = leaves // 2
    for d in range(peers):
        slots = arrived_ref[d, per * nrhs :, :].astype(f32).astype(jnp.int32)
        for c in range(per):
            s = slots[c, 0]
            h = s // half
            own_ref[h, pl.ds(pl.multiple_of((s - h * half) * nrhs, nrhs), nrhs), :] = arrived_ref[
                d, c * nrhs : (c + 1) * nrhs, :
            ]
    left = iota((nrhs, 128), 1) < 64
    skels = []
    for p in range(leaves // 2):
        h, q = divmod(p, half // 2)
        out = dot_t(own_ref[h, q * 64 : (q + 1) * 64, :], basis_ref[p])
        pair = jnp.where(left, out[:nrhs], out[nrhs:]).astype(bf16)
        own_ref[h, half * nrhs + q * nrhs : half * nrhs + (q + 1) * nrhs, :] = pair
        skels.append(pair)
    base = half * nrhs + (half // 2) * nrhs
    n_split = half * 24
    for h in range(2):
        own_ref[h, base : base + n_split, :] = split_ref[h * n_split : (h + 1) * n_split, :]
    kids = transfer_ref.shape[2] // 128
    n_pairs = len(skels) // (2 * kids)
    for p in range(n_pairs):
        stack = jnp.concatenate(
            [jnp.concatenate(skels[(2 * p + h) * kids : (2 * p + h + 1) * kids], axis=1) for h in range(2)], axis=0
        )
        out = dot_t(stack, transfer_ref[p])
        pair = jnp.where(left, out[:nrhs], out[nrhs:]).astype(bf16)
        for d in range(peers):
            node_ref[d, p * nrhs : (p + 1) * nrhs, :] = pair
    odd = lax.axis_index(AXES) % 2
    a_ref[...] = own_ref[1 - odd]
    b_ref[...] = own_ref[odd]


def doubled(pairs, out_ref, k):
    rows = pairs.shape[0]
    i, j = iota((128, 256), 0), iota((128, 256), 1)
    pick = jnp.where(i == (j % 64) + 64 * (j // 128), 1.0, 0.0).astype(bf16)
    both = dot(pairs, pick).astype(bf16)
    for p in range(rows // 32):
        for h in range(2):
            out_ref[k + 2 * p + h] = both[32 * p : 32 * p + 32, 128 * h : 128 * h + 128]


def far_left(ids, skel_ref):
    left = iota((32, 128), 1) < 64
    cols = []
    for j in range(0, len(ids), 4):
        a, b, c, d = (skel_ref[s] for s in ids[j : j + 4])
        cols.append(jnp.concatenate([jnp.where(left, a, c), jnp.where(left, b, d)], axis=0))
    return jnp.concatenate(cols, axis=1)


def near_pairs(list_ref, fs_ref, ft_ref, dens_ref, k_ref, near_ref):
    def item(i, u, part):
        return list_ref[i, part * UNROLL + u]

    def matrices(i):
        for u in range(UNROLL):
            x = jnp.concatenate([fs_ref[item(i, u, 1)], fs_ref[item(i, u, 2)]], axis=0)
            out = dot(x, ft_ref[item(i, u, 0)])
            r = lax.rsqrt(out[:, :128])
            k_ref[u] = ((out[:, 128:] * r) * (r * r)).astype(bf16)

    def apply(i):
        for u in range(UNROLL):
            lhs = jnp.concatenate([dens_ref[item(i, u, 1)], dens_ref[item(i, u, 2)]], axis=1)
            near_ref[item(i, u, 0)] += dot(lhs, k_ref[u])

    def step(i, _):
        apply(i - 1)
        matrices(i)
        return 0

    steps = jnp.maximum((list_ref[list_ref.shape[0] - 1, 0] + UNROLL - 1) // UNROLL, 1)
    matrices(0)
    lax.fori_loop(1, steps, step, 0)
    apply(steps - 1)


def own_kernel(
    list_hbm, fs_hbm, ft_hbm, own_ref, near_ref, fs_ref, ft_ref, dens_ref, k_ref, list_ref, sem
):
    leaves = fs_hbm.shape[0]
    half = leaves // 2
    nrhs = 32
    copies = [
        pltpu.make_async_copy(list_hbm, list_ref, sem.at[3]),
        pltpu.make_async_copy(fs_hbm, fs_ref.at[pl.ds(0, leaves)], sem.at[0]),
        pltpu.make_async_copy(ft_hbm, ft_ref.at[pl.ds(0, leaves)], sem.at[1]),
        pltpu.make_async_copy(fs_hbm.at[0], fs_ref.at[leaves], sem.at[2]),
    ]
    for c in copies:
        c.start()
    for l in range(leaves):
        dens_ref[l] = own_ref[l // half, l % half * nrhs : (l % half + 1) * nrhs, :]
    dens_ref[leaves] = jnp.zeros((nrhs, 128), bf16)
    near_ref[...] = jnp.zeros(near_ref.shape, f32)
    for c in copies:
        c.wait()
    near_pairs(list_ref, fs_ref, ft_ref, dens_ref, k_ref, near_ref)


def leaf_kernel(
    list_hbm, far_list_hbm, node_list_hbm, fs_own_ref, fd_own_ref, ft_hbm, wf_hbm, basis_hbm, transfer_hbm,
    own_ref, a_any, b_any, first_ref, all_skel_ref, gn_ref,
    out_hbm,
    a_ref, b_ref,
    fs_ref, fd_ref, ft_ref, wf_ref, basis_ref, transfer_ref,
    dens_ref, skel_ref, all_ref, near_ref, down_ref, far_ref, out_ref, k_ref, g_ref,
    list_ref, far_list_ref, node_list_ref, sem, out_sem,
):
    leaves = wf_ref.shape[0]
    nrhs = 32
    half = leaves // 2
    wide = leaves + 2 * REACH
    odd = lax.axis_index(AXES) % 2 == 1
    slots = g_ref.shape[1] // 32
    mine = pl.ds(REACH, leaves)
    copies = [
        pltpu.make_async_copy(fd_own_ref, fd_ref.at[mine], sem.at[0]),
        pltpu.make_async_copy(ft_hbm, ft_ref.at[pl.ds(0, leaves)], sem.at[1]),
        pltpu.make_async_copy(wf_hbm, wf_ref, sem.at[2]),
        pltpu.make_async_copy(fs_own_ref.at[0], fs_ref.at[wide], sem.at[3]),
        pltpu.make_async_copy(fd_own_ref.at[0], fd_ref.at[wide], sem.at[4]),
    ]
    copies += [
        pltpu.make_async_copy(list_hbm, list_ref, sem.at[5]),
        pltpu.make_async_copy(far_list_hbm, far_list_ref, sem.at[6]),
        pltpu.make_async_copy(node_list_hbm, node_list_ref, sem.at[7]),
    ]
    later = [
        copies.pop(2),
        copies.pop(0),
        pltpu.make_async_copy(basis_hbm, basis_ref, sem.at[8]),
        pltpu.make_async_copy(transfer_hbm, transfer_ref, sem.at[9]),
    ]
    arrived = [
        pltpu.make_async_copy(a_any, a_ref, sem.at[10]),
        pltpu.make_async_copy(b_any, b_ref, sem.at[11]),
    ]
    for c in arrived + copies + later:
        c.start()
    for c in arrived:
        c.wait()

    base = half * nrhs + (half // 2) * nrhs
    for right, k in ((False, 0), (True, REACH + leaves)):

        def halo(l, _, right=right, k=k):
            at = pl.ds(pl.multiple_of(base + l * 48, 16), 48)
            x, y = a_ref[at, :].astype(f32), b_ref[at, :].astype(f32)
            x = jnp.where(odd, y, x) if right else jnp.where(odd, x, y)
            for j in range(2):
                g = x[24 * j : 24 * j + 8] + x[24 * j + 8 : 24 * j + 16] + x[24 * j + 16 : 24 * j + 24]
                fs_ref[k + 2 * l + j], fd_ref[k + 2 * l + j] = sources(Features(g))
            return 0

        lax.fori_loop(0, half // 2, halo, 0, unroll=2)

    def fill(view, k, dens=True):
        if dens:
            for l in range(half):
                dens_ref[k + l] = view(l * nrhs, nrhs)
        doubled(view(half * nrhs, half // 2 * nrhs), skel_ref, k)

    fill(lambda at, n: jnp.where(odd, a_ref[at : at + n, :], b_ref[at : at + n, :]), 0)
    fill(lambda at, n: own_ref[0, at : at + n, :], REACH, False)
    fill(lambda at, n: own_ref[1, at : at + n, :], REACH + half, False)
    fill(lambda at, n: jnp.where(odd, b_ref[at : at + n, :], a_ref[at : at + n, :]), REACH + leaves)
    dens_ref[wide] = jnp.zeros((nrhs, 128), bf16)
    skel_ref[wide] = jnp.zeros((nrhs, 128), bf16)
    near_ref[...] = first_ref[...]
    pairs = all_skel_ref.shape[0] // nrhs
    doubled(all_skel_ref[...], all_ref, 0)
    all_ref[2 * pairs] = jnp.zeros((nrhs, 128), bf16)
    for c in copies:
        c.wait()
    near_pairs(list_ref, fs_ref, ft_ref, dens_ref, k_ref, near_ref)
    for c in later:
        c.wait()

    kids = transfer_ref.shape[2] // 128
    for p in range(gn_ref.shape[0]):
        ids = []
        for j in range(node_list_ref.shape[1]):
            e = node_list_ref[p, j]
            ids.append(jnp.where(e < 0, 2 * pairs, e))
        acc = dot(far_left(ids, all_ref), gn_ref[p])
        x = acc[:nrhs] + pltpu.roll(acc[nrhs:], 64, 1)
        down = dot(x[:, :64].astype(bf16), transfer_ref[p])
        for c in range(kids):
            down_ref[p * kids + c] = down[:, c * 128 : (c + 1) * 128]

    left = iota((nrhs, 128), 1) < 64
    left64 = iota((64, 128), 1) < 64

    def far_ids(t):
        return [far_list_ref[t, u] for u in range(slots)]

    def far_matrices(p):
        for h in range(FAR_UNROLL):
            ids = far_ids(FAR_UNROLL * p + h)
            x = [
                jnp.where(left64, fd_ref[ids[j]], fd_ref[ids[j + 1]]) for j in range(0, slots, 2)
            ]
            out = dot(jnp.concatenate(x, axis=0), wf_ref[FAR_UNROLL * p + h])
            g_ref[h] = (lax.rsqrt(out) * inv_four_pi).astype(bf16)

    def far_apply(p):
        for h in range(0, FAR_UNROLL, 2):
            t = FAR_UNROLL * p + h
            e, o = (dot(far_left(far_ids(t + k), skel_ref), g_ref[h + k]) for k in range(2))
            even = e[:nrhs] + pltpu.roll(e[nrhs:], 64, 1)
            odd_ = pltpu.roll(o[:nrhs], 64, 1) + o[nrhs:]
            far_ref[(FAR_UNROLL // 2) * p + h // 2] = jnp.where(left, even, odd_)

    def finish(p):
        for q in range(FAR_UNROLL // 2 * p, FAR_UNROLL // 2 * (p + 1)):
            local = (far_ref[q] + down_ref[q]).astype(bf16).astype(f32)
            both = jnp.concatenate(
                [jnp.where(left, local, 0.0), jnp.where(left, 0.0, local)], axis=0
            ).astype(bf16)
            y = dot(both, basis_ref[q])
            out_ref[2 * q] = (near_ref[2 * q] + y[:nrhs]).astype(bf16)
            out_ref[2 * q + 1] = (near_ref[2 * q + 1] + y[nrhs:]).astype(bf16)
        here = pl.ds(p * FAR_UNROLL, FAR_UNROLL)
        written = pltpu.make_async_copy(out_ref.at[here], out_hbm.at[here], out_sem.at[p])
        written.start()
        return written

    far_steps = leaves // FAR_UNROLL
    written = []
    for p in range(far_steps + 2):
        if p >= 2:
            written.append(finish(p - 2))
        if 1 <= p <= far_steps:
            far_apply(p - 1)
        if p < far_steps:
            far_matrices(p)
    for c in written:
        c.wait()


def vmem():
    return pl.BlockSpec(memory_space=pltpu.VMEM)


def smem():
    return pl.BlockSpec(memory_space=pltpu.SMEM)


def call(kernel, out, in_specs, scratch, name, flops, vmem_mib, out_specs=None):
    many = isinstance(out, tuple)
    if out_specs is None:
        out_specs = tuple(vmem() for _ in out) if many else vmem()
    return pl.pallas_call(
        kernel,
        out_shape=out,
        in_specs=in_specs,
        out_specs=out_specs,
        scratch_shapes=scratch,
        name=name,
        cost_estimate=pl.CostEstimate(flops=flops, bytes_accessed=1 << 20, transcendentals=0),
        compiler_params=pltpu.CompilerParams(vmem_limit_bytes=vmem_mib << 20),
    )


def pack(peers, per, density, leaf_target):
    leaves, nrhs, leaf = density.shape
    return call(
        lambda *r: pack_kernel(*r, peers=peers, per=per),
        jax.ShapeDtypeStruct((peers, per * nrhs + 8, leaf), bf16),
        [smem(), vmem()],
        [pltpu.SMEM((peers,), jnp.int32), pltpu.SMEM((leaves,), jnp.int32)],
        "pack",
        1 << 20,
        2,
    )(hbm(leaf_target), hbm(density))


def features(node_list, geometry, node_points, near_list, far_list):
    leaves, slots = near_list.shape
    nodes = node_points.shape[1] // 64
    nodes_here, node_slots = node_list.shape
    shape = jax.ShapeDtypeStruct
    return call(
        feature_kernel,
        (
            pltpu.HBM((leaves, 128, 128), bf16),
            pltpu.HBM((leaves, 64, 128), bf16),
            pltpu.HBM((leaves, 128, 256), bf16),
            pltpu.HBM((leaves, 128, 128), bf16),
            pltpu.VMEM((leaves * 24, 128), bf16),
            pltpu.VMEM((nodes_here, node_slots * 32, 128), bf16),
            pltpu.HBM((list_rows(slots, leaves), 128), jnp.int32),
            pltpu.HBM((list_rows(slots, leaves), 128), jnp.int32),
            pltpu.HBM((leaves, 128), jnp.int32),
        ),
        [smem()] + [vmem()] * 4,
        [
            pltpu.VMEM((8, leaves * 128), f32),
            pltpu.VMEM((8, nodes * 64), f32),
            pltpu.VMEM((nodes // 2, 128, 128), bf16),
            pltpu.VMEM((nodes_here, 128, 128), bf16),
        ],
        "features",
        1 << 30,
        14,
    )(hbm(node_list), hbm(geometry), hbm(node_points), hbm(near_list.T), hbm(far_list.T))


def skeletons(arrived, basis_in, transfer, split, per):
    peers = arrived.shape[0]
    leaves = peers * per
    nodes_here = transfer.shape[0]
    rows = leaves // 2 * 32 + leaves // 4 * 32 + leaves // 2 * 24
    shape = jax.ShapeDtypeStruct
    return call(
        lambda *r: skeleton_kernel(*r, per=per),
        (
            pltpu.VMEM((2, rows, 128), bf16),
            pltpu.HBM((rows, 128), bf16),
            pltpu.HBM((rows, 128), bf16),
            shape((peers, nodes_here // 2 * 32, 128), bf16),
        ),
        [vmem()] * 4,
        [],
        "skeleton",
        1 << 26,
        6,
    )(
        arrived,
        basis_in.reshape(leaves // 2, 128, -1),
        transfer.reshape(nodes_here // 2, 128, -1),
        split,
    )


def own_fields(own_list, fs, ft, own):
    leaves = ft.shape[0]
    anywhere = pl.BlockSpec(memory_space=pl.ANY)
    return call(
        own_kernel,
        pltpu.VMEM((leaves + 1, 32, 128), f32),
        [anywhere] * 3 + [vmem()],
        [
            pltpu.VMEM((leaves + 1, 128, 128), bf16),
            pltpu.VMEM((leaves + 1, 128, 256), bf16),
            pltpu.VMEM((leaves + 1, 32, 128), bf16),
            pltpu.VMEM((UNROLL, 256, 128), bf16),
            pltpu.SMEM(own_list.shape, jnp.int32),
            pltpu.SemaphoreType.DMA((4,)),
        ],
        "own",
        1 << 31,
        12,
    )(hbm(own_list), hbm(fs), hbm(ft), own)


def leaf_fields(
    far_slots, halo_list, far_list, node_list, fs, fd, ft, wf, basis_out, transfer, own, got_a, got_b, first, all_skel, gn
):
    leaves = ft.shape[0]
    wide = leaves + 2 * REACH
    nodes = all_skel.shape[0] // 16
    anywhere = pl.BlockSpec(memory_space=pl.ANY)
    basis_out = basis_out.reshape(leaves // 2, 128, -1)
    return call(
        leaf_kernel,
        jax.ShapeDtypeStruct((leaves, 32, 128), bf16),
        [anywhere] * 9 + [vmem()] + [anywhere] * 2 + [vmem()] * 3,
        [
            pltpu.VMEM(got_a.shape, bf16),
            pltpu.VMEM(got_a.shape, bf16),
            pltpu.VMEM((wide + 1, 128, 128), bf16),
            pltpu.VMEM((wide + 1, 64, 128), bf16),
            pltpu.VMEM((leaves + 1, 128, 256), bf16),
            pltpu.VMEM((leaves, 128, 128), bf16),
            pltpu.VMEM(basis_out.shape, bf16),
            pltpu.VMEM(transfer.shape, bf16),
            pltpu.VMEM((wide + 1, 32, 128), bf16),
            pltpu.VMEM((wide + 1, 32, 128), bf16),
            pltpu.VMEM((nodes + 1, 32, 128), bf16),
            pltpu.VMEM((leaves + 1, 32, 128), f32),
            pltpu.VMEM((leaves // 2, 32, 128), f32),
            pltpu.VMEM((leaves // 2, 32, 128), f32),
            pltpu.VMEM((leaves, 32, 128), bf16),
            pltpu.VMEM((UNROLL, 256, 128), bf16),
            pltpu.VMEM((FAR_UNROLL, gn.shape[1] // node_list.shape[1] * far_slots, 128), bf16),
            pltpu.SMEM(halo_list.shape, jnp.int32),
            pltpu.SMEM(far_list.shape, jnp.int32),
            pltpu.SMEM(node_list.shape, jnp.int32),
            pltpu.SemaphoreType.DMA((12,)),
            pltpu.SemaphoreType.DMA((leaves // FAR_UNROLL,)),
        ],
        "leaves",
        1 << 31,
        24,
        anywhere,
    )(
        *map(hbm, (halo_list, far_list, node_list, fs, fd, ft, wf, basis_out, transfer)),
        own, got_a, got_b, first, all_skel, gn,
    )


def hbm(x):
    return pltpu.with_memory_space_constraint(x, pltpu.HBM)


def on_device(
    density, leaf_target, geometry, near_list, far_list, node_list, basis_in, basis_out, transfer, node_points
):
    peers = lax.axis_size(AXES)
    per = density.shape[0] // peers
    outgoing = pack(peers, per, density, leaf_target)
    arrived = lax.all_to_all(outgoing, AXES, split_axis=0, concat_axis=0, tiled=True)
    fs, fd, ft, wf, split, gn, own_pairs, halo_pairs, far_rows = features(node_list, geometry, node_points, near_list, far_list)
    own, to_a, to_b, node_out = skeletons(arrived, basis_in, transfer, split, per)
    all_skel = lax.all_to_all(node_out, AXES, split_axis=0, concat_axis=0, tiled=True)
    swap_a = [(i, i ^ 1) for i in range(peers)]
    swap_b = [(i, i + 1) for i in range(1, peers - 1, 2)] + [(i + 1, i) for i in range(1, peers - 1, 2)]
    got_a = lax.ppermute(to_a, AXES, swap_a)
    got_b = lax.ppermute(to_b, AXES, swap_b)
    first = own_fields(own_pairs, fs, ft, own)
    return leaf_fields(
        far_list.shape[1], halo_pairs, far_rows, node_list, fs, fd, ft, wf, basis_out, transfer, own, got_a, got_b,
        first, all_skel.reshape(-1, 128), gn,
    )


def solution(mesh):
    split = ("grp", "row", "col")
    return jax.shard_map(
        on_device,
        mesh=mesh,
        in_specs=(
            P(split, None, None),
            P(split),
            P(None, split),
            P(split, None),
            P(split, None),
            P(split, None),
            P(split, None, None),
            P(split, None, None),
            P(split, None, None),
            P(None, "grp"),
        ),
        out_specs=P(split, None, None),
        check_vma=False,
    )
```

```python
import math

import jax
import jax.numpy as jnp
from jax import lax
from jax.experimental import pallas as pl
from jax.experimental.pallas import tpu as pltpu
from jax.sharding import PartitionSpec as P


REACH = 16
AXES = ("row", "col")

smoothing = 0.1
inv_four_pi = 0.25 / math.pi
grid_step = 16.0
UNROLL = 12
AHEAD = 2
FAR_UNROLL = 8
bf16 = jnp.bfloat16
f32 = jnp.float32


def split3(x):
    first = x.astype(bf16).astype(f32)
    rest = x - first
    second = rest.astype(bf16).astype(f32)
    third = (rest - second).astype(bf16).astype(f32)
    return first, second, third


def iota(shape, axis):
    return lax.broadcasted_iota(jnp.int32, shape, axis)


def dot(a, b):
    return lax.dot_general(a, b, (((1,), (0,)), ((), ())), preferred_element_type=f32)


def dot_t(a, b):
    return lax.dot_general(a, b, (((1,), (1,)), ((), ())), preferred_element_type=f32)


class Features:
    def __init__(self, g):
        self.shape = g.shape
        self.row = row = iota(g.shape, 0)
        point = row < 3
        c = jnp.where(point, g, 0.0)
        self.whole = whole = jnp.floor(c * grid_step + 0.5) * (1.0 / grid_step)
        part = c - whole
        self.part = split3(part)
        m = jnp.where(point, 0.0, g) * inv_four_pi
        self.m = split3(m)
        norm = jnp.sum(whole * whole, axis=0, keepdims=True)
        self.norm_hi = jnp.floor(norm)
        self.norm_lo = norm - self.norm_hi
        self.cross = jnp.sum(part * (2.0 * whole + part), axis=0, keepdims=True)
        self.q = split3(jnp.sum(m * pltpu.roll(c, 3, 0), axis=0, keepdims=True))
        self.low = {}

    def moved(self, x):
        if id(x) not in self.low:
            self.low[id(x)] = pltpu.roll(x, 3, 0)
        return self.low[id(x)]

    def tile(self, upper, lower, six, seven):
        row = self.row
        x = jnp.where(row < 3, upper, 0.0)
        if lower is not None:
            x = jnp.where(row < 3, upper, jnp.where(row < 6, lower, 0.0))
        if six is not None:
            x = jnp.where(row == 6, six, x)
        if seven is not None:
            x = jnp.where(row == 7, seven, x)
        return x

    def first(self, points, three, four, five, six):
        row = self.row
        x = jnp.where(row == 3, three, jnp.where(row == 4, four, 0.0))
        x = jnp.where(row == 5, five, jnp.where(row == 6, six, x))
        return jnp.where(row < 3, points, x)

    def zeros(self, rows):
        return jnp.zeros((rows, self.shape[1]), f32)

    def source_square(self):
        w, (p0, p1, p2) = self.whole, self.part
        c0, c1, c2 = split3(self.cross)
        move = self.moved
        return [
            self.first(w, self.norm_hi, self.norm_lo, 1.0, 1.0),
            self.tile(w, move(w), 1.0, 1.0),
            self.tile(w, move(p0), 1.0, c0),
            self.tile(p1, move(p2), c1, c2),
            self.tile(p0, move(p1), None, None),
            self.tile(p0, None, None, None),
            self.zeros(16),
        ]

    def source_normal(self):
        m0, m1, _ = self.m
        u0, u1, u2 = (pltpu.roll(x, 5, 0) for x in self.m)
        q0, q1, q2 = self.q
        return [
            self.tile(u0, m1, q0, q1),
            self.tile(u2, m0, q2, None),
            self.tile(u0, m0, None, None),
            self.tile(u1, m1, None, None),
            self.tile(u2, None, None, None),
            self.zeros(24),
        ]

    def target_square(self):
        w, part = -2.0 * self.whole, [-2.0 * p for p in self.part]
        p0, p1, p2 = part
        c0, c1, c2 = split3(self.cross + smoothing * smoothing)
        w3, p03, p13 = (pltpu.roll(x, 3, 0) for x in (w, p0, p1))
        return [
            self.first(w, 1.0, 1.0, self.norm_hi, self.norm_lo),
            self.tile(p0, p13, c0, c1),
            self.tile(p2, w3, c2, 1.0),
            self.tile(w, w3, 1.0, 1.0),
            self.tile(p0, p03, None, None),
            self.tile(p1, None, None, None),
            self.zeros(16),
        ]

    def target_normal(self):
        w, (p0, p1, p2) = self.whole, self.part
        move = self.moved
        return [
            self.tile(w, move(w), -1.0, -1.0),
            self.tile(w, move(p0), -1.0, None),
            self.tile(p1, move(p2), None, None),
            self.tile(p0, move(p1), None, None),
            self.tile(p0, None, None, None),
            self.zeros(24),
        ]


def sources(f):
    x = jnp.concatenate(f.source_square() + f.source_normal(), axis=0).T
    top = x[:64]
    left = iota(top.shape, 1) < 64
    return x.astype(bf16), jnp.where(left, top, pltpu.roll(top, 64, 1)).astype(bf16)


def point_sources(f):
    x = f.source_square()
    return jnp.concatenate(x + x, axis=0).T.astype(bf16)


def halves(x):
    left = iota(x.shape, 1) < 64
    a = jnp.where(left, x, 0.0)
    b = jnp.where(left, 0.0, x)
    return (a, pltpu.roll(a, 64, 1)), (pltpu.roll(b, 64, 1), b)


def pair_weights(square):
    return [jnp.concatenate(x, axis=0).astype(bf16) for x in halves(jnp.concatenate(square, axis=0))]


def compact(entries, first, dead):
    slots, targets = entries.shape
    place = iota(entries.shape, 0)
    out = jnp.full(entries.shape, dead, jnp.int32)
    count = jnp.zeros((1, targets), jnp.int32)
    for k in range(slots):
        e = entries[k : k + 1]
        live = e >= 0
        at = jnp.where(live, count, -1)
        out = jnp.where(place == at, e - first, out)
        count = count + jnp.where(live, 1, 0)
    return out, count


def items(near, count, dead, out_ref):
    slots, targets = near.shape
    mine = (count + 1) // 2
    before = jnp.where(iota((targets, targets), 0) < iota((targets, targets), 1), 1.0, 0.0).astype(bf16)
    start = dot(jnp.broadcast_to(mine.astype(f32), (8, targets)).astype(bf16), before)[0:1]
    total = jnp.sum(mine, axis=1, keepdims=True).astype(f32)
    table = near.astype(f32).astype(bf16)
    rows = out_ref.shape[0] - 1
    wide = iota((rows, targets), 1)
    slot = iota((rows, slots), 1)
    lane = iota((rows, 128), 1)
    out = jnp.zeros((rows, 128), f32)
    for u in range(UNROLL):
        place = (iota((rows, 1), 0) * UNROLL + u).astype(f32)
        begun = start <= place
        target = jnp.sum(jnp.where(begun, 1.0, 0.0), axis=1, keepdims=True) - 1.0
        base = jnp.max(jnp.where(begun, start, 0.0), axis=1, keepdims=True)
        pick = jnp.where(wide.astype(f32) == target, 1.0, 0.0).astype(bf16)
        lists = dot_t(pick, table)
        used = (place >= 0.0) & (place < total)
        first = 2.0 * (place - base)
        out = jnp.where(lane == u, jnp.where(used, target, float(targets)), out)
        for h in range(2):
            chosen = jnp.where(slot.astype(f32) == first + float(h), lists, 0.0)
            ids = jnp.where(used, jnp.sum(chosen, axis=1, keepdims=True), float(dead))
            out = jnp.where(lane == (h + 1) * UNROLL + u, ids, out)
    out_ref[0:rows] = out.astype(jnp.int32)
    out_ref[rows:] = jnp.broadcast_to(total, (1, 128)).astype(jnp.int32)


def list_rows(slots, leaves):
    return -(-(leaves * (slots // 2) // UNROLL + 1) // 8) * 8 + 1


def pack_kernel(target_ref, density_ref, out_ref, count_ref, slot_ref, *, peers, per):
    leaves, nrhs, leaf = density_ref.shape
    for d in range(peers):
        count_ref[d] = 0
    for k in range(leaves):
        t = target_ref[k]
        d = lax.div(t, leaves)
        c = count_ref[d]
        count_ref[d] = c + 1
        slot_ref[d * per + c] = t - d * leaves
        out_ref[d, pl.ds(pl.multiple_of(c * nrhs, nrhs), nrhs), :] = density_ref[k]
    row = iota((8, leaf), 0)
    for d in range(peers):
        x = jnp.zeros((8, leaf), f32)
        for c in range(per):
            x = jnp.where(row == c, slot_ref[d * per + c].astype(f32), x)
        out_ref[d, per * nrhs :, :] = x.astype(bf16)


def feature_kernel(
    node_list_ref, geo_ref, node_ref, near_ref, far_ref,
    fs_ref, fd_ref, ft_ref, wf_ref, split_ref, gn_ref, own_list_ref, halo_list_ref, far_list_ref, ready_ref,
    pad_ref, npad_ref, fsn_ref, wfn_ref, rows_ref, sem,
):
    leaves = fd_ref.shape[0]
    nodes_here = wfn_ref.shape[0]
    slots = near_ref.shape[0]
    index = lax.axis_index(AXES)
    first = index * leaves - REACH
    wide = leaves + 2 * REACH
    pad_ref[...] = jnp.zeros(pad_ref.shape, f32)
    pad_ref[0:6, :] = geo_ref[...]
    npad_ref[...] = jnp.zeros(npad_ref.shape, f32)
    npad_ref[0:3, :] = node_ref[...]
    entries = near_ref[...]
    local = (entries >= index * leaves) & (entries < (index + 1) * leaves)
    items(*compact(jnp.where(local, entries, -1), index * leaves, leaves), leaves, own_list_ref)
    listed = pltpu.make_async_copy(own_list_ref, rows_ref, sem.at[0])
    listed.start()
    items(*compact(jnp.where(local, -1, entries), first, wide), wide, halo_list_ref)
    far, _ = compact(far_ref[...], first, wide)
    same = jnp.where(iota((leaves, leaves), 0) == iota((leaves, leaves), 1), 1.0, 0.0).astype(bf16)
    far_list_ref[:, 0:slots] = dot_t(same, far.astype(f32).astype(bf16)).astype(jnp.int32)

    def leaf_step(l, _):
        g = pad_ref[:, pl.ds(pl.multiple_of(l * 128, 128), 128)]
        f = Features(g)
        fs_ref[l], fd_ref[l] = sources(f)
        square = f.target_square()
        normal = f.target_normal()
        ft_ref[l] = jnp.concatenate(
            [
                jnp.concatenate(square + [f.zeros(64)], axis=0),
                jnp.concatenate([f.zeros(64)] + normal, axis=0),
            ],
            axis=1,
        ).astype(bf16)
        wf_ref[l] = pair_weights(square)[0]
        return 0

    lax.fori_loop(0, leaves, leaf_step, 0, unroll=4)
    fs_ref[leaves] = fs_ref[0]
    ft_ref[leaves] = ft_ref[0]

    def split_step(l, _):
        parts = []
        for k in range(2):
            parts += split3(pad_ref[:, pl.ds(pl.multiple_of((l * 2 + k) * 128, 128), 128)])
        split_ref[pl.ds(pl.multiple_of(l * 48, 48), 48), :] = jnp.concatenate(parts, axis=0).astype(bf16)
        return 0

    lax.fori_loop(0, leaves // 2, split_step, 0, unroll=4)

    def node_step(l, _):
        fsn_ref[l] = point_sources(Features(npad_ref[:, pl.ds(pl.multiple_of(l * 128, 128), 128)]))
        return 0

    n_nodes = 2 * fsn_ref.shape[0]
    lax.fori_loop(0, n_nodes // 2, node_step, 0, unroll=4)
    chunk = index * (nodes_here // 2)
    for l in range(nodes_here // 2):
        f = Features(npad_ref[:, pl.ds(pl.multiple_of((chunk + l) * 128, 128), 128)])
        wfn_ref[2 * l], wfn_ref[2 * l + 1] = pair_weights(f.target_square())

    node_slots = node_list_ref.shape[1]
    left = iota((64, 128), 1) < 64

    def node_field(p, _):
        x = []
        for j in range(0, node_slots, 2):
            pair = []
            for u in range(2):
                s = jnp.maximum(node_list_ref[p, j + u], 0)
                pair.append(fsn_ref[s // 2, pl.ds(pl.multiple_of((s % 2) * 64, 64), 64), :])
            x.append(jnp.where(left, pair[0], pair[1]))
        out = dot(jnp.concatenate(x, axis=0), wfn_ref[p])
        gn_ref[p] = (lax.rsqrt(out) * inv_four_pi).astype(bf16)
        return 0

    lax.fori_loop(0, nodes_here, node_field, 0)
    listed.wait()
    for i in range(AHEAD):
        pair_matrices(rows_ref, i, fs_ref, ft_ref, ready_ref, i * UNROLL)


def skeleton_kernel(
    arrived_ref, basis_ref, transfer_ref, split_ref, own_ref, a_ref, b_ref, node_ref, *, per
):
    peers = arrived_ref.shape[0]
    leaves = peers * per
    nrhs = 32
    half = leaves // 2
    for d in range(peers):
        slots = arrived_ref[d, per * nrhs :, :].astype(f32).astype(jnp.int32)
        for c in range(per):
            s = slots[c, 0]
            h = s // half
            own_ref[h, pl.ds(pl.multiple_of((s - h * half) * nrhs, nrhs), nrhs), :] = arrived_ref[
                d, c * nrhs : (c + 1) * nrhs, :
            ]
    left = iota((nrhs, 128), 1) < 64
    skels = []
    for p in range(leaves // 2):
        h, q = divmod(p, half // 2)
        out = dot_t(own_ref[h, q * 64 : (q + 1) * 64, :], basis_ref[p])
        pair = jnp.where(left, out[:nrhs], out[nrhs:]).astype(bf16)
        own_ref[h, half * nrhs + q * nrhs : half * nrhs + (q + 1) * nrhs, :] = pair
        skels.append(pair)
    base = half * nrhs + (half // 2) * nrhs
    n_split = half * 24
    for h in range(2):
        own_ref[h, base : base + n_split, :] = split_ref[h * n_split : (h + 1) * n_split, :]
    kids = transfer_ref.shape[2] // 128
    n_pairs = len(skels) // (2 * kids)
    for p in range(n_pairs):
        stack = jnp.concatenate(
            [jnp.concatenate(skels[(2 * p + h) * kids : (2 * p + h + 1) * kids], axis=1) for h in range(2)], axis=0
        )
        out = dot_t(stack, transfer_ref[p])
        pair = jnp.where(left, out[:nrhs], out[nrhs:]).astype(bf16)
        for d in range(peers):
            node_ref[d, p * nrhs : (p + 1) * nrhs, :] = pair
    odd = lax.axis_index(AXES) % 2
    a_ref[...] = own_ref[1 - odd]
    b_ref[...] = own_ref[odd]


def doubled(pairs, out_ref, k):
    rows = pairs.shape[0]
    i, j = iota((128, 256), 0), iota((128, 256), 1)
    pick = jnp.where(i == (j % 64) + 64 * (j // 128), 1.0, 0.0).astype(bf16)
    both = dot(pairs, pick).astype(bf16)
    for p in range(rows // 32):
        for h in range(2):
            out_ref[k + 2 * p + h] = both[32 * p : 32 * p + 32, 128 * h : 128 * h + 128]


def far_left(ids, skel_ref):
    left = iota((32, 128), 1) < 64
    cols = []
    for j in range(0, len(ids), 4):
        a, b, c, d = (skel_ref[s] for s in ids[j : j + 4])
        cols.append(jnp.concatenate([jnp.where(left, a, c), jnp.where(left, b, d)], axis=0))
    return jnp.concatenate(cols, axis=1)


def pair_matrices(list_ref, i, fs_ref, ft_ref, k_ref, at=0):
    for u in range(UNROLL):
        x = jnp.concatenate([fs_ref[list_ref[i, (h + 1) * UNROLL + u]] for h in range(2)], axis=0)
        out = dot(x, ft_ref[list_ref[i, u]])
        r = lax.rsqrt(out[:, :128])
        k_ref[at + u] = ((out[:, 128:] * r) * (r * r)).astype(bf16)


def pair_apply(list_ref, i, dens_ref, k_ref, near_ref, at=0):
    for u in range(UNROLL):
        lhs = jnp.concatenate([dens_ref[list_ref[i, (h + 1) * UNROLL + u]] for h in range(2)], axis=1)
        near_ref[list_ref[i, u]] += dot(lhs, k_ref[at + u])


def near_pairs(list_ref, fs_ref, ft_ref, dens_ref, k_ref, near_ref, start=0):
    def step(i, _):
        pair_apply(list_ref, i - 1, dens_ref, k_ref, near_ref)
        pair_matrices(list_ref, i, fs_ref, ft_ref, k_ref)
        return 0

    steps = (list_ref[list_ref.shape[0] - 1, 0] + UNROLL - 1) // UNROLL
    steps = jnp.maximum(steps, start + 1)
    pair_matrices(list_ref, start, fs_ref, ft_ref, k_ref)
    lax.fori_loop(start + 1, steps, step, 0)
    pair_apply(list_ref, steps - 1, dens_ref, k_ref, near_ref)


def own_kernel(
    list_hbm, fs_hbm, ft_hbm, ready_hbm, own_ref,
    near_ref,
    fs_ref, ft_ref, ready_ref, dens_ref, k_ref, list_ref, sem,
):
    leaves = fs_hbm.shape[0] - 1
    half = leaves // 2
    nrhs = 32
    copies = [
        pltpu.make_async_copy(list_hbm, list_ref, sem.at[0]),
        pltpu.make_async_copy(ready_hbm, ready_ref, sem.at[3]),
        pltpu.make_async_copy(fs_hbm, fs_ref, sem.at[1]),
        pltpu.make_async_copy(ft_hbm, ft_ref, sem.at[2]),
    ]
    for c in copies:
        c.start()
    for l in range(leaves):
        dens_ref[l] = own_ref[l // half, l % half * nrhs : (l % half + 1) * nrhs, :]
    dens_ref[leaves] = jnp.zeros((nrhs, 128), bf16)
    near_ref[...] = jnp.zeros(near_ref.shape, f32)
    for c in copies[:2]:
        c.wait()
    for i in range(AHEAD):
        pair_apply(list_ref, i, dens_ref, ready_ref, near_ref, i * UNROLL)
    for c in copies[2:]:
        c.wait()
    near_pairs(list_ref, fs_ref, ft_ref, dens_ref, k_ref, near_ref, AHEAD)


def leaf_kernel(
    list_hbm, far_list_hbm, node_list_hbm, fs_own_ref, fd_own_ref, ft_hbm, wf_hbm, basis_hbm, transfer_hbm,
    own_ref, a_any, b_any, first_ref, all_skel_ref, gn_ref,
    out_hbm,
    a_ref, b_ref,
    fs_ref, fd_ref, ft_ref, wf_ref, basis_ref, transfer_ref,
    dens_ref, skel_ref, all_ref, near_ref, down_ref, far_ref, out_ref, k_ref, g_ref,
    list_ref, far_list_ref, node_list_ref, sem, out_sem,
):
    leaves = wf_ref.shape[0]
    nrhs = 32
    half = leaves // 2
    wide = leaves + 2 * REACH
    odd = lax.axis_index(AXES) % 2 == 1
    slots = g_ref.shape[1] // 32
    mine = pl.ds(REACH, leaves)
    copies = [
        pltpu.make_async_copy(fd_own_ref, fd_ref.at[mine], sem.at[0]),
        pltpu.make_async_copy(ft_hbm, ft_ref, sem.at[1]),
        pltpu.make_async_copy(wf_hbm, wf_ref, sem.at[2]),
        pltpu.make_async_copy(fs_own_ref.at[0], fs_ref.at[wide], sem.at[3]),
        pltpu.make_async_copy(fd_own_ref.at[0], fd_ref.at[wide], sem.at[4]),
    ]
    copies += [
        pltpu.make_async_copy(list_hbm, list_ref, sem.at[5]),
        pltpu.make_async_copy(far_list_hbm, far_list_ref, sem.at[6]),
        pltpu.make_async_copy(node_list_hbm, node_list_ref, sem.at[7]),
    ]
    later = [
        copies.pop(2),
        copies.pop(0),
        pltpu.make_async_copy(basis_hbm, basis_ref, sem.at[8]),
        pltpu.make_async_copy(transfer_hbm, transfer_ref, sem.at[9]),
    ]
    arrived = [
        pltpu.make_async_copy(a_any, a_ref, sem.at[10]),
        pltpu.make_async_copy(b_any, b_ref, sem.at[11]),
    ]
    for c in arrived + copies + later:
        c.start()
    for c in arrived:
        c.wait()

    base = half * nrhs + (half // 2) * nrhs
    for right, k in ((False, 0), (True, REACH + leaves)):

        def halo(l, _, right=right, k=k):
            at = pl.ds(pl.multiple_of(base + l * 48, 16), 48)
            x, y = a_ref[at, :].astype(f32), b_ref[at, :].astype(f32)
            x = jnp.where(odd, y, x) if right else jnp.where(odd, x, y)
            for j in range(2):
                g = x[24 * j : 24 * j + 8] + x[24 * j + 8 : 24 * j + 16] + x[24 * j + 16 : 24 * j + 24]
                fs_ref[k + 2 * l + j], fd_ref[k + 2 * l + j] = sources(Features(g))
            return 0

        lax.fori_loop(0, half // 2, halo, 0, unroll=2)

    def fill(view, k, dens=True):
        if dens:
            for l in range(half):
                dens_ref[k + l] = view(l * nrhs, nrhs)
        doubled(view(half * nrhs, half // 2 * nrhs), skel_ref, k)

    fill(lambda at, n: jnp.where(odd, a_ref[at : at + n, :], b_ref[at : at + n, :]), 0)
    fill(lambda at, n: own_ref[0, at : at + n, :], REACH, False)
    fill(lambda at, n: own_ref[1, at : at + n, :], REACH + half, False)
    fill(lambda at, n: jnp.where(odd, b_ref[at : at + n, :], a_ref[at : at + n, :]), REACH + leaves)
    dens_ref[wide] = jnp.zeros((nrhs, 128), bf16)
    skel_ref[wide] = jnp.zeros((nrhs, 128), bf16)
    near_ref[...] = first_ref[...]
    pairs = all_skel_ref.shape[0] // nrhs
    doubled(all_skel_ref[...], all_ref, 0)
    all_ref[2 * pairs] = jnp.zeros((nrhs, 128), bf16)
    for c in copies:
        c.wait()
    near_pairs(list_ref, fs_ref, ft_ref, dens_ref, k_ref, near_ref)
    for c in later:
        c.wait()

    kids = transfer_ref.shape[2] // 128
    for p in range(gn_ref.shape[0]):
        ids = []
        for j in range(node_list_ref.shape[1]):
            e = node_list_ref[p, j]
            ids.append(jnp.where(e < 0, 2 * pairs, e))
        acc = dot(far_left(ids, all_ref), gn_ref[p])
        x = acc[:nrhs] + pltpu.roll(acc[nrhs:], 64, 1)
        down = dot(x[:, :64].astype(bf16), transfer_ref[p])
        for c in range(kids):
            down_ref[p * kids + c] = down[:, c * 128 : (c + 1) * 128]

    left = iota((nrhs, 128), 1) < 64
    left64 = iota((64, 128), 1) < 64

    def far_ids(t):
        return [far_list_ref[t, u] for u in range(slots)]

    def far_matrices(p):
        for h in range(FAR_UNROLL):
            ids = far_ids(FAR_UNROLL * p + h)
            x = [
                jnp.where(left64, fd_ref[ids[j]], fd_ref[ids[j + 1]]) for j in range(0, slots, 2)
            ]
            out = dot(jnp.concatenate(x, axis=0), wf_ref[FAR_UNROLL * p + h])
            g_ref[h] = (lax.rsqrt(out) * inv_four_pi).astype(bf16)

    def far_apply(p):
        for h in range(0, FAR_UNROLL, 2):
            t = FAR_UNROLL * p + h
            e, o = (dot(far_left(far_ids(t + k), skel_ref), g_ref[h + k]) for k in range(2))
            even = e[:nrhs] + pltpu.roll(e[nrhs:], 64, 1)
            odd_ = pltpu.roll(o[:nrhs], 64, 1) + o[nrhs:]
            far_ref[(FAR_UNROLL // 2) * p + h // 2] = jnp.where(left, even, odd_)

    def finish(p):
        for q in range(FAR_UNROLL // 2 * p, FAR_UNROLL // 2 * (p + 1)):
            local = (far_ref[q] + down_ref[q]).astype(bf16).astype(f32)
            both = jnp.concatenate(
                [jnp.where(left, local, 0.0), jnp.where(left, 0.0, local)], axis=0
            ).astype(bf16)
            y = dot(both, basis_ref[q])
            out_ref[2 * q] = (near_ref[2 * q] + y[:nrhs]).astype(bf16)
            out_ref[2 * q + 1] = (near_ref[2 * q + 1] + y[nrhs:]).astype(bf16)
        here = pl.ds(p * FAR_UNROLL, FAR_UNROLL)
        written = pltpu.make_async_copy(out_ref.at[here], out_hbm.at[here], out_sem.at[p])
        written.start()
        return written

    far_steps = leaves // FAR_UNROLL
    written = []
    for p in range(far_steps + 2):
        if p >= 2:
            written.append(finish(p - 2))
        if 1 <= p <= far_steps:
            far_apply(p - 1)
        if p < far_steps:
            far_matrices(p)
    for c in written:
        c.wait()


def vmem():
    return pl.BlockSpec(memory_space=pltpu.VMEM)


def smem():
    return pl.BlockSpec(memory_space=pltpu.SMEM)


def call(kernel, out, in_specs, scratch, flops, vmem_mib, out_specs=None):
    many = isinstance(out, tuple)
    if out_specs is None:
        out_specs = tuple(vmem() for _ in out) if many else vmem()
    return pl.pallas_call(
        kernel,
        out_shape=out,
        in_specs=in_specs,
        out_specs=out_specs,
        scratch_shapes=scratch,
        cost_estimate=pl.CostEstimate(flops=flops, bytes_accessed=1 << 20, transcendentals=0),
        compiler_params=pltpu.CompilerParams(vmem_limit_bytes=vmem_mib << 20),
    )


def pack(peers, per, density, leaf_target):
    leaves, nrhs, leaf = density.shape
    return call(
        lambda *r: pack_kernel(*r, peers=peers, per=per),
        jax.ShapeDtypeStruct((peers, per * nrhs + 8, leaf), bf16),
        [smem(), vmem()],
        [pltpu.SMEM((peers,), jnp.int32), pltpu.SMEM((leaves,), jnp.int32)],
        1 << 20,
        2,
    )(hbm(leaf_target), hbm(density))


def features(node_list, geometry, node_points, near_list, far_list):
    leaves, slots = near_list.shape
    nodes = node_points.shape[1] // 64
    nodes_here, node_slots = node_list.shape
    return call(
        feature_kernel,
        (
            pltpu.HBM((leaves + 1, 128, 128), bf16),
            pltpu.HBM((leaves, 64, 128), bf16),
            pltpu.HBM((leaves + 1, 128, 256), bf16),
            pltpu.HBM((leaves, 128, 128), bf16),
            pltpu.VMEM((leaves * 24, 128), bf16),
            pltpu.VMEM((nodes_here, node_slots * 32, 128), bf16),
            pltpu.HBM((list_rows(slots, leaves), 128), jnp.int32),
            pltpu.HBM((list_rows(slots, leaves), 128), jnp.int32),
            pltpu.HBM((leaves, 128), jnp.int32),
            pltpu.HBM((AHEAD * UNROLL, 256, 128), bf16),
        ),
        [smem()] + [vmem()] * 4,
        [
            pltpu.VMEM((8, leaves * 128), f32),
            pltpu.VMEM((8, nodes * 64), f32),
            pltpu.VMEM((nodes // 2, 128, 128), bf16),
            pltpu.VMEM((nodes_here, 128, 128), bf16),
            pltpu.SMEM((list_rows(slots, leaves), 128), jnp.int32),
            pltpu.SemaphoreType.DMA((1,)),
        ],
        1 << 30,
        18,
    )(hbm(node_list), hbm(geometry), hbm(node_points), hbm(near_list.T), hbm(far_list.T))


def skeletons(arrived, basis_in, transfer, split, per):
    peers = arrived.shape[0]
    leaves = peers * per
    nodes_here = transfer.shape[0]
    rows = leaves // 2 * 32 + leaves // 4 * 32 + leaves // 2 * 24
    shape = jax.ShapeDtypeStruct
    return call(
        lambda *r: skeleton_kernel(*r, per=per),
        (
            pltpu.VMEM((2, rows, 128), bf16),
            pltpu.HBM((rows, 128), bf16),
            pltpu.HBM((rows, 128), bf16),
            shape((peers, nodes_here // 2 * 32, 128), bf16),
        ),
        [vmem()] * 4,
        [],
        1 << 26,
        6,
    )(
        arrived,
        basis_in.reshape(leaves // 2, 128, -1),
        transfer.reshape(nodes_here // 2, 128, -1),
        split,
    )


def own_fields(own_list, fs, ft, own, ready):
    anywhere = pl.BlockSpec(memory_space=pl.ANY)
    return call(
        own_kernel,
        pltpu.VMEM((fs.shape[0], 32, 128), f32),
        [anywhere] * 4 + [vmem()],
        [
            pltpu.VMEM(fs.shape, bf16),
            pltpu.VMEM(ft.shape, bf16),
            pltpu.VMEM(ready.shape, bf16),
            pltpu.VMEM((fs.shape[0], 32, 128), bf16),
            pltpu.VMEM((UNROLL, 256, 128), bf16),
            pltpu.SMEM(own_list.shape, jnp.int32),
            pltpu.SemaphoreType.DMA((4,)),
        ],
        1 << 31,
        12,
    )(hbm(own_list), hbm(fs), hbm(ft), hbm(ready), own)


def leaf_fields(
    far_slots, halo_list, far_list, node_list, fs, fd, ft, wf, basis_out, transfer, own, got_a, got_b, first, all_skel, gn
):
    leaves = wf.shape[0]
    wide = leaves + 2 * REACH
    nodes = all_skel.shape[0] // 16
    anywhere = pl.BlockSpec(memory_space=pl.ANY)
    basis_out = basis_out.reshape(leaves // 2, 128, -1)
    return call(
        leaf_kernel,
        jax.ShapeDtypeStruct((leaves, 32, 128), bf16),
        [anywhere] * 9 + [vmem()] + [anywhere] * 2 + [vmem()] * 3,
        [
            pltpu.VMEM(got_a.shape, bf16),
            pltpu.VMEM(got_a.shape, bf16),
            pltpu.VMEM((wide + 1, 128, 128), bf16),
            pltpu.VMEM((wide + 1, 64, 128), bf16),
            pltpu.VMEM((leaves + 1, 128, 256), bf16),
            pltpu.VMEM((leaves, 128, 128), bf16),
            pltpu.VMEM(basis_out.shape, bf16),
            pltpu.VMEM(transfer.shape, bf16),
            pltpu.VMEM((wide + 1, 32, 128), bf16),
            pltpu.VMEM((wide + 1, 32, 128), bf16),
            pltpu.VMEM((nodes + 1, 32, 128), bf16),
            pltpu.VMEM((leaves + 1, 32, 128), f32),
            pltpu.VMEM((leaves // 2, 32, 128), f32),
            pltpu.VMEM((leaves // 2, 32, 128), f32),
            pltpu.VMEM((leaves, 32, 128), bf16),
            pltpu.VMEM((UNROLL, 256, 128), bf16),
            pltpu.VMEM((FAR_UNROLL, gn.shape[1] // node_list.shape[1] * far_slots, 128), bf16),
            pltpu.SMEM(halo_list.shape, jnp.int32),
            pltpu.SMEM(far_list.shape, jnp.int32),
            pltpu.SMEM(node_list.shape, jnp.int32),
            pltpu.SemaphoreType.DMA((12,)),
            pltpu.SemaphoreType.DMA((leaves // FAR_UNROLL,)),
        ],
        1 << 31,
        24,
        anywhere,
    )(
        *map(hbm, (halo_list, far_list, node_list, fs, fd, ft, wf, basis_out, transfer)),
        own, got_a, got_b, first, all_skel, gn,
    )


def hbm(x):
    return pltpu.with_memory_space_constraint(x, pltpu.HBM)


def on_device(
    density, leaf_target, geometry, near_list, far_list, node_list, basis_in, basis_out, transfer, node_points
):
    peers = lax.axis_size(AXES)
    per = density.shape[0] // peers
    outgoing = pack(peers, per, density, leaf_target)
    arrived = lax.all_to_all(outgoing, AXES, split_axis=0, concat_axis=0, tiled=True)
    fs, fd, ft, wf, split, gn, own_pairs, halo_pairs, far_rows, ready = features(node_list, geometry, node_points, near_list, far_list)
    own, to_a, to_b, node_out = skeletons(arrived, basis_in, transfer, split, per)
    swap_a = [(i, i ^ 1) for i in range(peers)]
    swap_b = [(i, i + 1) for i in range(1, peers - 1, 2)] + [(i + 1, i) for i in range(1, peers - 1, 2)]
    got_a = lax.ppermute(to_a, AXES, swap_a)
    got_b = lax.ppermute(to_b, AXES, swap_b)
    all_skel = lax.all_to_all(node_out, AXES, split_axis=0, concat_axis=0, tiled=True)
    first = own_fields(own_pairs, fs, ft, own, ready)
    return leaf_fields(
        far_list.shape[1], halo_pairs, far_rows, node_list, fs, fd, ft, wf, basis_out, transfer, own, got_a, got_b,
        first, all_skel.reshape(-1, 128), gn,
    )


def solution(mesh):
    split = ("grp", "row", "col")
    return jax.shard_map(
        on_device,
        mesh=mesh,
        in_specs=(
            P(split, None, None),
            P(split),
            P(None, split),
            P(split, None),
            P(split, None),
            P(split, None),
            P(split, None, None),
            P(split, None, None),
            P(split, None, None),
            P(None, "grp"),
        ),
        out_specs=P(split, None, None),
        check_vma=False,
    )
```

```python
import math

import jax
import jax.numpy as jnp
from jax import lax
from jax.experimental import pallas as pl
from jax.experimental.pallas import tpu as pltpu
from jax.sharding import PartitionSpec as P

REACH = 16
AXES = ("row", "col")

smoothing = 0.1
inv_four_pi = 0.25 / math.pi
grid_step = 16.0
UNROLL = 12
AHEAD = 6
FAR_UNROLL = 8
bf16 = jnp.bfloat16
f32 = jnp.float32


def split3(x):
    first = x.astype(bf16).astype(f32)
    rest = x - first
    second = rest.astype(bf16).astype(f32)
    third = (rest - second).astype(bf16).astype(f32)
    return first, second, third


def iota(shape, axis):
    return lax.broadcasted_iota(jnp.int32, shape, axis)


def dot(a, b):
    return lax.dot_general(a, b, (((1,), (0,)), ((), ())), preferred_element_type=f32)


def dot_t(a, b):
    return lax.dot_general(a, b, (((1,), (1,)), ((), ())), preferred_element_type=f32)


class Features:
    def __init__(self, g):
        self.shape = g.shape
        self.row = row = iota(g.shape, 0)
        point = row < 3
        c = jnp.where(point, g, 0.0)
        self.whole = whole = jnp.floor(c * grid_step + 0.5) * (1.0 / grid_step)
        part = c - whole
        self.part = split3(part)
        m = jnp.where(point, 0.0, g) * inv_four_pi
        self.m = split3(m)
        norm = jnp.sum(whole * whole, axis=0, keepdims=True)
        self.norm_hi = jnp.floor(norm)
        self.norm_lo = norm - self.norm_hi
        self.cross = jnp.sum(part * (2.0 * whole + part), axis=0, keepdims=True)
        self.q = split3(jnp.sum(m * pltpu.roll(c, 3, 0), axis=0, keepdims=True))
        self.low = {}

    def moved(self, x):
        if id(x) not in self.low:
            self.low[id(x)] = pltpu.roll(x, 3, 0)
        return self.low[id(x)]

    def tile(self, upper, lower, six, seven):
        row = self.row
        x = jnp.where(row < 3, upper, 0.0)
        if lower is not None:
            x = jnp.where(row < 3, upper, jnp.where(row < 6, lower, 0.0))
        if six is not None:
            x = jnp.where(row == 6, six, x)
        if seven is not None:
            x = jnp.where(row == 7, seven, x)
        return x

    def first(self, points, three, four, five, six):
        row = self.row
        x = jnp.where(row == 3, three, jnp.where(row == 4, four, 0.0))
        x = jnp.where(row == 5, five, jnp.where(row == 6, six, x))
        return jnp.where(row < 3, points, x)

    def zeros(self, rows):
        return jnp.zeros((rows, self.shape[1]), f32)

    def source_square(self):
        w, (p0, p1, p2) = self.whole, self.part
        c0, c1, c2 = split3(self.cross)
        move = self.moved
        return [
            self.first(w, self.norm_hi, self.norm_lo, 1.0, 1.0),
            self.tile(w, move(w), 1.0, 1.0),
            self.tile(w, move(p0), 1.0, c0),
            self.tile(p1, move(p2), c1, c2),
            self.tile(p0, move(p1), None, None),
            self.tile(p0, None, None, None),
            self.zeros(16),
        ]

    def source_normal(self):
        m0, m1, _ = self.m
        u0, u1, u2 = (pltpu.roll(x, 5, 0) for x in self.m)
        q0, q1, q2 = self.q
        return [
            self.tile(u0, m1, q0, q1),
            self.tile(u2, m0, q2, None),
            self.tile(u0, m0, None, None),
            self.tile(u1, m1, None, None),
            self.tile(u2, None, None, None),
            self.zeros(24),
        ]

    def target_square(self):
        w, part = -2.0 * self.whole, [-2.0 * p for p in self.part]
        p0, p1, p2 = part
        c0, c1, c2 = split3(self.cross + smoothing * smoothing)
        w3, p03, p13 = (pltpu.roll(x, 3, 0) for x in (w, p0, p1))
        return [
            self.first(w, 1.0, 1.0, self.norm_hi, self.norm_lo),
            self.tile(p0, p13, c0, c1),
            self.tile(p2, w3, c2, 1.0),
            self.tile(w, w3, 1.0, 1.0),
            self.tile(p0, p03, None, None),
            self.tile(p1, None, None, None),
            self.zeros(16),
        ]

    def target_normal(self):
        w, (p0, p1, p2) = self.whole, self.part
        move = self.moved
        return [
            self.tile(w, move(w), -1.0, -1.0),
            self.tile(w, move(p0), -1.0, None),
            self.tile(p1, move(p2), None, None),
            self.tile(p0, move(p1), None, None),
            self.tile(p0, None, None, None),
            self.zeros(24),
        ]


def sources(f):
    x = jnp.concatenate(f.source_square() + f.source_normal(), axis=0).T
    top = x[:64]
    left = iota(top.shape, 1) < 64
    return x.astype(bf16), jnp.where(left, top, pltpu.roll(top, 64, 1)).astype(bf16)


def point_sources(f):
    x = f.source_square()
    return jnp.concatenate(x + x, axis=0).T.astype(bf16)


def halves(x):
    left = iota(x.shape, 1) < 64
    a = jnp.where(left, x, 0.0)
    b = jnp.where(left, 0.0, x)
    return (a, pltpu.roll(a, 64, 1)), (pltpu.roll(b, 64, 1), b)


def pair_weights(square):
    return [jnp.concatenate(x, axis=0).astype(bf16) for x in halves(jnp.concatenate(square, axis=0))]


def compact(entries, first, dead):
    slots, targets = entries.shape
    place = iota(entries.shape, 0)
    out = jnp.full(entries.shape, dead, jnp.int32)
    count = jnp.zeros((1, targets), jnp.int32)
    for k in range(slots):
        e = entries[k : k + 1]
        live = e >= 0
        at = jnp.where(live, count, -1)
        out = jnp.where(place == at, e - first, out)
        count = count + jnp.where(live, 1, 0)
    return out, count


def items(near, count, dead, out_ref):
    slots, targets = near.shape
    mine = (count + 1) // 2
    before = jnp.where(iota((targets, targets), 0) < iota((targets, targets), 1), 1.0, 0.0).astype(bf16)
    start = dot(jnp.broadcast_to(mine.astype(f32), (8, targets)).astype(bf16), before)[0:1]
    total = jnp.sum(mine, axis=1, keepdims=True).astype(f32)
    table = near.astype(f32).astype(bf16)
    rows = out_ref.shape[0] - 1
    wide = iota((rows, targets), 1)
    slot = iota((rows, slots), 1)
    lane = iota((rows, 128), 1)
    out = jnp.zeros((rows, 128), f32)
    for u in range(UNROLL):
        place = (iota((rows, 1), 0) * UNROLL + u).astype(f32)
        begun = start <= place
        target = jnp.sum(jnp.where(begun, 1.0, 0.0), axis=1, keepdims=True) - 1.0
        base = jnp.max(jnp.where(begun, start, 0.0), axis=1, keepdims=True)
        pick = jnp.where(wide.astype(f32) == target, 1.0, 0.0).astype(bf16)
        lists = dot_t(pick, table)
        used = (place >= 0.0) & (place < total)
        first = 2.0 * (place - base)
        out = jnp.where(lane == u, jnp.where(used, target, float(targets)), out)
        for h in range(2):
            chosen = jnp.where(slot.astype(f32) == first + float(h), lists, 0.0)
            ids = jnp.where(used, jnp.sum(chosen, axis=1, keepdims=True), float(dead))
            out = jnp.where(lane == (h + 1) * UNROLL + u, ids, out)
    out_ref[0:rows] = out.astype(jnp.int32)
    out_ref[rows:] = jnp.broadcast_to(total, (1, 128)).astype(jnp.int32)


def list_rows(slots, leaves):
    return -(-(leaves * (slots // 2) // UNROLL + 1) // 8) * 8 + 1


def pack_kernel(target_ref, density_ref, out_ref, count_ref, slot_ref, *, peers, per):
    leaves, nrhs, leaf = density_ref.shape
    for d in range(peers):
        count_ref[d] = 0
    for k in range(leaves):
        t = target_ref[k]
        d = lax.div(t, leaves)
        c = count_ref[d]
        count_ref[d] = c + 1
        slot_ref[d * per + c] = t - d * leaves
        out_ref[d, pl.ds(pl.multiple_of(c * nrhs, nrhs), nrhs), :] = density_ref[k]
    row = iota((8, leaf), 0)
    for d in range(peers):
        x = jnp.zeros((8, leaf), f32)
        for c in range(per):
            x = jnp.where(row == c, slot_ref[d * per + c].astype(f32), x)
        out_ref[d, per * nrhs :, :] = x.astype(bf16)


def feature_kernel(
    node_list_ref, geo_ref, node_ref, near_ref, far_ref,
    fs_hbm, fd_hbm, ft_hbm, wf_hbm, split_ref, gn_ref, own_list_ref, halo_list_ref, far_list_ref, ready_hbm,
    fs_ref, fd_ref, ft_ref, wf_ref, ready_ref, pad_ref, npad_ref, fsn_ref, wfn_ref, rows_ref, sem,
):
    leaves = fd_ref.shape[0]
    nodes_here = wfn_ref.shape[0]
    slots = near_ref.shape[0]
    index = lax.axis_index(AXES)
    first = index * leaves - REACH
    wide = leaves + 2 * REACH
    pad_ref[...] = jnp.zeros(pad_ref.shape, f32)
    pad_ref[0:6, :] = geo_ref[...]
    npad_ref[...] = jnp.zeros(npad_ref.shape, f32)
    npad_ref[0:3, :] = node_ref[...]
    entries = near_ref[...]
    local = (entries >= index * leaves) & (entries < (index + 1) * leaves)
    items(*compact(jnp.where(local, entries, -1), index * leaves, leaves), leaves, own_list_ref)
    listed = pltpu.make_async_copy(own_list_ref, rows_ref, sem.at[0])
    listed.start()
    items(*compact(jnp.where(local, -1, entries), first, wide), wide, halo_list_ref)
    far, _ = compact(far_ref[...], first, wide)
    same = jnp.where(iota((leaves, leaves), 0) == iota((leaves, leaves), 1), 1.0, 0.0).astype(bf16)
    far_list_ref[:, 0:slots] = dot_t(same, far.astype(f32).astype(bf16)).astype(jnp.int32)

    def leaf_step(l, _):
        g = pad_ref[:, pl.ds(pl.multiple_of(l * 128, 128), 128)]
        f = Features(g)
        fs_ref[l], fd_ref[l] = sources(f)
        square = f.target_square()
        normal = f.target_normal()
        ft_ref[l] = jnp.concatenate(
            [
                jnp.concatenate(square + [f.zeros(64)], axis=0),
                jnp.concatenate([f.zeros(64)] + normal, axis=0),
            ],
            axis=1,
        ).astype(bf16)
        wf_ref[l] = pair_weights(square)[0]
        return 0

    lax.fori_loop(0, leaves, leaf_step, 0, unroll=8)
    fs_ref[leaves] = fs_ref[0]
    ft_ref[leaves] = ft_ref[0]
    sent = [
        pltpu.make_async_copy(fs_ref, fs_hbm, sem.at[1]),
        pltpu.make_async_copy(ft_ref, ft_hbm, sem.at[2]),
        pltpu.make_async_copy(fd_ref, fd_hbm, sem.at[3]),
        pltpu.make_async_copy(wf_ref, wf_hbm, sem.at[4]),
    ]
    for c in sent:
        c.start()

    def split_step(l, _):
        parts = []
        for k in range(2):
            parts += split3(pad_ref[:, pl.ds(pl.multiple_of((l * 2 + k) * 128, 128), 128)])
        split_ref[pl.ds(pl.multiple_of(l * 48, 48), 48), :] = jnp.concatenate(parts, axis=0).astype(bf16)
        return 0

    lax.fori_loop(0, leaves // 2, split_step, 0, unroll=4)

    def node_step(l, _):
        fsn_ref[l] = point_sources(Features(npad_ref[:, pl.ds(pl.multiple_of(l * 128, 128), 128)]))
        return 0

    n_nodes = 2 * fsn_ref.shape[0]
    lax.fori_loop(0, n_nodes // 2, node_step, 0, unroll=8)
    chunk = index * (nodes_here // 2)
    for l in range(nodes_here // 2):
        f = Features(npad_ref[:, pl.ds(pl.multiple_of((chunk + l) * 128, 128), 128)])
        wfn_ref[2 * l], wfn_ref[2 * l + 1] = pair_weights(f.target_square())

    node_slots = node_list_ref.shape[1]
    left = iota((64, 128), 1) < 64

    def node_field(p, _):
        x = []
        for j in range(0, node_slots, 2):
            pair = []
            for u in range(2):
                s = jnp.maximum(node_list_ref[p, j + u], 0)
                pair.append(fsn_ref[s // 2, pl.ds(pl.multiple_of((s % 2) * 64, 64), 64), :])
            x.append(jnp.where(left, pair[0], pair[1]))
        out = dot(jnp.concatenate(x, axis=0), wfn_ref[p])
        gn_ref[p] = (lax.rsqrt(out) * inv_four_pi).astype(bf16)
        return 0

    lax.fori_loop(0, nodes_here, node_field, 0, unroll=2)
    listed.wait()
    for i in range(AHEAD):
        pair_matrices(rows_ref, i, fs_ref, ft_ref, ready_ref, i * UNROLL)
        here = pl.ds(i * UNROLL, UNROLL)
        sent.append(pltpu.make_async_copy(ready_ref.at[here], ready_hbm.at[here], sem.at[5 + i]))
        sent[-1].start()
    for c in sent:
        c.wait()


def skeleton_kernel(
    arrived_ref, basis_ref, transfer_ref, split_ref, own_ref, a_ref, b_ref, node_ref, *, per
):
    peers = arrived_ref.shape[0]
    leaves = peers * per
    nrhs = 32
    half = leaves // 2
    for d in range(peers):
        slots = arrived_ref[d, per * nrhs :, :].astype(f32).astype(jnp.int32)
        for c in range(per):
            s = slots[c, 0]
            h = lax.div(s, half)
            own_ref[h, pl.ds(pl.multiple_of((s - h * half) * nrhs, nrhs), nrhs), :] = arrived_ref[
                d, c * nrhs : (c + 1) * nrhs, :
            ]
    left = iota((nrhs, 128), 1) < 64
    skels = []
    for p in range(leaves // 2):
        h, q = divmod(p, half // 2)
        out = dot_t(own_ref[h, q * 64 : (q + 1) * 64, :], basis_ref[p])
        pair = jnp.where(left, out[:nrhs], out[nrhs:]).astype(bf16)
        own_ref[h, half * nrhs + q * nrhs : half * nrhs + (q + 1) * nrhs, :] = pair
        skels.append(pair)
    base = half * nrhs + (half // 2) * nrhs
    n_split = half * 24
    for h in range(2):
        own_ref[h, base : base + n_split, :] = split_ref[h * n_split : (h + 1) * n_split, :]
    kids = transfer_ref.shape[2] // 128
    n_pairs = len(skels) // (2 * kids)
    for p in range(n_pairs):
        stack = jnp.concatenate(
            [jnp.concatenate(skels[(2 * p + h) * kids : (2 * p + h + 1) * kids], axis=1) for h in range(2)], axis=0
        )
        out = dot_t(stack, transfer_ref[p])
        pair = jnp.where(left, out[:nrhs], out[nrhs:]).astype(bf16)
        for d in range(peers):
            node_ref[d, p * nrhs : (p + 1) * nrhs, :] = pair
    odd = lax.axis_index(AXES) % 2
    a_ref[...] = own_ref[1 - odd]
    b_ref[...] = own_ref[odd]


def doubled(pairs, out_ref, k):
    rows = pairs.shape[0]
    i, j = iota((128, 256), 0), iota((128, 256), 1)
    pick = jnp.where(i == (j % 64) + 64 * (j // 128), 1.0, 0.0).astype(bf16)
    both = dot(pairs, pick).astype(bf16)
    for p in range(rows // 32):
        for h in range(2):
            out_ref[k + 2 * p + h] = both[32 * p : 32 * p + 32, 128 * h : 128 * h + 128]


def far_left(ids, skel_ref):
    left = iota((32, 128), 1) < 64
    cols = []
    for j in range(0, len(ids), 4):
        a, b, c, d = (skel_ref[s] for s in ids[j : j + 4])
        cols.append(jnp.concatenate([jnp.where(left, a, c), jnp.where(left, b, d)], axis=0))
    return jnp.concatenate(cols, axis=1)


def pair_matrices(list_ref, i, fs_ref, ft_ref, k_ref, at=0):
    for u in range(UNROLL):
        x = jnp.concatenate([fs_ref[list_ref[i, (h + 1) * UNROLL + u]] for h in range(2)], axis=0)
        out = dot(x, ft_ref[list_ref[i, u]])
        r = lax.rsqrt(out[:, :128])
        k_ref[at + u] = ((out[:, 128:] * r) * (r * r)).astype(bf16)


def pair_apply(list_ref, i, dens_ref, k_ref, near_ref, at=0):
    for u in range(UNROLL):
        lhs = jnp.concatenate([dens_ref[list_ref[i, (h + 1) * UNROLL + u]] for h in range(2)], axis=1)
        near_ref[list_ref[i, u]] += dot(lhs, k_ref[at + u])


def near_pairs(list_ref, fs_ref, ft_ref, dens_ref, k_ref, near_ref, start=0):
    def step(i, _):
        pair_apply(list_ref, i - 1, dens_ref, k_ref, near_ref)
        pair_matrices(list_ref, i, fs_ref, ft_ref, k_ref)
        return 0

    steps = (list_ref[list_ref.shape[0] - 1, 0] + UNROLL - 1) // UNROLL
    steps = jnp.maximum(steps, start + 1)
    pair_matrices(list_ref, start, fs_ref, ft_ref, k_ref)
    lax.fori_loop(start + 1, steps, step, 0)
    pair_apply(list_ref, steps - 1, dens_ref, k_ref, near_ref)


def own_kernel(
    list_hbm, fs_hbm, ft_hbm, ready_hbm, own_ref,
    near_ref,
    fs_ref, ft_ref, ready_ref, dens_ref, k_ref, list_ref, sem,
):
    leaves = fs_hbm.shape[0] - 1
    half = leaves // 2
    nrhs = 32
    copies = [
        pltpu.make_async_copy(list_hbm, list_ref, sem.at[0]),
        pltpu.make_async_copy(fs_hbm, fs_ref, sem.at[1]),
        pltpu.make_async_copy(ft_hbm, ft_ref, sem.at[2]),
    ]
    for i in range(AHEAD):
        here = pl.ds(i * UNROLL, UNROLL)
        copies.insert(1 + i, pltpu.make_async_copy(ready_hbm.at[here], ready_ref.at[here], sem.at[3 + i]))
    for c in copies:
        c.start()
    for l in range(leaves):
        dens_ref[l] = own_ref[l // half, l % half * nrhs : (l % half + 1) * nrhs, :]
    dens_ref[leaves] = jnp.zeros((nrhs, 128), bf16)
    near_ref[...] = jnp.zeros(near_ref.shape, f32)
    copies[0].wait()
    for i in range(AHEAD):
        copies[1 + i].wait()
        pair_apply(list_ref, i, dens_ref, ready_ref, near_ref, i * UNROLL)
    for c in copies[1 + AHEAD :]:
        c.wait()
    near_pairs(list_ref, fs_ref, ft_ref, dens_ref, k_ref, near_ref, AHEAD)


def leaf_kernel(
    list_hbm, far_list_hbm, node_list_hbm, fs_own_ref, fd_own_ref, ft_hbm, wf_hbm, basis_hbm, transfer_hbm,
    own_ref, a_any, b_any, first_ref, all_skel_ref, gn_ref,
    out_hbm,
    a_ref, b_ref,
    fs_ref, fd_ref, ft_ref, wf_ref, basis_ref, transfer_ref,
    dens_ref, skel_ref, all_ref, near_ref, down_ref, far_ref, out_ref, k_ref, g_ref,
    list_ref, far_list_ref, node_list_ref, sem, out_sem,
):
    leaves = wf_ref.shape[0]
    nrhs = 32
    half = leaves // 2
    wide = leaves + 2 * REACH
    odd = lax.axis_index(AXES) % 2 == 1
    slots = g_ref.shape[1] // 32
    mine = pl.ds(REACH, leaves)
    copies = [
        pltpu.make_async_copy(fd_own_ref, fd_ref.at[mine], sem.at[0]),
        pltpu.make_async_copy(ft_hbm, ft_ref, sem.at[1]),
        pltpu.make_async_copy(wf_hbm, wf_ref, sem.at[2]),
        pltpu.make_async_copy(fs_own_ref.at[0], fs_ref.at[wide], sem.at[3]),
        pltpu.make_async_copy(fd_own_ref.at[0], fd_ref.at[wide], sem.at[4]),
    ]
    copies += [
        pltpu.make_async_copy(list_hbm, list_ref, sem.at[5]),
        pltpu.make_async_copy(far_list_hbm, far_list_ref, sem.at[6]),
        pltpu.make_async_copy(node_list_hbm, node_list_ref, sem.at[7]),
    ]
    later = [
        copies.pop(2),
        copies.pop(0),
        pltpu.make_async_copy(basis_hbm, basis_ref, sem.at[8]),
        pltpu.make_async_copy(transfer_hbm, transfer_ref, sem.at[9]),
    ]
    arrived = [
        pltpu.make_async_copy(a_any, a_ref, sem.at[10]),
        pltpu.make_async_copy(b_any, b_ref, sem.at[11]),
    ]
    for c in arrived + copies + later:
        c.start()
    for c in arrived:
        c.wait()

    base = half * nrhs + (half // 2) * nrhs
    for right, k in ((False, 0), (True, REACH + leaves)):

        def halo(l, _, right=right, k=k):
            at = pl.ds(pl.multiple_of(base + l * 48, 16), 48)
            x, y = a_ref[at, :].astype(f32), b_ref[at, :].astype(f32)
            x = jnp.where(odd, y, x) if right else jnp.where(odd, x, y)
            for j in range(2):
                g = x[24 * j : 24 * j + 8] + x[24 * j + 8 : 24 * j + 16] + x[24 * j + 16 : 24 * j + 24]
                fs_ref[k + 2 * l + j], fd_ref[k + 2 * l + j] = sources(Features(g))
            return 0

        lax.fori_loop(0, half // 2, halo, 0, unroll=4)

    def fill(view, k, dens=True):
        if dens:
            for l in range(half):
                dens_ref[k + l] = view(l * nrhs, nrhs)
        doubled(view(half * nrhs, half // 2 * nrhs), skel_ref, k)

    fill(lambda at, n: jnp.where(odd, a_ref[at : at + n, :], b_ref[at : at + n, :]), 0)
    fill(lambda at, n: own_ref[0, at : at + n, :], REACH, False)
    fill(lambda at, n: own_ref[1, at : at + n, :], REACH + half, False)
    fill(lambda at, n: jnp.where(odd, b_ref[at : at + n, :], a_ref[at : at + n, :]), REACH + leaves)
    dens_ref[wide] = jnp.zeros((nrhs, 128), bf16)
    skel_ref[wide] = jnp.zeros((nrhs, 128), bf16)
    near_ref[...] = first_ref[...]
    pairs = all_skel_ref.shape[0] // nrhs
    doubled(all_skel_ref[...], all_ref, 0)
    all_ref[2 * pairs] = jnp.zeros((nrhs, 128), bf16)
    for c in copies:
        c.wait()
    near_pairs(list_ref, fs_ref, ft_ref, dens_ref, k_ref, near_ref)
    for c in later:
        c.wait()

    kids = transfer_ref.shape[2] // 128
    for p in range(gn_ref.shape[0]):
        ids = []
        for j in range(node_list_ref.shape[1]):
            e = node_list_ref[p, j]
            ids.append(jnp.where(e < 0, 2 * pairs, e))
        acc = dot(far_left(ids, all_ref), gn_ref[p])
        x = acc[:nrhs] + pltpu.roll(acc[nrhs:], 64, 1)
        down = dot(x[:, :64].astype(bf16), transfer_ref[p])
        for c in range(kids):
            down_ref[p * kids + c] = down[:, c * 128 : (c + 1) * 128]

    left = iota((nrhs, 128), 1) < 64
    left64 = iota((64, 128), 1) < 64

    def far_ids(t):
        return [far_list_ref[t, u] for u in range(slots)]

    def far_matrices(p):
        for h in range(FAR_UNROLL):
            ids = far_ids(FAR_UNROLL * p + h)
            x = [
                jnp.where(left64, fd_ref[ids[j]], fd_ref[ids[j + 1]]) for j in range(0, slots, 2)
            ]
            out = dot(jnp.concatenate(x, axis=0), wf_ref[FAR_UNROLL * p + h])
            g_ref[h] = (lax.rsqrt(out) * inv_four_pi).astype(bf16)

    def far_apply(p):
        for h in range(0, FAR_UNROLL, 2):
            t = FAR_UNROLL * p + h
            e, o = (dot(far_left(far_ids(t + k), skel_ref), g_ref[h + k]) for k in range(2))
            even = e[:nrhs] + pltpu.roll(e[nrhs:], 64, 1)
            odd_ = pltpu.roll(o[:nrhs], 64, 1) + o[nrhs:]
            far_ref[(FAR_UNROLL // 2) * p + h // 2] = jnp.where(left, even, odd_)

    def finish(p):
        for q in range(FAR_UNROLL // 2 * p, FAR_UNROLL // 2 * (p + 1)):
            local = (far_ref[q] + down_ref[q]).astype(bf16).astype(f32)
            both = jnp.concatenate(
                [jnp.where(left, local, 0.0), jnp.where(left, 0.0, local)], axis=0
            ).astype(bf16)
            y = dot(both, basis_ref[q])
            out_ref[2 * q] = (near_ref[2 * q] + y[:nrhs]).astype(bf16)
            out_ref[2 * q + 1] = (near_ref[2 * q + 1] + y[nrhs:]).astype(bf16)
        here = pl.ds(p * FAR_UNROLL, FAR_UNROLL)
        written = pltpu.make_async_copy(out_ref.at[here], out_hbm.at[here], out_sem.at[p])
        written.start()
        return written

    far_steps = leaves // FAR_UNROLL
    written = []
    for p in range(far_steps + 2):
        if p >= 2:
            written.append(finish(p - 2))
        if 1 <= p <= far_steps:
            far_apply(p - 1)
        if p < far_steps:
            far_matrices(p)
    for c in written:
        c.wait()


def vmem():
    return pl.BlockSpec(memory_space=pltpu.VMEM)


def smem():
    return pl.BlockSpec(memory_space=pltpu.SMEM)


def call(kernel, out, in_specs, scratch, flops, vmem_mib, out_specs=None):
    many = isinstance(out, tuple)
    if out_specs is None:
        out_specs = tuple(vmem() for _ in out) if many else vmem()
    return pl.pallas_call(
        kernel,
        out_shape=out,
        in_specs=in_specs,
        out_specs=out_specs,
        scratch_shapes=scratch,
        cost_estimate=pl.CostEstimate(flops=flops, bytes_accessed=1 << 20, transcendentals=0),
        compiler_params=pltpu.CompilerParams(vmem_limit_bytes=vmem_mib << 20),
    )


def pack(peers, per, density, leaf_target):
    leaves, nrhs, leaf = density.shape
    return call(
        lambda *r: pack_kernel(*r, peers=peers, per=per),
        jax.ShapeDtypeStruct((peers, per * nrhs + 8, leaf), bf16),
        [smem(), vmem()],
        [pltpu.SMEM((peers,), jnp.int32), pltpu.SMEM((leaves,), jnp.int32)],
        1 << 20,
        2,
    )(hbm(leaf_target), hbm(density))


def features(node_list, geometry, node_points, near_list, far_list):
    leaves, slots = near_list.shape
    nodes = node_points.shape[1] // 64
    nodes_here, node_slots = node_list.shape
    anywhere = pl.BlockSpec(memory_space=pl.ANY)
    return call(
        feature_kernel,
        (
            pltpu.HBM((leaves + 1, 128, 128), bf16),
            pltpu.HBM((leaves, 64, 128), bf16),
            pltpu.HBM((leaves + 1, 128, 256), bf16),
            pltpu.HBM((leaves, 128, 128), bf16),
            pltpu.VMEM((leaves * 24, 128), bf16),
            pltpu.VMEM((nodes_here, node_slots * 32, 128), bf16),
            pltpu.HBM((list_rows(slots, leaves), 128), jnp.int32),
            pltpu.HBM((list_rows(slots, leaves), 128), jnp.int32),
            pltpu.HBM((leaves, 128), jnp.int32),
            pltpu.HBM((AHEAD * UNROLL, 256, 128), bf16),
        ),
        [smem()] + [vmem()] * 4,
        [
            pltpu.VMEM((leaves + 1, 128, 128), bf16),
            pltpu.VMEM((leaves, 64, 128), bf16),
            pltpu.VMEM((leaves + 1, 128, 256), bf16),
            pltpu.VMEM((leaves, 128, 128), bf16),
            pltpu.VMEM((AHEAD * UNROLL, 256, 128), bf16),
            pltpu.VMEM((8, leaves * 128), f32),
            pltpu.VMEM((8, nodes * 64), f32),
            pltpu.VMEM((nodes // 2, 128, 128), bf16),
            pltpu.VMEM((nodes_here, 128, 128), bf16),
            pltpu.SMEM((list_rows(slots, leaves), 128), jnp.int32),
            pltpu.SemaphoreType.DMA((5 + AHEAD,)),
        ],
        1 << 30,
        24,
        tuple([anywhere] * 4 + [vmem()] * 5 + [anywhere]),
    )(hbm(node_list), hbm(geometry), hbm(node_points), hbm(near_list.T), hbm(far_list.T))


def skeletons(arrived, basis_in, transfer, split, per):
    peers = arrived.shape[0]
    leaves = peers * per
    nodes_here = transfer.shape[0]
    rows = leaves // 2 * 32 + leaves // 4 * 32 + leaves // 2 * 24
    shape = jax.ShapeDtypeStruct
    return call(
        lambda *r: skeleton_kernel(*r, per=per),
        (
            pltpu.VMEM((2, rows, 128), bf16),
            pltpu.HBM((rows, 128), bf16),
            pltpu.HBM((rows, 128), bf16),
            shape((peers, nodes_here // 2 * 32, 128), bf16),
        ),
        [vmem()] * 4,
        [],
        1 << 26,
        6,
    )(
        arrived,
        basis_in.reshape(leaves // 2, 128, -1),
        transfer.reshape(nodes_here // 2, 128, -1),
        split,
    )


def own_fields(own_list, fs, ft, own, ready):
    anywhere = pl.BlockSpec(memory_space=pl.ANY)
    return call(
        own_kernel,
        pltpu.VMEM((fs.shape[0], 32, 128), f32),
        [anywhere] * 4 + [vmem()],
        [
            pltpu.VMEM(fs.shape, bf16),
            pltpu.VMEM(ft.shape, bf16),
            pltpu.VMEM(ready.shape, bf16),
            pltpu.VMEM((fs.shape[0], 32, 128), bf16),
            pltpu.VMEM((UNROLL, 256, 128), bf16),
            pltpu.SMEM(own_list.shape, jnp.int32),
            pltpu.SemaphoreType.DMA((3 + AHEAD,)),
        ],
        1 << 31,
        14,
    )(hbm(own_list), hbm(fs), hbm(ft), hbm(ready), own)


def leaf_fields(
    far_slots, halo_list, far_list, node_list, fs, fd, ft, wf, basis_out, transfer, own, got_a, got_b, first, all_skel, gn
):
    leaves = wf.shape[0]
    wide = leaves + 2 * REACH
    nodes = all_skel.shape[0] // 16
    anywhere = pl.BlockSpec(memory_space=pl.ANY)
    basis_out = basis_out.reshape(leaves // 2, 128, -1)
    return call(
        leaf_kernel,
        jax.ShapeDtypeStruct((leaves, 32, 128), bf16),
        [anywhere] * 9 + [vmem()] + [anywhere] * 2 + [vmem()] * 3,
        [
            pltpu.VMEM(got_a.shape, bf16),
            pltpu.VMEM(got_a.shape, bf16),
            pltpu.VMEM((wide + 1, 128, 128), bf16),
            pltpu.VMEM((wide + 1, 64, 128), bf16),
            pltpu.VMEM((leaves + 1, 128, 256), bf16),
            pltpu.VMEM((leaves, 128, 128), bf16),
            pltpu.VMEM(basis_out.shape, bf16),
            pltpu.VMEM(transfer.shape, bf16),
            pltpu.VMEM((wide + 1, 32, 128), bf16),
            pltpu.VMEM((wide + 1, 32, 128), bf16),
            pltpu.VMEM((nodes + 1, 32, 128), bf16),
            pltpu.VMEM((leaves + 1, 32, 128), f32),
            pltpu.VMEM((leaves // 2, 32, 128), f32),
            pltpu.VMEM((leaves // 2, 32, 128), f32),
            pltpu.VMEM((leaves, 32, 128), bf16),
            pltpu.VMEM((UNROLL, 256, 128), bf16),
            pltpu.VMEM((FAR_UNROLL, gn.shape[1] // node_list.shape[1] * far_slots, 128), bf16),
            pltpu.SMEM(halo_list.shape, jnp.int32),
            pltpu.SMEM(far_list.shape, jnp.int32),
            pltpu.SMEM(node_list.shape, jnp.int32),
            pltpu.SemaphoreType.DMA((12,)),
            pltpu.SemaphoreType.DMA((leaves // FAR_UNROLL,)),
        ],
        1 << 31,
        24,
        anywhere,
    )(
        *map(hbm, (halo_list, far_list, node_list, fs, fd, ft, wf, basis_out, transfer)),
        own, got_a, got_b, first, all_skel, gn,
    )


def hbm(x):
    return pltpu.with_memory_space_constraint(x, pltpu.HBM)


def on_device(
    density, leaf_target, geometry, near_list, far_list, node_list, basis_in, basis_out, transfer, node_points
):
    peers = lax.axis_size(AXES)
    per = density.shape[0] // peers
    outgoing = pack(peers, per, density, leaf_target)
    arrived = lax.all_to_all(outgoing, AXES, split_axis=0, concat_axis=0, tiled=True)
    fs, fd, ft, wf, split, gn, own_pairs, halo_pairs, far_rows, ready = features(node_list, geometry, node_points, near_list, far_list)
    own, to_a, to_b, node_out = skeletons(arrived, basis_in, transfer, split, per)
    swap_a = [(i, i ^ 1) for i in range(peers)]
    swap_b = [(i, i + 1) for i in range(1, peers - 1, 2)] + [(i + 1, i) for i in range(1, peers - 1, 2)]
    got_a = lax.ppermute(to_a, AXES, swap_a)
    got_b = lax.ppermute(to_b, AXES, swap_b)
    all_skel = lax.all_to_all(node_out, AXES, split_axis=0, concat_axis=0, tiled=True)
    first = own_fields(own_pairs, fs, ft, own, ready)
    return leaf_fields(
        far_list.shape[1], halo_pairs, far_rows, node_list, fs, fd, ft, wf, basis_out, transfer, own, got_a, got_b,
        first, all_skel.reshape(-1, 128), gn,
    )


def solution(mesh):
    split = ("grp", "row", "col")
    return jax.shard_map(
        on_device,
        mesh=mesh,
        in_specs=(
            P(split, None, None),
            P(split),
            P(None, split),
            P(split, None),
            P(split, None),
            P(split, None),
            P(split, None, None),
            P(split, None, None),
            P(split, None, None),
            P(None, "grp"),
        ),
        out_specs=P(split, None, None),
        check_vma=False,
    )
```
